32 devices in a mesh: fsdp: 8 (over z, y), ctx: 2 (over x), tp: 2 (over core).
Axes of the slice: x: 2, y: 2, z: 4, core: 2. Of those that a mesh axis runs over, the one named last changes fastest.
Arguments:
- hidden_in: bfloat16 [8, 1024, 2048], P('fsdp', 'ctx'), may hold values from -6 to 6
- segments: int32 [8, 1024], P('fsdp'), may hold values from 0 to 7, never falling along the last dimension, each value on 1 to 512 neighbouring positions
- gain_attn: float32 [2048], P(('fsdp', 'ctx')), may hold values from 0.5 to 1.5
- query_weight: bfloat16 [2048, 2048], P(('fsdp', 'ctx'), 'tp'), may hold values from -0.5 to 0.5
- key_weight: bfloat16 [2048, 512], P(('fsdp', 'ctx'), 'tp'), may hold values from -0.5 to 0.5
- value_weight: bfloat16 [2048, 512], P(('fsdp', 'ctx'), 'tp'), may hold values from -0.125 to 0.125
- out_weight: bfloat16 [2048, 2048], P(('fsdp', 'ctx'), 'tp'), may hold values from -2 to 2
- gain_ffn: float32 [2048], P(('fsdp', 'ctx')), may hold values from 0.5 to 1.5
- gate_weight: bfloat16 [2048, 8192], P(('fsdp', 'ctx'), 'tp'), may hold values from -0.125 to 0.125
- up_weight: bfloat16 [2048, 8192], P(('fsdp', 'ctx'), 'tp'), may hold values from -0.125 to 0.125
- down_weight: bfloat16 [2048, 8192], P(('fsdp', 'ctx'), 'tp'), may hold values from -0.375 to 0.375
- cotangent: bfloat16 [8, 1024, 2048], P('fsdp', 'ctx'), may hold values from -6 to 6
Outputs:
- layer_out: bfloat16 [8, 1024, 2048], P('fsdp', 'ctx')
- input_grad: float32 [8, 1024, 2048], P('fsdp', 'ctx')
- grad_gain_attn: float32 [2048], P(('fsdp', 'ctx'))
- grad_query: float32 [2048, 2048], P(('fsdp', 'ctx'), 'tp')
- grad_key: float32 [2048, 512], P(('fsdp', 'ctx'), 'tp')
- grad_value: float32 [2048, 512], P(('fsdp', 'ctx'), 'tp')
- grad_out: float32 [2048, 2048], P(('fsdp', 'ctx'), 'tp')
- grad_gain_ffn: float32 [2048], P(('fsdp', 'ctx'))
- grad_gate: float32 [2048, 8192], P(('fsdp', 'ctx'), 'tp')
- grad_up: float32 [2048, 8192], P(('fsdp', 'ctx'), 'tp')
- grad_down: float32 [2048, 8192], P(('fsdp', 'ctx'), 'tp')
The draws below stay inside these ranges and needn't reach their ends.
Inputs may be any that keep to these rules, and one draw needn't show every extreme that they name: `segments`: in each sequence the ids start at 0 and never fall; each of the 8 ids covers 1 to 512 consecutive tokens, and one document of each sequence has exactly 512.
All inputs are finite; a program needn't handle non-finite values.
Results may differ from the reference program's by a relative error of at most 0.038.
Values may be sent and summed in bfloat16 or wider, within the bound.
No kernel may reach another device: no remote copies, remote signals or barrier semaphores. Data moves between devices by JAX's collectives and lax.ppermute only.
A program may use at most 320 MiB of HBM per device.

```python
import math
import jax
import jax.numpy as jnp
import numpy as np
from jax import lax

D = 2048
HQ = 32
KVH = 8
HD = 64
FF = 8192
LEN = 1024
DOCS = 8
NSEQ = 8


def block_levels(own_key, extent, split, smallest, top_value):
    level, own = 1.0, jax.random.fold_in(own_key, 6)
    for position, shards_of in split:
        draws = jnp.exp(jax.random.uniform(jax.random.fold_in(own, position), (shards_of,), jnp.float32, smallest / len(split), top_value / len(split)))
        level = level * jnp.repeat(draws, extent[position] // shards_of).reshape([-1 if axis == position else 1 for axis in range(len(extent))])
    return level


def length_profile(amount, total, most, skew):
    loads = [(1 << 20) // math.isqrt(standing ** skew) + 1 for standing in range(2, amount + 1)]
    rest, counts = total - most - (amount - 1), [1] * (amount - 1)
    while rest > 0:
        movable = [i for i in range(amount - 1) if counts[i] < most]
        whole, left = sum([loads[i] for i in movable]), rest
        for i in movable:
            addition = min(most - counts[i], max(1, left * loads[i] // whole), rest)
            counts[i] = counts[i] + addition
            rest = rest - addition
    return np.array([most] + counts)


def uneven(own_key, number_of, total, limit, skew):
    if number_of == 2:
        one = jax.random.randint(own_key, (), max(1, total - limit), min(limit, total - 1) + 1)
        return jnp.stack([one, total - one])
    lengths = jnp.asarray(length_profile(number_of, total, limit, skew), jnp.int32)
    couples = (number_of - 1) // 2
    giver, sink = lengths[1:1 + 2 * couples:2], lengths[2:2 + 2 * couples:2]
    room = jnp.minimum(giver - 1, limit - sink)
    passed = jax.random.randint(jax.random.fold_in(own_key, 1), (couples,), 0, 1 << 20) % (room + 1)
    lengths = lengths.at[1:1 + 2 * couples:2].set(giver - passed).at[2:2 + 2 * couples:2].set(sink + passed)
    return lengths[jax.random.permutation(jax.random.fold_in(own_key, 2), number_of)]


def scatter_about(own_key, extent, scale, reach, cuts=(), kind=jnp.bfloat16):
    drawn = jax.random.normal(own_key, extent, jnp.float32) * scale
    if len(cuts) > 0:
        drawn = block_levels(own_key, extent, cuts, -0.22, 0.18) * drawn
    return jnp.clip(drawn, min=-reach, max=reach).astype(kind)


def setup_inputs(seed: int = 0) -> dict:
    keys = jax.random.split(jax.random.key(seed), 13)
    hidden_in = scatter_about(keys[0], (NSEQ, LEN, D), 1.0, 6.0, ((0, 8), (1, 2)))
    segments = jax.vmap(lambda own: jnp.searchsorted(jnp.cumsum(uneven(own, DOCS, LEN, LEN // 2, 2)), jnp.arange(LEN), side="right"))(jax.random.split(keys[1], NSEQ)).reshape((NSEQ, LEN)).astype(jnp.int32)
    gain_attn = jnp.clip(1.0 + 0.1 * jax.random.normal(keys[2], (D,), jnp.float32), 0.5, 1.5)
    query_weight = scatter_about(keys[3], (D, HQ * HD), (D // 16) ** -0.5, 0.5, ((0, 16), (1, 2)))
    key_weight = scatter_about(keys[4], (D, KVH * HD), (D // 16) ** -0.5, 0.5, ((0, 16), (1, 2)))
    value_weight = scatter_about(keys[5], (D, KVH * HD), D ** -0.5, 0.125, ((0, 16), (1, 2)))
    out_weight = scatter_about(keys[6], (D, HQ * HD), (HQ * HD // 256 + 1) ** -0.5, 2.0, ((0, 16), (1, 2)))
    gain_ffn = jnp.clip(1.0 + 0.1 * jax.random.normal(keys[7], (D,), jnp.float32), 0.5, 1.5)
    gate_weight = scatter_about(keys[8], (D, FF), D ** -0.5, 0.125, ((0, 16), (1, 2)))
    up_weight = scatter_about(keys[9], (D, FF), D ** -0.5, 0.125, ((0, 16), (1, 2)))
    down_weight = scatter_about(keys[10], (D, FF), (FF // 32) ** -0.5, 0.375, ((0, 16), (1, 2)))
    cotangent = scatter_about(keys[11], (NSEQ, LEN, D), 1.0, 6.0, ((0, 8), (1, 2)))
    return {"hidden_in": hidden_in, "segments": segments, "gain_attn": gain_attn, "query_weight": query_weight, "key_weight": key_weight, "value_weight": value_weight, "out_weight": out_weight, "gain_ffn": gain_ffn, "gate_weight": gate_weight, "up_weight": up_weight, "down_weight": down_weight, "cotangent": cotangent}


EPSILON = 1e-05
SCALE = 0.015625
RESIDUAL = 0.22
THETA = 10000000.0
HIGHEST = lax.Precision.HIGHEST

@jax.custom_vjp
def low(v):
    return lax.optimization_barrier(v.astype(jnp.bfloat16)).astype(jnp.float32)

@jax.custom_vjp
def low_back(v):
    return v

def low_keep(v):
    return (low(v), None)

def low_pass(kept, grad):
    return (grad,)

def back_keep(v):
    return (v, None)

def back_low(kept, grad):
    return (low(grad),)
low.defvjp(low_keep, low_pass)
low_back.defvjp(back_keep, back_low)

def matmul_high(left, right):
    flat = left.reshape(-1, left.shape[-1])
    return jnp.dot(flat, right, precision=HIGHEST).reshape(left.shape[:-1] + (right.shape[-1],))

def matmul_trans(left, right):
    flat = left.reshape(-1, left.shape[-1])
    return jnp.dot(flat, right.T, precision=HIGHEST).reshape(left.shape[:-1] + (right.shape[0],))

def rms_scale(values, gain):
    return values * lax.rsqrt(lax.optimization_barrier(jnp.mean(values * values, axis=-1, keepdims=True)) + EPSILON) * gain

def rotate_pairs(values, cosine, sine):
    half = values.shape[-1] // 2
    swapped = jnp.concatenate([-values[..., half:], values[..., :half]], axis=-1)
    return values * cosine + swapped * sine

def angles(seg_rows):
    length = seg_rows.shape[-1]
    before = lax.optimization_barrier(jnp.sum((seg_rows[..., None, :] < seg_rows[..., :, None]).astype(jnp.int32), axis=-1)).astype(jnp.int32)
    places = (jnp.arange(length, dtype=jnp.int32)[None, :] - before).astype(jnp.float32)
    freqs = THETA ** (-jnp.arange(0, HD, 2, dtype=jnp.float32) / HD)
    phase = places[..., None] * freqs
    phase = jnp.concatenate([phase, phase], axis=-1)
    return (jnp.cos(phase), jnp.sin(phase))

def attend(pieces):
    queries, key_rows, values, seg_one = pieces
    length = seg_one.shape[0]
    places = jnp.arange(length, dtype=jnp.int32)
    allowed = (seg_one[:, None] == seg_one[None, :]) & (places[None, :] <= places[:, None])
    scores = low_back(jnp.einsum('qngd,knd->ngqk', queries, key_rows, precision=HIGHEST) * SCALE)
    scores = jnp.where(allowed, scores, -1e+30)
    highest = lax.optimization_barrier(jnp.max(scores, axis=-1, keepdims=True))
    raised = jnp.exp(scores - highest)
    attn_weights = raised / lax.optimization_barrier(jnp.sum(raised, axis=-1, keepdims=True))
    return jnp.einsum('ngqk,knd->qngd', low(attn_weights), values, precision=HIGHEST)

def layer_forward(inputs_f, weights_f, seg_rows, cosine, sine):
    gain_a, query_w, key_w, value_w, out_w, gain_f, gate_w, up_w, down_w = weights_f
    seq_count = inputs_f.shape[0]
    normed = low(rms_scale(inputs_f, gain_a))
    queries = low_back(matmul_high(normed, query_w)).reshape(seq_count, LEN, KVH, HQ // KVH, HD)
    key_rows = low_back(matmul_high(normed, key_w)).reshape(seq_count, LEN, KVH, HD)
    values = low(low_back(matmul_high(normed, value_w))).reshape(seq_count, LEN, KVH, HD)
    queries = low(rotate_pairs(queries, cosine[:, :, None, None, :], sine[:, :, None, None, :]))
    key_rows = low(rotate_pairs(key_rows, cosine[:, :, None, :], sine[:, :, None, :]))
    mixed = lax.map(jax.checkpoint(attend), (queries, key_rows, values, seg_rows))
    mixed = low_back(low(mixed.reshape(seq_count, LEN, HQ * HD)))
    branch_a = low_back(matmul_trans(mixed, out_w))
    middle = inputs_f + RESIDUAL * branch_a
    normed_f = low(rms_scale(middle, gain_f))
    gate_pre = low_back(matmul_high(normed_f, gate_w))
    upward = low_back(matmul_high(normed_f, up_w))
    hidden = low(gate_pre * jax.nn.sigmoid(gate_pre) * upward)
    branch_f = low_back(matmul_trans(hidden, down_w))
    return middle + RESIDUAL * branch_f

def reference(hidden_in, segments, gain_attn, query_weight, key_weight, value_weight, out_weight, gain_ffn, gate_weight, up_weight, down_weight, cotangent):
    weights_f = tuple((weight.astype(jnp.float32) for weight in (gain_attn, query_weight, key_weight, value_weight, out_weight, gain_ffn, gate_weight, up_weight, down_weight)))
    groups = NSEQ // 4
    inputs = hidden_in.astype(jnp.float32).reshape(groups, 4, LEN, D)
    cotans = cotangent.astype(jnp.float32).reshape(groups, 4, LEN, D)
    seg_groups = segments.reshape(groups, 4, LEN)

    def group_step(totals, group_item):
        inputs_g, cotan_g, seg_g = group_item
        cosine, sine = angles(seg_g)

        def forward(inputs_x, weights_g):
            return layer_forward(inputs_x, weights_g, seg_g, cosine, sine)
        outputs, pullback = jax.vjp(forward, inputs_g, weights_f)
        grad_in, grad_weights = pullback(cotan_g)
        summed = tuple((total + extra for total, extra in zip(totals, grad_weights)))
        return (summed, (outputs.astype(jnp.bfloat16), grad_in))
    start_totals = tuple((jnp.zeros_like(weight) for weight in weights_f))
    totals, (outputs, grads_in) = lax.scan(group_step, start_totals, (inputs, cotans, seg_groups))
    return (outputs.reshape(NSEQ, LEN, D), grads_in.reshape(NSEQ, LEN, D), totals[0], totals[1], totals[2], totals[3], totals[4], totals[5], totals[6], totals[7], totals[8])
```

```python
import functools

import jax
import jax.numpy as jnp
from jax import lax
from jax.experimental import pallas as pl
from jax.experimental.pallas import tpu as pltpu
from jax.sharding import Mesh
from jax.sharding import PartitionSpec as P

HQ = 32
KVH = 8
HD = 64


EPSILON = 1e-05
SCALE = 0.015625
RESIDUAL = 0.22
THETA = 10000000.0


def rotate_pairs(values, cosine, sine):
    half = values.shape[-1] // 2
    swapped = jnp.concatenate([-values[..., half:], values[..., :half]], axis=-1)
    return values * cosine + swapped * sine


def matmul_low(left, right):
    return jnp.dot(left, right, preferred_element_type=jnp.float32)


def matmul_trans(left, right):
    return lax.dot_general(
        left, right, (((1,), (1,)), ((), ())), preferred_element_type=jnp.float32
    )


def matmul_outer(left, right):
    return lax.dot_general(
        left, right, (((0,), (0,)), ((), ())), preferred_element_type=jnp.float32
    )


def norm_back(grad_normed, gain, unit_rows, inv_rms):
    scaled = grad_normed * gain
    return inv_rms * (scaled - unit_rows * jnp.mean(scaled * unit_rows, axis=-1, keepdims=True))


def reduce_low(grad):
    low = lax.psum_scatter(
        grad.astype(jnp.bfloat16), ("fsdp", "ctx"), scatter_dimension=0, tiled=True
    )
    return low.astype(jnp.float32)


def generic_shards(
    hidden_in,
    segments,
    gain_attn,
    query_weight,
    key_weight,
    value_weight,
    out_weight,
    gain_ffn,
    gate_weight,
    up_weight,
    down_weight,
    cotangent,
):
    seqs_here, rows_here, width = hidden_in.shape
    length = segments.shape[1]
    tokens = seqs_here * rows_here
    kv_local = key_weight.shape[1] // HD
    group_size = HQ // KVH
    head_cols = kv_local * group_size * HD
    bfloat = jnp.bfloat16
    first_row = lax.axis_index("ctx") * rows_here
    own_seg = lax.dynamic_slice_in_dim(segments, first_row, rows_here, 1)
    before = jnp.sum((segments[:, None, :] < own_seg[:, :, None]).astype(jnp.int32), axis=2)
    own_place = first_row + jnp.arange(rows_here, dtype=jnp.int32)
    places = (own_place[None, :] - before).astype(jnp.float32)
    freqs = THETA ** (-jnp.arange(0, HD, 2, dtype=jnp.float32) / HD)
    phase = places[:, :, None] * freqs
    phase = jnp.concatenate([phase, phase], axis=-1)
    cosine = jnp.cos(phase)
    sine = jnp.sin(phase)
    key_place = jnp.arange(length, dtype=jnp.int32)
    allowed = (own_seg[:, :, None] == segments[:, None, :]) & (
        key_place[None, None, :] <= own_place[None, :, None]
    )
    allowed = allowed[:, None, None, :, :]
    attn_full = (
        lax.all_gather(gain_attn.astype(jnp.bfloat16), ("fsdp", "ctx"), axis=0, tiled=True).astype(
            gain_attn.dtype
        ),
        lax.all_gather(query_weight, ("fsdp", "ctx"), axis=0, tiled=True),
        lax.all_gather(key_weight, ("fsdp", "ctx"), axis=0, tiled=True),
        lax.all_gather(value_weight, ("fsdp", "ctx"), axis=0, tiled=True),
        lax.all_gather(out_weight, ("fsdp", "ctx"), axis=0, tiled=True),
    )
    gain_a, query_full, key_full, value_full, out_full = attn_full
    inputs_f = hidden_in.reshape(tokens, width).astype(jnp.float32)
    inv_a = lax.rsqrt(jnp.mean(inputs_f * inputs_f, axis=-1, keepdims=True) + EPSILON)
    unit_a = inputs_f * inv_a
    normed_a = (unit_a * gain_a).astype(bfloat)
    query_raw = matmul_low(normed_a, query_full).reshape(
        seqs_here, rows_here, kv_local, group_size, HD
    )
    key_raw = matmul_low(normed_a, key_full).reshape(seqs_here, rows_here, kv_local, HD)
    value_low = (
        matmul_low(normed_a, value_full).astype(bfloat).reshape(seqs_here, rows_here, kv_local * HD)
    )
    query_rot = rotate_pairs(
        query_raw, cosine[:, :, None, None, :], sine[:, :, None, None, :]
    ).astype(bfloat)
    key_rot = rotate_pairs(key_raw, cosine[:, :, None, :], sine[:, :, None, :]).astype(bfloat)
    key_rot = key_rot.reshape(seqs_here, rows_here, kv_local * HD)
    key_all, value_all = (
        lax.all_gather(key_rot, "ctx", axis=1, tiled=True),
        lax.all_gather(value_low, "ctx", axis=1, tiled=True),
    )
    key_all = key_all.reshape(seqs_here, length, kv_local, HD)
    value_all = value_all.reshape(seqs_here, length, kv_local, HD)

    def masked_scores():
        scores = (
            jnp.einsum("srngd,slnd->sngrl", query_rot, key_all, preferred_element_type=jnp.float32)
            * SCALE
        )
        return jnp.where(allowed, scores, -1e30)

    scores = masked_scores()
    highest = jnp.max(scores, axis=-1, keepdims=True)
    raised = jnp.exp(scores - highest)
    totals = jnp.sum(raised, axis=-1, keepdims=True)
    log_total = highest + jnp.log(totals)
    probs_low = (raised / totals).astype(bfloat)
    mixed = jnp.einsum(
        "sngrl,slnd->srngd", probs_low, value_all, preferred_element_type=jnp.float32
    )
    mixed = mixed.astype(bfloat).reshape(tokens, head_cols)
    branch_a = lax.psum(matmul_trans(mixed, out_full).astype(jnp.bfloat16), "tp").astype(
        jnp.float32
    )
    middle = inputs_f + RESIDUAL * branch_a
    ffn_full = (
        lax.all_gather(gain_ffn.astype(jnp.bfloat16), ("fsdp", "ctx"), axis=0, tiled=True).astype(
            gain_ffn.dtype
        ),
        lax.all_gather(gate_weight, ("fsdp", "ctx"), axis=0, tiled=True),
        lax.all_gather(up_weight, ("fsdp", "ctx"), axis=0, tiled=True),
        lax.all_gather(down_weight, ("fsdp", "ctx"), axis=0, tiled=True),
    )
    gain_f, gate_full, up_full, down_full = ffn_full
    inv_f = lax.rsqrt(jnp.mean(middle * middle, axis=-1, keepdims=True) + EPSILON)
    unit_f = middle * inv_f
    normed_f = (unit_f * gain_f).astype(bfloat)
    gate_pre = matmul_low(normed_f, gate_full)
    upward = matmul_low(normed_f, up_full)
    sigma = jax.nn.sigmoid(gate_pre)
    active = gate_pre * sigma
    hidden = (active * upward).astype(bfloat)
    branch_f = lax.psum(matmul_trans(hidden, down_full).astype(jnp.bfloat16), "tp").astype(
        jnp.float32
    )
    layer_out = (middle + RESIDUAL * branch_f).astype(bfloat).reshape(seqs_here, rows_here, width)
    gain_fb, gate_back, up_back, down_back = (
        lax.all_gather(gain_ffn.astype(jnp.bfloat16), ("fsdp", "ctx"), axis=0, tiled=True).astype(
            gain_ffn.dtype
        ),
        lax.all_gather(gate_weight, ("fsdp", "ctx"), axis=0, tiled=True),
        lax.all_gather(up_weight, ("fsdp", "ctx"), axis=0, tiled=True),
        lax.all_gather(down_weight, ("fsdp", "ctx"), axis=0, tiled=True),
    )
    grad_y = cotangent.reshape(tokens, width).astype(jnp.float32)
    d_branch_f = (RESIDUAL * grad_y).astype(bfloat)
    grad_down = matmul_outer(d_branch_f, hidden)
    d_hidden = matmul_low(d_branch_f, down_back)
    d_gate = (d_hidden * upward * sigma * (1.0 + gate_pre * (1.0 - sigma))).astype(bfloat)
    d_up = (d_hidden * active).astype(bfloat)
    grad_gate = matmul_outer(normed_f, d_gate)
    grad_up = matmul_outer(normed_f, d_up)
    d_normed_f = lax.psum(
        (matmul_trans(d_gate, gate_back) + matmul_trans(d_up, up_back)).astype(jnp.bfloat16), "tp"
    ).astype(jnp.float32)
    grad_gain_ffn = jnp.sum(d_normed_f * unit_f, axis=0)
    d_middle = grad_y + norm_back(d_normed_f, gain_fb, unit_f, inv_f)
    ffn_grads = (
        lax.psum_scatter(grad_gain_ffn, ("fsdp", "ctx"), scatter_dimension=0, tiled=True),
        reduce_low(grad_gate),
        reduce_low(grad_up),
        reduce_low(grad_down),
    )
    gain_ab, query_back, key_back, value_back, out_back = (
        lax.all_gather(gain_attn.astype(jnp.bfloat16), ("fsdp", "ctx"), axis=0, tiled=True).astype(
            gain_attn.dtype
        ),
        lax.all_gather(query_weight, ("fsdp", "ctx"), axis=0, tiled=True),
        lax.all_gather(key_weight, ("fsdp", "ctx"), axis=0, tiled=True),
        lax.all_gather(value_weight, ("fsdp", "ctx"), axis=0, tiled=True),
        lax.all_gather(out_weight, ("fsdp", "ctx"), axis=0, tiled=True),
    )
    d_branch_a = (RESIDUAL * d_middle).astype(bfloat)
    grad_out = matmul_outer(d_branch_a, mixed)
    d_mixed = (
        matmul_low(d_branch_a, out_back)
        .astype(bfloat)
        .reshape(seqs_here, rows_here, kv_local, group_size, HD)
    )
    probs_again = jnp.exp(masked_scores() - log_total)
    probs_again_low = probs_again.astype(bfloat)
    d_probs = jnp.einsum(
        "srngd,slnd->sngrl", d_mixed, value_all, preferred_element_type=jnp.float32
    )
    inner = jnp.sum(probs_again * d_probs, axis=-1, keepdims=True)
    d_scores = (probs_again * (d_probs - inner)).astype(bfloat)
    d_query_rot = (
        jnp.einsum("sngrl,slnd->srngd", d_scores, key_all, preferred_element_type=jnp.float32)
        * SCALE
    )
    d_key_all = (
        jnp.einsum("sngrl,srngd->slnd", d_scores, query_rot, preferred_element_type=jnp.float32)
        * SCALE
    )
    d_value_all = jnp.einsum(
        "sngrl,srngd->slnd", probs_again_low, d_mixed, preferred_element_type=jnp.float32
    )
    d_key_own, d_value_own = (
        lax.psum_scatter(
            d_key_all.reshape(seqs_here, length, kv_local * HD).astype(jnp.bfloat16),
            "ctx",
            scatter_dimension=1,
            tiled=True,
        ).astype(jnp.float32),
        lax.psum_scatter(
            d_value_all.reshape(seqs_here, length, kv_local * HD).astype(jnp.bfloat16),
            "ctx",
            scatter_dimension=1,
            tiled=True,
        ).astype(jnp.float32),
    )
    d_query = (
        rotate_pairs(d_query_rot, cosine[:, :, None, None, :], -sine[:, :, None, None, :])
        .astype(bfloat)
        .reshape(tokens, head_cols)
    )
    d_key = rotate_pairs(
        d_key_own.reshape(seqs_here, rows_here, kv_local, HD),
        cosine[:, :, None, :],
        -sine[:, :, None, :],
    )
    d_key = d_key.astype(bfloat).reshape(tokens, kv_local * HD)
    d_value = d_value_own.reshape(tokens, kv_local * HD).astype(bfloat)
    grad_query = matmul_outer(normed_a, d_query)
    grad_key = matmul_outer(normed_a, d_key)
    grad_value = matmul_outer(normed_a, d_value)
    d_normed_part = (
        matmul_trans(d_query, query_back)
        + matmul_trans(d_key, key_back)
        + matmul_trans(d_value, value_back)
    )
    d_normed_a = lax.psum(d_normed_part.astype(jnp.bfloat16), "tp").astype(jnp.float32)
    grad_gain_attn = jnp.sum(d_normed_a * unit_a, axis=0)
    input_grad = (d_middle + norm_back(d_normed_a, gain_ab, unit_a, inv_a)).reshape(
        seqs_here, rows_here, width
    )
    attn_grads = (
        lax.psum_scatter(grad_gain_attn, ("fsdp", "ctx"), scatter_dimension=0, tiled=True),
        reduce_low(grad_query),
        reduce_low(grad_key),
        reduce_low(grad_value),
        reduce_low(grad_out),
    )
    return (
        layer_out,
        input_grad,
        attn_grads[0],
        attn_grads[1],
        attn_grads[2],
        attn_grads[3],
        attn_grads[4],
        ffn_grads[0],
        ffn_grads[1],
        ffn_grads[2],
        ffn_grads[3],
    )


MAX_DOC = 512
LANES = 128
NEG = -1e30


def half_lanes(rows):
    lane = lax.broadcasted_iota(jnp.int32, (rows, LANES), 1)
    return lane % HD < HD // 2, lane < HD


def turn(slab, cosine, sine_signed):
    first, _ = half_lanes(slab.shape[0])
    swapped = jnp.where(
        first,
        pltpu.roll(slab, LANES - HD // 2, 1),
        pltpu.roll(slab, HD // 2, 1),
    )
    return slab * cosine + swapped * sine_signed


def dot_nt(left, right):
    return lax.dot_general(left, right, (((1,), (1,)), ((), ())), preferred_element_type=jnp.float32)


def dot_tn(left, right):
    return lax.dot_general(left, right, (((0,), (0,)), ((), ())), preferred_element_type=jnp.float32)


def window_mask(start, first_query, first_key, rows, keys):
    query = first_query + lax.broadcasted_iota(jnp.int32, (rows, keys), 0)
    key = first_key + lax.broadcasted_iota(jnp.int32, (rows, keys), 1)
    return (key <= query) & (key >= start)


def attend_kernel(
    rows, window, heads, place_ref, qkv_ref, inv_ref, cos_ref, sin_ref, start_ref,
    query_ref, kv_ref, mixed_ref, lse_ref, keys, values,
):
    step = pl.program_id(1)
    _, low_half = half_lanes(rows)
    inv = inv_ref[...]
    cosine, sine = cos_ref[...], sin_ref[...]

    @pl.when(step == 0)
    def _():
        keys[...] = jnp.zeros_like(keys)
        values[...] = jnp.zeros_like(values)

    width = heads * HD
    raw = qkv_ref[:, width:] * inv
    kv = jnp.where(low_half, turn(raw, cosine, sine), raw)
    kv_ref[...] = kv.astype(jnp.bfloat16)
    moved = pltpu.roll(kv, HD, 1)
    own = pl.ds(pl.multiple_of(step * rows, rows), rows)
    keys[own, :] = jnp.where(low_half, kv, moved).astype(jnp.bfloat16)
    values[own, :] = jnp.where(low_half, moved, kv).astype(jnp.bfloat16)

    first_key = pl.multiple_of(jnp.maximum((step + 1) * rows - window, 0), rows)
    keys_w = keys[pl.ds(first_key, window), :]
    values_w = values[pl.ds(first_key, window), :]
    allowed = window_mask(start_ref[...], step * rows, first_key, rows, window)
    for slab in range(width // LANES):
        at = slice(slab * LANES, (slab + 1) * LANES)
        rot = turn(qkv_ref[:, at] * inv, cosine, sine).astype(jnp.bfloat16)
        query_ref[:, at] = rot
        both = []
        for part in range(2):
            mine = low_half if part == 0 else jnp.logical_not(low_half)
            one = jnp.where(mine, rot, jnp.zeros_like(rot))
            scores = jnp.where(allowed, dot_nt(one, keys_w) * SCALE, NEG)
            highest = jnp.max(scores, axis=1, keepdims=True)
            raised = jnp.exp(scores - highest)
            total = jnp.sum(raised, axis=1, keepdims=True)
            mixed = jnp.dot(
                raised.astype(jnp.bfloat16), values_w, preferred_element_type=jnp.float32
            )
            both.append(mixed / total)
            head = slab * 2 + part
            lse_ref[:, head : head + 1] = highest + jnp.log(total)
        mixed_ref[:, at] = jnp.where(low_half, both[0], both[1]).astype(jnp.bfloat16)


def attend_back_kernel(
    rows, window, heads, blocks, place_ref, query_ref, kv_ref, lse_ref, grad_ref, inv_ref, cos_ref, sin_ref, start_ref,
    out_ref, keys, values, d_keys, d_values,
):
    seq = pl.program_id(0)
    step = blocks - 1 - pl.program_id(1)
    _, low_half = half_lanes(rows)
    inv = inv_ref[...]
    cosine, sine = cos_ref[...], sin_ref[...]

    @pl.when(step == blocks - 1)
    def _():
        for block in range(blocks):
            source = pl.multiple_of(place_ref[seq * blocks + block] * rows, rows)
            kv = kv_ref[pl.ds(source, rows), :].astype(jnp.float32)
            moved = pltpu.roll(kv, HD, 1)
            at = slice(block * rows, (block + 1) * rows)
            keys[at, :] = jnp.where(low_half, kv, moved).astype(jnp.bfloat16)
            values[at, :] = jnp.where(low_half, moved, kv).astype(jnp.bfloat16)
        d_keys[...] = jnp.zeros_like(d_keys)
        d_values[...] = jnp.zeros_like(d_values)

    first_key = pl.multiple_of(jnp.maximum((step + 1) * rows - window, 0), rows)
    span = pl.ds(first_key, window)
    keys_w = keys[span, :]
    values_w = values[span, :]
    allowed = window_mask(start_ref[...], step * rows, first_key, rows, window)
    d_keys_w = jnp.zeros((window, LANES), jnp.float32)
    d_values_w = jnp.zeros((window, LANES), jnp.float32)
    width = heads * HD
    for slab in range(width // LANES):
        at = slice(slab * LANES, (slab + 1) * LANES)
        query, grad = query_ref[:, at], grad_ref[:, at]
        both = []
        for part in range(2):
            mine = low_half if part == 0 else jnp.logical_not(low_half)
            head = slab * 2 + part
            one = jnp.where(mine, query, jnp.zeros_like(query))
            one_grad = jnp.where(mine, grad, jnp.zeros_like(grad))
            scores = dot_nt(one, keys_w) * SCALE - lse_ref[:, head : head + 1]
            probs = jnp.exp(jnp.where(allowed, scores, NEG))
            d_probs = dot_nt(one_grad, values_w)
            inner = jnp.sum(probs * d_probs, axis=1, keepdims=True)
            d_scores = (probs * (d_probs - inner)).astype(jnp.bfloat16)
            both.append(jnp.dot(d_scores, keys_w, preferred_element_type=jnp.float32))
            d_keys_w = d_keys_w + dot_tn(d_scores, one)
            d_values_w = d_values_w + dot_tn(probs.astype(jnp.bfloat16), one_grad)
        d_query = jnp.where(low_half, both[0], both[1]) * SCALE
        out_ref[:, at] = (turn(d_query, cosine, -sine) * inv).astype(jnp.bfloat16)
    d_keys[span, :] += d_keys_w
    d_values[span, :] += d_values_w
    own = pl.ds(pl.multiple_of(step * rows, rows), rows)
    d_key = d_keys[own, :] * SCALE
    d_key = turn(d_key + pltpu.roll(d_key, HD, 1), cosine, -sine)
    d_value = d_values[own, :]
    d_value = d_value + pltpu.roll(d_value, HD, 1)
    out_ref[:, width:] = (jnp.where(low_half, d_key, d_value) * inv).astype(jnp.bfloat16)


def attend(place, qkv, inv, cosine, sine, start, seqs, blocks, rows, heads):
    tokens = qkv.shape[0]
    width = heads * HD
    window = min(blocks * rows, rows + -(-MAX_DOC // rows) * rows)

    def placed(cols):
        return pl.BlockSpec((rows, cols), lambda s, i, place: (place[s * blocks + i], 0))

    def natural(cols):
        return pl.BlockSpec((rows, cols), lambda s, i, place: (s * blocks + i, 0))

    return pl.pallas_call(
        functools.partial(attend_kernel, rows, window, heads),
        out_shape=(
            jax.ShapeDtypeStruct((tokens, width), jnp.bfloat16),
            jax.ShapeDtypeStruct((tokens, LANES), jnp.bfloat16),
            jax.ShapeDtypeStruct((tokens, width), jnp.bfloat16),
            jax.ShapeDtypeStruct((tokens, heads), jnp.float32),
        ),
        grid_spec=pltpu.PrefetchScalarGridSpec(
            num_scalar_prefetch=1,
            grid=(seqs, blocks),
            in_specs=[placed(width + LANES), placed(1), natural(LANES), natural(LANES), natural(1)],
            out_specs=[placed(width), placed(LANES), placed(width), placed(heads)],
            scratch_shapes=[pltpu.VMEM((blocks * rows, LANES), jnp.bfloat16)] * 2,
        ),
        compiler_params=pltpu.CompilerParams(vmem_limit_bytes=48 << 20),
        name="attend",
    )(place, qkv, inv, cosine, sine, start)


def attend_back(place, query, kv, lse, grad, inv, cosine, sine, start, seqs, blocks, rows, heads):
    tokens = query.shape[0]
    width = heads * HD
    window = min(blocks * rows, rows + -(-MAX_DOC // rows) * rows)

    def placed(cols):
        return pl.BlockSpec(
            (rows, cols), lambda s, i, place: (place[s * blocks + blocks - 1 - i], 0)
        )

    def natural(cols):
        return pl.BlockSpec((rows, cols), lambda s, i, place: (s * blocks + blocks - 1 - i, 0))

    return pl.pallas_call(
        functools.partial(attend_back_kernel, rows, window, heads, blocks),
        out_shape=jax.ShapeDtypeStruct((tokens, width + LANES), jnp.bfloat16),
        grid_spec=pltpu.PrefetchScalarGridSpec(
            num_scalar_prefetch=1,
            grid=(seqs, blocks),
            in_specs=[
                placed(width),
                pl.BlockSpec((tokens, LANES), lambda s, i, place: (0, 0)),
                placed(heads),
                placed(width),
                placed(1),
                natural(LANES),
                natural(LANES),
                natural(1),
            ],
            out_specs=placed(width + LANES),
            scratch_shapes=[pltpu.VMEM((blocks * rows, LANES), jnp.bfloat16)] * 2
            + [pltpu.VMEM((blocks * rows, LANES), jnp.float32)] * 2,
        ),
        compiler_params=pltpu.CompilerParams(vmem_limit_bytes=48 << 20),
        name="attend_back",
    )(place, query, kv, lse, grad, inv, cosine, sine, start)


def tied(value, *others):
    return lax.optimization_barrier((value, *others))[0]


def group_shards(
    group, cores,
    hidden_in, segments, gain_attn, query_weight, key_weight, value_weight, out_weight,
    gain_ffn, gate_weight, up_weight, down_weight, cotangent,
):
    bfloat = jnp.bfloat16
    seqs_here, rows_here, width = hidden_in.shape
    length = segments.shape[1]
    rows = rows_here // cores
    near = group // (length // rows_here)
    blocks = length // rows
    heads = HQ // KVH
    me = lax.axis_index(("near", "ctx"))
    me_core = lax.axis_index("tp")

    def swap(value, m):
        return lax.ppermute(value, ("near", "ctx"), [(i, i ^ m) for i in range(group)])

    def swap_core(value):
        return lax.ppermute(value, "tp", [(0, 1), (1, 0)])

    def gather(own):
        same = [own] + [swap(own, m) for m in range(1, group)]
        return same, jnp.concatenate(same + [swap_core(v) for v in same], axis=0)

    def scatter(product, left):
        half = group * rows
        other = swap_core(product(left[half:]).astype(bfloat))
        mine = product(left[:half]) + other.astype(jnp.float32)
        low = mine.astype(bfloat)
        total = mine[:rows]
        for m in range(1, group):
            total = total + swap(low[m * rows : (m + 1) * rows], m).astype(jnp.float32)
        return total

    def own_half(value):
        return lax.dynamic_slice_in_dim(value, me_core * rows, rows, 0)

    def both_halves(own):
        other = swap_core(own)
        whole = jnp.zeros((rows_here, own.shape[1]), own.dtype)
        whole = lax.dynamic_update_slice_in_dim(whole, own, me_core * rows, 0)
        return lax.dynamic_update_slice_in_dim(whole, other, (1 - me_core) * rows, 0)

    def to_columns(weight):
        deep, cols = weight.shape[0], weight.shape[1] // group
        whole = jnp.zeros((group * deep, cols), weight.dtype)
        for m in range(group):
            piece = lax.dynamic_slice_in_dim(weight, (me ^ m) * cols, cols, 1)
            piece = swap(piece, m) if m else piece
            whole = lax.dynamic_update_slice_in_dim(whole, piece, (me ^ m) * deep, 0)
        return whole

    def to_rows(grad):
        deep, cols = grad.shape[0] // group, grad.shape[1]
        whole = jnp.zeros((deep, group * cols), grad.dtype)
        for m in range(group):
            piece = lax.dynamic_slice_in_dim(grad, (me ^ m) * deep, deep, 0)
            piece = swap(piece, m) if m else piece
            whole = lax.dynamic_update_slice_in_dim(whole, piece, (me ^ m) * cols, 1)
        return whole

    def far_gather(weight):
        return lax.all_gather(weight, "far", axis=0, tiled=True)

    def far_scatter(grad):
        low = lax.psum_scatter(grad.astype(bfloat), "far", scatter_dimension=0, tiled=True)
        return to_rows(low).astype(jnp.float32)

    deep = query_weight.shape[0]
    col_gain_a, col_gain_f = gain_attn[:, None], gain_ffn[:, None]

    def scaled(weight, gain):
        return (weight.astype(jnp.float32) * gain).astype(bfloat)

    def chunks(weight):
        return weight.reshape(deep, group, weight.shape[1] // group)

    attn_local = jnp.concatenate(
        [
            chunks(scaled(query_weight, col_gain_a)),
            chunks(scaled(key_weight, col_gain_a)),
            chunks(scaled(value_weight, col_gain_a)),
            chunks(out_weight),
        ],
        axis=2,
    ).reshape(deep, -1)
    attn_cols = to_columns(attn_local)
    attn_w = far_gather(attn_cols)
    head_cols = heads * HD
    in_w, out_w = attn_w[:, : head_cols + 2 * HD], attn_w[:, head_cols + 2 * HD :]

    own_in = tied(own_half(hidden_in.reshape(rows_here, width)), attn_cols)
    pieces, inputs = gather(own_in)
    last = pieces[-1]
    gate_cols = to_columns(tied(scaled(gate_weight, col_gain_f), last))
    up_cols = to_columns(tied(scaled(up_weight, col_gain_f), gate_cols))
    down_cols = to_columns(tied(down_weight, up_cols))
    gate_w = far_gather(gate_cols)
    up_w = far_gather(up_cols)
    down_w = far_gather(down_cols)
    own_cot = own_half(cotangent.reshape(rows_here, width))
    _, cots = gather(tied(own_cot, down_cols))

    seg_all = jnp.concatenate(
        [segments]
        + [swap(segments, n * (group // near)) for n in range(1, near)],
        axis=0,
    )
    start = jnp.sum((seg_all[:, None, :] < seg_all[:, :, None]).astype(jnp.int32), axis=2)
    places = (jnp.arange(length, dtype=jnp.int32)[None, :] - start).astype(jnp.float32)
    freqs = THETA ** (-jnp.arange(0, HD, 2, dtype=jnp.float32) / HD)
    phase = places.reshape(-1)[:, None] * freqs
    cosine, sine = jnp.cos(phase), jnp.sin(phase)
    cosine = jnp.concatenate([cosine, cosine, cosine, cosine], axis=1)
    sine = jnp.concatenate([-sine, sine, -sine, sine], axis=1)
    start = start.reshape(-1)[:, None]
    at = jnp.arange(near * blocks, dtype=jnp.int32)
    in_seq = at % blocks
    here_ctx = lax.axis_index("ctx")
    place = (
        ((in_seq % cores) ^ me_core) * group
        + (at // blocks) * (group // near)
        + ((in_seq // cores) ^ here_ctx)
    ).astype(jnp.int32)

    def inverse_rms(values):
        values = values.astype(jnp.float32)
        return lax.rsqrt(jnp.mean(values * values, axis=-1, keepdims=True) + EPSILON)

    inv_a = inverse_rms(inputs)
    qkv = matmul_low(inputs, in_w)
    query, kv, mixed, lse = attend(
        place, qkv, inv_a, cosine, sine, start, near, blocks, rows, heads
    )
    branch_a = scatter(lambda left: matmul_trans(left, out_w), mixed)
    own_f = own_in.astype(jnp.float32)
    middle = own_f + RESIDUAL * branch_a

    _, mids = gather(middle.astype(bfloat))
    inv_f = inverse_rms(mids)
    gate_pre = matmul_low(mids, gate_w) * inv_f
    upward = matmul_low(mids, up_w) * inv_f
    sigma = jax.nn.sigmoid(gate_pre)
    active = gate_pre * sigma
    hidden = (active * upward).astype(bfloat)
    branch_f = scatter(lambda left: matmul_trans(left, down_w), hidden)
    layer_out = both_halves((middle + RESIDUAL * branch_f).astype(bfloat))
    grad_down = far_scatter(matmul_outer(cots, hidden)) * RESIDUAL
    d_hidden = matmul_low(cots, down_w) * RESIDUAL
    d_gate = (inv_f * (d_hidden * upward * sigma * (1.0 + gate_pre * (1.0 - sigma)))).astype(bfloat)
    d_up = (inv_f * (d_hidden * active)).astype(bfloat)
    grad_gate = far_scatter(matmul_outer(mids, d_gate))
    grad_up = far_scatter(matmul_outer(mids, d_up))
    both = jnp.concatenate([d_gate, d_up], axis=1)
    back_f = scatter(
        lambda left: matmul_trans(left[:, : d_gate.shape[1]], gate_w)
        + matmul_trans(left[:, d_gate.shape[1] :], up_w),
        both,
    )

    def through_norm(grad, unit):
        return grad - unit * jnp.mean(grad * unit, axis=-1, keepdims=True)

    d_middle = own_cot.astype(jnp.float32) + through_norm(back_f, middle * inverse_rms(middle))

    _, d_mids = gather(d_middle.astype(bfloat))
    d_mixed = (matmul_low(d_mids, out_w) * RESIDUAL).astype(bfloat)
    grad_out_part = matmul_outer(d_mids, mixed) * RESIDUAL
    d_qkv = attend_back(
        place, query, kv, lse, d_mixed, inv_a, cosine, sine, start, near, blocks, rows, heads
    )
    grad_attn = jnp.concatenate(
        [matmul_outer(inputs, d_qkv).astype(bfloat), grad_out_part.astype(bfloat)], axis=1
    )
    grad_attn = far_scatter(grad_attn).reshape(deep, group, -1)
    back_a = scatter(lambda left: matmul_trans(left, in_w), d_qkv)
    input_grad = d_middle + through_norm(back_a, own_f * inverse_rms(own_f))
    input_grad = both_halves(input_grad)

    def cut(first, size):
        return grad_attn[:, :, first : first + size].reshape(deep, group * size)

    grad_query, grad_key, grad_value, grad_out = (
        cut(0, head_cols),
        cut(head_cols, HD),
        cut(head_cols + HD, HD),
        cut(head_cols + 2 * HD, head_cols),
    )

    def row_sum(*pairs):
        return sum(jnp.sum(weight.astype(jnp.float32) * grad, axis=1) for weight, grad in pairs)

    gain_grads = jnp.stack(
        [
            row_sum(
                (query_weight, grad_query), (key_weight, grad_key), (value_weight, grad_value)
            ),
            row_sum((gate_weight, grad_gate), (up_weight, grad_up)),
        ]
    )
    gain_grads = gain_grads + swap_core(gain_grads)
    return (
        layer_out.reshape(hidden_in.shape),
        input_grad.reshape(hidden_in.shape),
        gain_grads[0],
        grad_query * col_gain_a,
        grad_key * col_gain_a,
        grad_value * col_gain_a,
        grad_out,
        gain_grads[1],
        grad_gate * col_gain_f,
        grad_up * col_gain_f,
        grad_down,
    )


def solution(mesh):
    sizes = dict(mesh.shape)
    fsdp, ctx, tp = sizes["fsdp"], sizes["ctx"], sizes["tp"]
    near = KVH // (ctx * tp)
    group = near * ctx
    fits = (
        tuple(mesh.axis_names) == ("fsdp", "ctx", "tp")
        and tp == 2
        and near > 0
        and group * tp == KVH
        and fsdp % near == 0
        and group & (group - 1) == 0
    )
    if fits:
        mesh = Mesh(
            mesh.devices.reshape(fsdp // near, near, ctx, tp), ("far", "near", "ctx", "tp")
        )
        body, data = functools.partial(group_shards, group, tp), ("far", "near")
    else:
        body, data = generic_shards, ("fsdp",)
    owner = (*data, "ctx")
    weight, gain, tokens = P(owner, "tp"), P(owner), P(data, "ctx", None)
    in_specs = (
        tokens,
        P(data, None),
        gain,
        weight,
        weight,
        weight,
        weight,
        gain,
        weight,
        weight,
        weight,
        tokens,
    )
    out_specs = (
        tokens,
        tokens,
        gain,
        weight,
        weight,
        weight,
        weight,
        gain,
        weight,
        weight,
        weight,
    )
    return jax.shard_map(body, mesh=mesh, in_specs=in_specs, out_specs=out_specs, check_vma=False)
```

```python
import functools

import jax
import jax.numpy as jnp
from jax import lax
from jax.experimental import pallas as pl
from jax.experimental.pallas import tpu as pltpu
from jax.sharding import Mesh
from jax.sharding import PartitionSpec as P

HQ = 32
KVH = 8
HD = 64


EPSILON = 1e-05
SCALE = 0.015625
RESIDUAL = 0.22
THETA = 10000000.0


def rotate_pairs(values, cosine, sine):
    half = values.shape[-1] // 2
    swapped = jnp.concatenate([-values[..., half:], values[..., :half]], axis=-1)
    return values * cosine + swapped * sine


def matmul_low(left, right):
    return jnp.dot(left, right, preferred_element_type=jnp.float32)


def matmul_trans(left, right):
    return lax.dot_general(
        left, right, (((1,), (1,)), ((), ())), preferred_element_type=jnp.float32
    )


def matmul_outer(left, right):
    return lax.dot_general(
        left, right, (((0,), (0,)), ((), ())), preferred_element_type=jnp.float32
    )


def norm_back(grad_normed, gain, unit_rows, inv_rms):
    scaled = grad_normed * gain
    return inv_rms * (scaled - unit_rows * jnp.mean(scaled * unit_rows, axis=-1, keepdims=True))


def reduce_low(grad):
    low = lax.psum_scatter(
        grad.astype(jnp.bfloat16), ("fsdp", "ctx"), scatter_dimension=0, tiled=True
    )
    return low.astype(jnp.float32)


def generic_shards(
    hidden_in,
    segments,
    gain_attn,
    query_weight,
    key_weight,
    value_weight,
    out_weight,
    gain_ffn,
    gate_weight,
    up_weight,
    down_weight,
    cotangent,
):
    seqs_here, rows_here, width = hidden_in.shape
    length = segments.shape[1]
    tokens = seqs_here * rows_here
    kv_local = key_weight.shape[1] // HD
    group_size = HQ // KVH
    head_cols = kv_local * group_size * HD
    bfloat = jnp.bfloat16
    first_row = lax.axis_index("ctx") * rows_here
    own_seg = lax.dynamic_slice_in_dim(segments, first_row, rows_here, 1)
    before = jnp.sum((segments[:, None, :] < own_seg[:, :, None]).astype(jnp.int32), axis=2)
    own_place = first_row + jnp.arange(rows_here, dtype=jnp.int32)
    places = (own_place[None, :] - before).astype(jnp.float32)
    freqs = THETA ** (-jnp.arange(0, HD, 2, dtype=jnp.float32) / HD)
    phase = places[:, :, None] * freqs
    phase = jnp.concatenate([phase, phase], axis=-1)
    cosine = jnp.cos(phase)
    sine = jnp.sin(phase)
    key_place = jnp.arange(length, dtype=jnp.int32)
    allowed = (own_seg[:, :, None] == segments[:, None, :]) & (
        key_place[None, None, :] <= own_place[None, :, None]
    )
    allowed = allowed[:, None, None, :, :]
    attn_full = (
        lax.all_gather(gain_attn.astype(jnp.bfloat16), ("fsdp", "ctx"), axis=0, tiled=True).astype(
            gain_attn.dtype
        ),
        lax.all_gather(query_weight, ("fsdp", "ctx"), axis=0, tiled=True),
        lax.all_gather(key_weight, ("fsdp", "ctx"), axis=0, tiled=True),
        lax.all_gather(value_weight, ("fsdp", "ctx"), axis=0, tiled=True),
        lax.all_gather(out_weight, ("fsdp", "ctx"), axis=0, tiled=True),
    )
    gain_a, query_full, key_full, value_full, out_full = attn_full
    inputs_f = hidden_in.reshape(tokens, width).astype(jnp.float32)
    inv_a = lax.rsqrt(jnp.mean(inputs_f * inputs_f, axis=-1, keepdims=True) + EPSILON)
    unit_a = inputs_f * inv_a
    normed_a = (unit_a * gain_a).astype(bfloat)
    query_raw = matmul_low(normed_a, query_full).reshape(
        seqs_here, rows_here, kv_local, group_size, HD
    )
    key_raw = matmul_low(normed_a, key_full).reshape(seqs_here, rows_here, kv_local, HD)
    value_low = (
        matmul_low(normed_a, value_full).astype(bfloat).reshape(seqs_here, rows_here, kv_local * HD)
    )
    query_rot = rotate_pairs(
        query_raw, cosine[:, :, None, None, :], sine[:, :, None, None, :]
    ).astype(bfloat)
    key_rot = rotate_pairs(key_raw, cosine[:, :, None, :], sine[:, :, None, :]).astype(bfloat)
    key_rot = key_rot.reshape(seqs_here, rows_here, kv_local * HD)
    key_all, value_all = (
        lax.all_gather(key_rot, "ctx", axis=1, tiled=True),
        lax.all_gather(value_low, "ctx", axis=1, tiled=True),
    )
    key_all = key_all.reshape(seqs_here, length, kv_local, HD)
    value_all = value_all.reshape(seqs_here, length, kv_local, HD)

    def masked_scores():
        scores = (
            jnp.einsum("srngd,slnd->sngrl", query_rot, key_all, preferred_element_type=jnp.float32)
            * SCALE
        )
        return jnp.where(allowed, scores, -1e30)

    scores = masked_scores()
    highest = jnp.max(scores, axis=-1, keepdims=True)
    raised = jnp.exp(scores - highest)
    totals = jnp.sum(raised, axis=-1, keepdims=True)
    log_total = highest + jnp.log(totals)
    probs_low = (raised / totals).astype(bfloat)
    mixed = jnp.einsum(
        "sngrl,slnd->srngd", probs_low, value_all, preferred_element_type=jnp.float32
    )
    mixed = mixed.astype(bfloat).reshape(tokens, head_cols)
    branch_a = lax.psum(matmul_trans(mixed, out_full).astype(jnp.bfloat16), "tp").astype(
        jnp.float32
    )
    middle = inputs_f + RESIDUAL * branch_a
    ffn_full = (
        lax.all_gather(gain_ffn.astype(jnp.bfloat16), ("fsdp", "ctx"), axis=0, tiled=True).astype(
            gain_ffn.dtype
        ),
        lax.all_gather(gate_weight, ("fsdp", "ctx"), axis=0, tiled=True),
        lax.all_gather(up_weight, ("fsdp", "ctx"), axis=0, tiled=True),
        lax.all_gather(down_weight, ("fsdp", "ctx"), axis=0, tiled=True),
    )
    gain_f, gate_full, up_full, down_full = ffn_full
    inv_f = lax.rsqrt(jnp.mean(middle * middle, axis=-1, keepdims=True) + EPSILON)
    unit_f = middle * inv_f
    normed_f = (unit_f * gain_f).astype(bfloat)
    gate_pre = matmul_low(normed_f, gate_full)
    upward = matmul_low(normed_f, up_full)
    sigma = jax.nn.sigmoid(gate_pre)
    active = gate_pre * sigma
    hidden = (active * upward).astype(bfloat)
    branch_f = lax.psum(matmul_trans(hidden, down_full).astype(jnp.bfloat16), "tp").astype(
        jnp.float32
    )
    layer_out = (middle + RESIDUAL * branch_f).astype(bfloat).reshape(seqs_here, rows_here, width)
    gain_fb, gate_back, up_back, down_back = (
        lax.all_gather(gain_ffn.astype(jnp.bfloat16), ("fsdp", "ctx"), axis=0, tiled=True).astype(
            gain_ffn.dtype
        ),
        lax.all_gather(gate_weight, ("fsdp", "ctx"), axis=0, tiled=True),
        lax.all_gather(up_weight, ("fsdp", "ctx"), axis=0, tiled=True),
        lax.all_gather(down_weight, ("fsdp", "ctx"), axis=0, tiled=True),
    )
    grad_y = cotangent.reshape(tokens, width).astype(jnp.float32)
    d_branch_f = (RESIDUAL * grad_y).astype(bfloat)
    grad_down = matmul_outer(d_branch_f, hidden)
    d_hidden = matmul_low(d_branch_f, down_back)
    d_gate = (d_hidden * upward * sigma * (1.0 + gate_pre * (1.0 - sigma))).astype(bfloat)
    d_up = (d_hidden * active).astype(bfloat)
    grad_gate = matmul_outer(normed_f, d_gate)
    grad_up = matmul_outer(normed_f, d_up)
    d_normed_f = lax.psum(
        (matmul_trans(d_gate, gate_back) + matmul_trans(d_up, up_back)).astype(jnp.bfloat16), "tp"
    ).astype(jnp.float32)
    grad_gain_ffn = jnp.sum(d_normed_f * unit_f, axis=0)
    d_middle = grad_y + norm_back(d_normed_f, gain_fb, unit_f, inv_f)
    ffn_grads = (
        lax.psum_scatter(grad_gain_ffn, ("fsdp", "ctx"), scatter_dimension=0, tiled=True),
        reduce_low(grad_gate),
        reduce_low(grad_up),
        reduce_low(grad_down),
    )
    gain_ab, query_back, key_back, value_back, out_back = (
        lax.all_gather(gain_attn.astype(jnp.bfloat16), ("fsdp", "ctx"), axis=0, tiled=True).astype(
            gain_attn.dtype
        ),
        lax.all_gather(query_weight, ("fsdp", "ctx"), axis=0, tiled=True),
        lax.all_gather(key_weight, ("fsdp", "ctx"), axis=0, tiled=True),
        lax.all_gather(value_weight, ("fsdp", "ctx"), axis=0, tiled=True),
        lax.all_gather(out_weight, ("fsdp", "ctx"), axis=0, tiled=True),
    )
    d_branch_a = (RESIDUAL * d_middle).astype(bfloat)
    grad_out = matmul_outer(d_branch_a, mixed)
    d_mixed = (
        matmul_low(d_branch_a, out_back)
        .astype(bfloat)
        .reshape(seqs_here, rows_here, kv_local, group_size, HD)
    )
    probs_again = jnp.exp(masked_scores() - log_total)
    probs_again_low = probs_again.astype(bfloat)
    d_probs = jnp.einsum(
        "srngd,slnd->sngrl", d_mixed, value_all, preferred_element_type=jnp.float32
    )
    inner = jnp.sum(probs_again * d_probs, axis=-1, keepdims=True)
    d_scores = (probs_again * (d_probs - inner)).astype(bfloat)
    d_query_rot = (
        jnp.einsum("sngrl,slnd->srngd", d_scores, key_all, preferred_element_type=jnp.float32)
        * SCALE
    )
    d_key_all = (
        jnp.einsum("sngrl,srngd->slnd", d_scores, query_rot, preferred_element_type=jnp.float32)
        * SCALE
    )
    d_value_all = jnp.einsum(
        "sngrl,srngd->slnd", probs_again_low, d_mixed, preferred_element_type=jnp.float32
    )
    d_key_own, d_value_own = (
        lax.psum_scatter(
            d_key_all.reshape(seqs_here, length, kv_local * HD).astype(jnp.bfloat16),
            "ctx",
            scatter_dimension=1,
            tiled=True,
        ).astype(jnp.float32),
        lax.psum_scatter(
            d_value_all.reshape(seqs_here, length, kv_local * HD).astype(jnp.bfloat16),
            "ctx",
            scatter_dimension=1,
            tiled=True,
        ).astype(jnp.float32),
    )
    d_query = (
        rotate_pairs(d_query_rot, cosine[:, :, None, None, :], -sine[:, :, None, None, :])
        .astype(bfloat)
        .reshape(tokens, head_cols)
    )
    d_key = rotate_pairs(
        d_key_own.reshape(seqs_here, rows_here, kv_local, HD),
        cosine[:, :, None, :],
        -sine[:, :, None, :],
    )
    d_key = d_key.astype(bfloat).reshape(tokens, kv_local * HD)
    d_value = d_value_own.reshape(tokens, kv_local * HD).astype(bfloat)
    grad_query = matmul_outer(normed_a, d_query)
    grad_key = matmul_outer(normed_a, d_key)
    grad_value = matmul_outer(normed_a, d_value)
    d_normed_part = (
        matmul_trans(d_query, query_back)
        + matmul_trans(d_key, key_back)
        + matmul_trans(d_value, value_back)
    )
    d_normed_a = lax.psum(d_normed_part.astype(jnp.bfloat16), "tp").astype(jnp.float32)
    grad_gain_attn = jnp.sum(d_normed_a * unit_a, axis=0)
    input_grad = (d_middle + norm_back(d_normed_a, gain_ab, unit_a, inv_a)).reshape(
        seqs_here, rows_here, width
    )
    attn_grads = (
        lax.psum_scatter(grad_gain_attn, ("fsdp", "ctx"), scatter_dimension=0, tiled=True),
        reduce_low(grad_query),
        reduce_low(grad_key),
        reduce_low(grad_value),
        reduce_low(grad_out),
    )
    return (
        layer_out,
        input_grad,
        attn_grads[0],
        attn_grads[1],
        attn_grads[2],
        attn_grads[3],
        attn_grads[4],
        ffn_grads[0],
        ffn_grads[1],
        ffn_grads[2],
        ffn_grads[3],
    )


MAX_DOC = 512
LANES = 128
NEG = -1e30


def half_lanes(rows):
    lane = lax.broadcasted_iota(jnp.int32, (rows, LANES), 1)
    return lane % HD < HD // 2, lane < HD


def turn(slab, cosine, sine_signed):
    first, _ = half_lanes(slab.shape[0])
    swapped = jnp.where(
        first,
        pltpu.roll(slab, LANES - HD // 2, 1),
        pltpu.roll(slab, HD // 2, 1),
    )
    return slab * cosine + swapped * sine_signed


def dot_nt(left, right):
    return lax.dot_general(left, right, (((1,), (1,)), ((), ())), preferred_element_type=jnp.float32)


def dot_tn(left, right):
    return lax.dot_general(left, right, (((0,), (0,)), ((), ())), preferred_element_type=jnp.float32)


def window_mask(start, first_query, first_key, rows, keys):
    query = first_query + lax.broadcasted_iota(jnp.int32, (rows, keys), 0)
    key = first_key + lax.broadcasted_iota(jnp.int32, (rows, keys), 1)
    return (key <= query) & (key >= start)


def attend_kernel(
    rows, window, heads, place_ref, qkv_ref, cos_ref, sin_ref, start_ref, *rest,
):
    query_ref, kv_ref, mixed_ref, lse_ref, keys, values = rest[-6:]
    step = pl.program_id(1)
    _, low_half = half_lanes(rows)
    cosine, sine = cos_ref[...], sin_ref[...]

    @pl.when(step == 0)
    def _():
        keys[...] = jnp.zeros_like(keys)
        values[...] = jnp.zeros_like(values)

    width = heads * HD
    raw = qkv_ref[:, width:]
    kv = jnp.where(low_half, turn(raw, cosine, sine), raw)
    kv_ref[...] = kv.astype(jnp.bfloat16)
    moved = pltpu.roll(kv, HD, 1)
    own = pl.ds(pl.multiple_of(step * rows, rows), rows)
    keys[own, :] = jnp.where(low_half, kv, moved).astype(jnp.bfloat16)
    values[own, :] = jnp.where(low_half, moved, kv).astype(jnp.bfloat16)

    first_key = pl.multiple_of(jnp.maximum((step + 1) * rows - window, 0), rows)
    keys_w = keys[pl.ds(first_key, window), :]
    values_w = values[pl.ds(first_key, window), :]
    allowed = window_mask(start_ref[...], step * rows, first_key, rows, window)
    for slab in range(width // LANES):
        at = slice(slab * LANES, (slab + 1) * LANES)
        rot = turn(qkv_ref[:, at], cosine, sine).astype(jnp.bfloat16)
        query_ref[:, at] = rot
        both = []
        for part in range(2):
            mine = low_half if part == 0 else jnp.logical_not(low_half)
            one = jnp.where(mine, rot, jnp.zeros_like(rot))
            scores = jnp.where(allowed, dot_nt(one, keys_w) * SCALE, NEG)
            highest = jnp.max(scores, axis=1, keepdims=True)
            raised = jnp.exp(scores - highest)
            total = jnp.sum(raised, axis=1, keepdims=True)
            mixed = jnp.dot(
                raised.astype(jnp.bfloat16), values_w, preferred_element_type=jnp.float32
            )
            both.append(mixed / total)
            head = slab * 2 + part
            lse_ref[:, head : head + 1] = highest + jnp.log(total)
        mixed_ref[:, at] = jnp.where(low_half, both[0], both[1]).astype(jnp.bfloat16)


def attend_back_kernel(
    rows, window, heads, blocks, place_ref, query_ref, kv_ref, lse_ref, grad_ref, inv_ref, cos_ref, sin_ref, start_ref,
    out_ref, keys, values, d_keys, d_values,
):
    seq = pl.program_id(0)
    step = blocks - 1 - pl.program_id(1)
    _, low_half = half_lanes(rows)
    inv = inv_ref[...]
    cosine, sine = cos_ref[...], sin_ref[...]

    @pl.when(step == blocks - 1)
    def _():
        for block in range(blocks):
            source = pl.multiple_of(place_ref[seq * blocks + block] * rows, rows)
            kv = kv_ref[pl.ds(source, rows), :].astype(jnp.float32)
            moved = pltpu.roll(kv, HD, 1)
            at = slice(block * rows, (block + 1) * rows)
            keys[at, :] = jnp.where(low_half, kv, moved).astype(jnp.bfloat16)
            values[at, :] = jnp.where(low_half, moved, kv).astype(jnp.bfloat16)
        d_keys[...] = jnp.zeros_like(d_keys)
        d_values[...] = jnp.zeros_like(d_values)

    first_key = pl.multiple_of(jnp.maximum((step + 1) * rows - window, 0), rows)
    span = pl.ds(first_key, window)
    keys_w = keys[span, :]
    values_w = values[span, :]
    allowed = window_mask(start_ref[...], step * rows, first_key, rows, window)
    d_keys_w = jnp.zeros((window, LANES), jnp.float32)
    d_values_w = jnp.zeros((window, LANES), jnp.float32)
    width = heads * HD
    for slab in range(width // LANES):
        at = slice(slab * LANES, (slab + 1) * LANES)
        query, grad = query_ref[:, at], grad_ref[:, at]
        both = []
        for part in range(2):
            mine = low_half if part == 0 else jnp.logical_not(low_half)
            head = slab * 2 + part
            one = jnp.where(mine, query, jnp.zeros_like(query))
            one_grad = jnp.where(mine, grad, jnp.zeros_like(grad))
            scores = dot_nt(one, keys_w) * SCALE - lse_ref[:, head : head + 1]
            probs = jnp.exp(jnp.where(allowed, scores, NEG))
            d_probs = dot_nt(one_grad, values_w)
            inner = jnp.sum(probs * d_probs, axis=1, keepdims=True)
            d_scores = (probs * (d_probs - inner)).astype(jnp.bfloat16)
            both.append(jnp.dot(d_scores, keys_w, preferred_element_type=jnp.float32))
            d_keys_w = d_keys_w + dot_tn(d_scores, one)
            d_values_w = d_values_w + dot_tn(probs.astype(jnp.bfloat16), one_grad)
        d_query = jnp.where(low_half, both[0], both[1]) * SCALE
        out_ref[:, at] = (turn(d_query, cosine, -sine) * inv).astype(jnp.bfloat16)
    d_keys[span, :] += d_keys_w
    d_values[span, :] += d_values_w
    own = pl.ds(pl.multiple_of(step * rows, rows), rows)
    d_key = d_keys[own, :] * SCALE
    d_key = turn(d_key + pltpu.roll(d_key, HD, 1), cosine, -sine)
    d_value = d_values[own, :]
    d_value = d_value + pltpu.roll(d_value, HD, 1)
    out_ref[:, width:] = (jnp.where(low_half, d_key, d_value) * inv).astype(jnp.bfloat16)


def attend(place, qkv, cosine, sine, start, seqs, blocks, rows, heads, others):
    tokens = qkv.shape[0]
    width = heads * HD
    window = min(blocks * rows, rows + -(-MAX_DOC // rows) * rows)

    def placed(cols):
        return pl.BlockSpec((rows, cols), lambda s, i, place: (place[s * blocks + i], 0))

    def natural(cols):
        return pl.BlockSpec((rows, cols), lambda s, i, place: (s * blocks + i, 0))

    return pl.pallas_call(
        functools.partial(attend_kernel, rows, window, heads),
        out_shape=(
            jax.ShapeDtypeStruct((tokens, width), jnp.bfloat16),
            jax.ShapeDtypeStruct((tokens, LANES), jnp.bfloat16),
            jax.ShapeDtypeStruct((tokens, width), jnp.bfloat16),
            jax.ShapeDtypeStruct((tokens, heads), jnp.float32),
        ),
        grid_spec=pltpu.PrefetchScalarGridSpec(
            num_scalar_prefetch=1,
            grid=(seqs, blocks),
            in_specs=[placed(width + LANES), natural(LANES), natural(LANES), natural(1)]
            + [ANYWHERE] * len(others),
            out_specs=[placed(width), placed(LANES), placed(width), placed(heads)],
            scratch_shapes=[pltpu.VMEM((blocks * rows, LANES), jnp.bfloat16)] * 2,
        ),
        compiler_params=pltpu.CompilerParams(vmem_limit_bytes=48 << 20),
        name="attend",
    )(place, qkv, cosine, sine, start, *others)


def attend_back(place, query, kv, lse, grad, inv, cosine, sine, start, seqs, blocks, rows, heads):
    tokens = query.shape[0]
    width = heads * HD
    window = min(blocks * rows, rows + -(-MAX_DOC // rows) * rows)

    def placed(cols):
        return pl.BlockSpec(
            (rows, cols), lambda s, i, place: (place[s * blocks + blocks - 1 - i], 0)
        )

    def natural(cols):
        return pl.BlockSpec((rows, cols), lambda s, i, place: (s * blocks + blocks - 1 - i, 0))

    return pl.pallas_call(
        functools.partial(attend_back_kernel, rows, window, heads, blocks),
        out_shape=jax.ShapeDtypeStruct((tokens, width + LANES), jnp.bfloat16),
        grid_spec=pltpu.PrefetchScalarGridSpec(
            num_scalar_prefetch=1,
            grid=(seqs, blocks),
            in_specs=[
                placed(width),
                pl.BlockSpec((tokens, LANES), lambda s, i, place: (0, 0)),
                placed(heads),
                placed(width),
                placed(1),
                natural(LANES),
                natural(LANES),
                natural(1),
            ],
            out_specs=placed(width + LANES),
            scratch_shapes=[pltpu.VMEM((blocks * rows, LANES), jnp.bfloat16)] * 2
            + [pltpu.VMEM((blocks * rows, LANES), jnp.float32)] * 2,
        ),
        compiler_params=pltpu.CompilerParams(vmem_limit_bytes=48 << 20),
        cost_estimate=pl.CostEstimate(
            flops=48 * tokens * window * heads * LANES,
            transcendentals=tokens * window * heads,
            bytes_accessed=tokens * (8 * width + 12 * LANES),
        ),
        name="attend_back",
    )(place, query, kv, lse, grad, inv, cosine, sine, start)


VMEM_LIMIT = 56 << 20
ANYWHERE = pl.BlockSpec(memory_space=pl.ANY)


def fetch(pieces, whole, sems):
    copies, at = [], 0
    for n, piece in enumerate(pieces):
        span = slice(at, at + piece.shape[0])
        copy = pltpu.make_async_copy(piece, whole.at[span, :], sems.at[n])
        copy.start()
        copies.append((copy, span))
        at += piece.shape[0]
    return copies


def inverse_rms(values):
    values = values.astype(jnp.float32)
    return lax.rsqrt(jnp.mean(values * values, axis=-1, keepdims=True) + EPSILON)


def rows_of(pieces):
    return sum(piece.shape[0] for piece in pieces)


def project_kernel(count, tokens, normed, factor, *refs):
    pieces, rest = refs[:count], refs[count + tokens :]
    weight_ref, out_ref = rest[:2]
    whole, sems = rest[-2:]
    for copy, span in fetch(pieces, whole, sems):
        copy.wait()
        values = whole[span, :]
        product = jnp.dot(values, weight_ref[...], preferred_element_type=jnp.float32)
        if normed:
            inv = inverse_rms(values)
            rest[2][span, :] = inv
            product = product * inv
        else:
            product = product * factor
        out_ref[span, :] = product.astype(out_ref.dtype)


def project(pieces, weight, normed, factor, dtype, tokens=()):
    count, width = rows_of(pieces), pieces[0].shape[1]
    out_shape = [jax.ShapeDtypeStruct((count, weight.shape[1]), dtype)]
    if normed:
        out_shape.append(jax.ShapeDtypeStruct((count, 1), jnp.float32))
    vmem = pl.BlockSpec(memory_space=pltpu.VMEM)
    return pl.pallas_call(
        functools.partial(project_kernel, len(pieces), len(tokens), normed, factor),
        out_shape=out_shape,
        in_specs=[ANYWHERE] * (len(pieces) + len(tokens)) + [vmem],
        out_specs=[vmem] * len(out_shape),
        scratch_shapes=[
            pltpu.VMEM((count, width), jnp.bfloat16),
            pltpu.SemaphoreType.DMA((len(pieces),)),
        ],
        compiler_params=pltpu.CompilerParams(vmem_limit_bytes=VMEM_LIMIT),
        cost_estimate=pl.CostEstimate(
            flops=4 * count * width * weight.shape[1],
            transcendentals=0,
            bytes_accessed=2 * count * width,
        ),
        name="project",
    )(*pieces, *tokens, weight)


def gated_kernel(count, chunk, *refs):
    pieces, rest = refs[:count], refs[count:]
    pair_w, gate_ref, up_ref, hidden_ref, inv_ref, whole, sems = rest
    block = gate_ref.shape[1]

    @pl.when(pl.program_id(0) == 0)
    def _():
        for copy, span in fetch(pieces, whole, sems):
            copy.wait()
            inv_ref[span, :] = inverse_rms(whole[span, :])

    for at in range(0, whole.shape[0], chunk):
        span = slice(at, at + chunk)
        both = jnp.dot(whole[span, :], pair_w[...], preferred_element_type=jnp.float32)
        both = both * inv_ref[span, :]
        gate, up = both[:, :block], both[:, block:]
        gate_ref[span, :] = gate.astype(jnp.bfloat16)
        up_ref[span, :] = up.astype(jnp.bfloat16)
        hidden_ref[span, :] = (gate * lax.logistic(gate) * up).astype(jnp.bfloat16)


def gated(pieces, pair_w, block, chunk):
    tokens, width = rows_of(pieces), pieces[0].shape[1]
    units = pair_w.shape[1] // 2
    low = jax.ShapeDtypeStruct((tokens, units), jnp.bfloat16)
    out = pl.BlockSpec((tokens, block), lambda j: (0, j))
    return pl.pallas_call(
        functools.partial(gated_kernel, len(pieces), chunk),
        out_shape=[low, low, low, jax.ShapeDtypeStruct((tokens, 1), jnp.float32)],
        grid=(units // block,),
        in_specs=[ANYWHERE] * len(pieces)
        + [pl.BlockSpec((width, 2 * block), lambda j: (0, j))],
        out_specs=[out, out, out, pl.BlockSpec((tokens, 1), lambda j: (0, 0))],
        scratch_shapes=[
            pltpu.VMEM((tokens, width), jnp.bfloat16),
            pltpu.SemaphoreType.DMA((len(pieces),)),
        ],
        compiler_params=pltpu.CompilerParams(vmem_limit_bytes=VMEM_LIMIT),
        name="gated",
    )(*pieces, pair_w)


def gated_back_kernel(count, tokens, chunk, *refs):
    pieces, rest = refs[:count], refs[count + tokens :]
    down_w, gate_ref, up_ref, inv_ref, out_ref, whole, sems = rest
    block = gate_ref.shape[1]

    @pl.when(pl.program_id(0) == 0)
    def _():
        for copy, _ in fetch(pieces, whole, sems):
            copy.wait()

    for at in range(0, whole.shape[0], chunk):
        span = slice(at, at + chunk)
        d_hidden = jnp.dot(whole[span, :], down_w[...], preferred_element_type=jnp.float32)
        d_hidden = d_hidden * (RESIDUAL * inv_ref[span, :])
        gate = gate_ref[span, :].astype(jnp.float32)
        up = up_ref[span, :].astype(jnp.float32)
        sigma = lax.logistic(gate)
        out_ref[span, :block] = (d_hidden * up * sigma * (1.0 + gate * (1.0 - sigma))).astype(
            jnp.bfloat16
        )
        out_ref[span, block:] = (d_hidden * gate * sigma).astype(jnp.bfloat16)


def gated_back(pieces, down_w, gate, up, inv, block, chunk, others):
    tokens, width = rows_of(pieces), pieces[0].shape[1]
    units = down_w.shape[1]
    tall = pl.BlockSpec((tokens, block), lambda j: (0, j))
    return pl.pallas_call(
        functools.partial(gated_back_kernel, len(pieces), len(others), chunk),
        out_shape=jax.ShapeDtypeStruct((tokens, 2 * units), jnp.bfloat16),
        grid=(units // block,),
        in_specs=[ANYWHERE] * (len(pieces) + len(others))
        + [
            pl.BlockSpec((width, block), lambda j: (0, j)),
            tall,
            tall,
            pl.BlockSpec((tokens, 1), lambda j: (0, 0)),
        ],
        out_specs=pl.BlockSpec((tokens, 2 * block), lambda j: (0, j)),
        scratch_shapes=[
            pltpu.VMEM((tokens, width), jnp.bfloat16),
            pltpu.SemaphoreType.DMA((len(pieces),)),
        ],
        compiler_params=pltpu.CompilerParams(vmem_limit_bytes=VMEM_LIMIT),
        name="gated_back",
    )(*pieces, *others, down_w, gate, up, inv)


def outer_kernel(counts, tokens, block, *refs):
    sources, at = [], 0
    for count, rights in counts:
        sources.append((refs[at : at + count], refs[at + count : at + count + rights]))
        at += count + rights
    out_ref, scratch = refs[at + tokens], refs[at + tokens + 1 :]
    step = pl.program_id(0)

    @pl.when(step == 0)
    def _():
        copies = []
        for n, (pieces, _) in enumerate(sources):
            copies += fetch(pieces, scratch[2 * n], scratch[2 * n + 1])
        for copy, _ in copies:
            copy.wait()

    first = 0
    columns = pl.ds(pl.multiple_of(step * block, block), block)
    for n, (_, rights) in enumerate(sources):
        left = scratch[2 * n][:, columns]
        for right in rights:
            out_ref[:, first : first + right.shape[1]] = dot_tn(left, right[...]).astype(
                out_ref.dtype
            )
            first += right.shape[1]


def outer(sources, block, tokens=(), cost=None):
    operands, in_specs, scratch, counts, total = [], [], [], [], 0
    for pieces, rights in sources:
        count, width = rows_of(pieces), pieces[0].shape[1]
        operands += [*pieces, *rights]
        in_specs += [ANYWHERE] * len(pieces)
        in_specs += [pl.BlockSpec(right.shape, lambda j: (0, 0)) for right in rights]
        scratch += [
            pltpu.VMEM((count, width), jnp.bfloat16),
            pltpu.SemaphoreType.DMA((len(pieces),)),
        ]
        counts.append((len(pieces), len(rights)))
        total += sum(right.shape[1] for right in rights)
    return pl.pallas_call(
        functools.partial(outer_kernel, counts, len(tokens), block),
        out_shape=jax.ShapeDtypeStruct((width, total), jnp.bfloat16),
        grid=(width // block,),
        in_specs=in_specs + [ANYWHERE] * len(tokens),
        out_specs=pl.BlockSpec((block, total), lambda j: (j, 0)),
        scratch_shapes=scratch,
        compiler_params=pltpu.CompilerParams(vmem_limit_bytes=VMEM_LIMIT),
        cost_estimate=cost,
        name="outer",
    )(*operands, *tokens)


def add_low(one, other):
    return (one.astype(jnp.float32) + other.astype(jnp.float32)).astype(jnp.bfloat16)


def after_kernel(*refs):
    del refs


def after(value, *tokens):
    return pl.pallas_call(
        after_kernel,
        out_shape=jax.ShapeDtypeStruct(value.shape, value.dtype),
        in_specs=[ANYWHERE] * (1 + len(tokens)),
        out_specs=ANYWHERE,
        input_output_aliases={0: 0},
        name="after",
    )(value, *tokens)


def group_shards(
    group, cores,
    hidden_in, segments, gain_attn, query_weight, key_weight, value_weight, out_weight,
    gain_ffn, gate_weight, up_weight, down_weight, cotangent,
):
    bfloat = jnp.bfloat16
    seqs_here, rows_here, width = hidden_in.shape
    length = segments.shape[1]
    rows = rows_here // cores
    near = group // (length // rows_here)
    blocks = length // rows
    heads = HQ // KVH
    me = lax.axis_index(("near", "ctx")).astype(jnp.uint32)
    me_core = lax.axis_index("tp").astype(jnp.uint32)

    def swap(value, m):
        return lax.ppermute(value, ("near", "ctx"), [(i, i ^ m) for i in range(group)])

    def swap_core(value):
        return lax.ppermute(value, "tp", [(0, 1), (1, 0)])

    def gather(own, later=()):
        half = own.shape[0] // 2
        by_ctx, by_near = swap(own, 1), swap(own, 2)
        if later:
            by_ctx, by_near = after(by_ctx, *later), after(by_near, *later)
        opposite = [swap(by_ctx[:half], 2), swap(by_near[half:], 1)]
        same = [own, by_ctx, by_near, *opposite]
        return same + [swap_core(v) for v in same]

    def send_half(product):
        side = group * rows
        return swap_core(product(side, side, None, bfloat))

    def own_side(product, other):
        return product(0, group * rows, other, bfloat)

    def scatter(mine):
        half = rows // 2
        ctx_low, near_low, opposite = (mine[m * rows : (m + 1) * rows] for m in range(1, group))
        from_near, from_ctx = swap(opposite[:half], 2), swap(opposite[half:], 1)
        near_first, ctx_last = swap(near_low[:half], 2), swap(ctx_low[half:], 1)
        ctx_first = swap(add_low(ctx_low[:half], from_near), 1)
        near_last = swap(add_low(near_low[half:], from_ctx), 2)
        total = jnp.concatenate(
            [
                mine[:half].astype(jnp.float32)
                + ctx_first.astype(jnp.float32)
                + near_first.astype(jnp.float32),
                mine[half:rows].astype(jnp.float32)
                + ctx_last.astype(jnp.float32)
                + near_last.astype(jnp.float32),
            ]
        )
        return total

    def scatter_direct(mine):
        total = mine[:rows].astype(jnp.float32)
        for m in range(1, group):
            total = total + swap(mine[m * rows : (m + 1) * rows], m).astype(jnp.float32)
        return total

    def plain(left, weight):
        def product(first, size, add, dtype):
            out = matmul_trans(left[first : first + size], weight)
            return (out if add is None else out + add.astype(jnp.float32)).astype(dtype)

        return product

    def own_half(value):
        return cut(value, me_core, rows, 0)

    def both_halves(own):
        other = swap_core(own)
        whole = jnp.zeros((rows_here, own.shape[1]), own.dtype)
        whole = put(whole, own, me_core, 0)
        return put(whole, other, me_core ^ jnp.uint32(1), 0)

    def cut(value, index, size, axis):
        starts = [jnp.uint32(0)] * value.ndim
        starts[axis] = index * jnp.uint32(size)
        sizes = list(value.shape)
        sizes[axis] = size
        return lax.dynamic_slice(value, starts, sizes)

    def put(whole, piece, index, axis):
        starts = [jnp.uint32(0)] * whole.ndim
        starts[axis] = index * jnp.uint32(piece.shape[axis])
        return lax.dynamic_update_slice(whole, piece, starts)

    def to_columns(*weights, parts=1):
        whole = None
        for m in range(group):
            there = me ^ jnp.uint32(m)
            own = [cut(w, there, w.shape[1] // group, 1) for w in weights]
            sizes = [w.shape[1] // parts for w in own]
            piece = jnp.concatenate(
                [w[:, n * size : (n + 1) * size] for n in range(parts) for w, size in zip(own, sizes)],
                axis=1,
            )
            piece = swap(piece, m) if m else piece
            if whole is None:
                whole = jnp.zeros((group * piece.shape[0], piece.shape[1]), piece.dtype)
            whole = put(whole, piece, there, 0)
        return whole

    def to_rows(grad):
        deep = grad.shape[0] // group
        pieces = [cut(grad, me ^ jnp.uint32(m), deep, 0) for m in range(group)]
        return [swap(piece, m) if m else piece for m, piece in enumerate(pieces)]

    def unpack(pieces, widths, factors, parts=1):
        first, wholes, turn_width = 0, [], sum(widths) // parts
        for cols, factor in zip(widths, factors):
            size = cols // parts
            whole = jnp.zeros((pieces[0].shape[0], group * cols), jnp.float32)
            for m, piece in enumerate(pieces):
                part = jnp.concatenate(
                    [
                        piece[:, n * turn_width + first : n * turn_width + first + size]
                        for n in range(parts)
                    ],
                    axis=1,
                )
                part = part.astype(jnp.float32) * factor
                whole = put(whole, part, me ^ jnp.uint32(m), 1)
            first += size
            wholes.append(whole)
        return wholes

    def far_gather(weight):
        return lax.all_gather(weight, "far", axis=0, tiled=True)

    def far_scatter(grad):
        return lax.psum_scatter(grad.astype(bfloat), "far", scatter_dimension=0, tiled=True)

    deep = query_weight.shape[0]
    col_gain_a, col_gain_f = gain_attn[:, None], gain_ffn[:, None]

    def scaled(weight, gain):
        return (weight.astype(jnp.float32) * gain).astype(bfloat)

    attn_cols = to_columns(
        scaled(query_weight, col_gain_a),
        scaled(key_weight, col_gain_a),
        scaled(value_weight, col_gain_a),
        out_weight,
    )
    attn_w = far_gather(attn_cols)
    head_cols = heads * HD
    in_w, out_w = attn_w[:, : head_cols + 2 * HD], attn_w[:, head_cols + 2 * HD :]

    gain_later = after(col_gain_f, attn_cols)
    units = down_weight.shape[1] // group
    block = min(units, 256)
    pair_cols = to_columns(
        scaled(gate_weight, gain_later), scaled(up_weight, gain_later), parts=units // block
    )
    own_in = after(own_half(hidden_in.reshape(rows_here, width)), pair_cols)
    inputs = gather(own_in)
    pair_w = far_gather(pair_cols)
    own_cot = own_half(cotangent.reshape(rows_here, width))
    down_cols = to_columns(down_weight)
    down_w = far_gather(down_cols)

    seg_all = jnp.concatenate(
        [segments]
        + [swap(segments, n * (group // near)) for n in range(1, near)],
        axis=0,
    )
    start = jnp.sum((seg_all[:, None, :] < seg_all[:, :, None]).astype(jnp.int32), axis=2)
    places = (jnp.arange(length, dtype=jnp.int32)[None, :] - start).astype(jnp.float32)
    freqs = THETA ** (-jnp.arange(0, HD, 2, dtype=jnp.float32) / HD)
    phase = places.reshape(-1)[:, None] * freqs
    cosine, sine = jnp.cos(phase), jnp.sin(phase)
    cosine = jnp.concatenate([cosine, cosine, cosine, cosine], axis=1)
    sine = jnp.concatenate([-sine, sine, -sine, sine], axis=1)
    start = start.reshape(-1)[:, None]
    at = jnp.arange(near * blocks, dtype=jnp.int32)
    in_seq = at % blocks
    here_ctx = lax.axis_index("ctx")
    place = (
        ((in_seq % cores) ^ lax.axis_index("tp")) * group
        + (at // blocks) * (group // near)
        + ((in_seq // cores) ^ here_ctx)
    ).astype(jnp.int32)

    qkv, inv_a = project(inputs, in_w, True, None, jnp.float32)
    query, kv, mixed, lse = attend(
        place, qkv, cosine, sine, start, near, blocks, rows, heads, (down_cols,)
    )
    product = plain(mixed, out_w)
    branch_a = scatter(own_side(product, send_half(product)))
    own_f = own_in.astype(jnp.float32)
    middle = own_f + RESIDUAL * branch_a

    mids = gather(middle.astype(bfloat))
    gate_pre, upward, hidden, inv_f = gated(mids, pair_w, block, 512)
    cots = gather(after(own_cot, *mids[1 : len(mids) // 2]), (inv_f,))
    down_part = outer([(cots, [hidden])], 256)
    down_far = far_scatter(down_part)
    d_both = gated_back(cots, down_w, gate_pre, upward, inv_f, block, 512, (down_part,))
    product = plain(d_both, pair_w)
    other = send_half(product)
    pair_part = outer([(mids, [d_both])], 256, (other,))
    pair_far = far_scatter(pair_part)
    back_mine = own_side(product, after(other, pair_part, down_far))
    back_f = scatter(back_mine)
    product = plain(after(hidden, back_mine), down_w)
    branch_mine = own_side(product, send_half(product))

    def through_norm(grad, unit):
        return grad - unit * jnp.mean(grad * unit, axis=-1, keepdims=True)

    d_middle = own_cot.astype(jnp.float32) + through_norm(back_f, middle * inverse_rms(middle))

    d_mids = gather(after(d_middle.astype(bfloat), branch_mine))
    branch_f = scatter_direct(after(branch_mine, *d_mids[1 : len(d_mids) // 2]))
    middle_out = (middle + RESIDUAL * branch_f).astype(bfloat)
    (d_mixed,) = project(d_mids, out_w, False, RESIDUAL, bfloat)
    down_rows = to_rows(after(down_far, d_mixed))
    d_qkv = attend_back(
        place, query, kv, lse, d_mixed, inv_a, cosine, sine, start, near, blocks, rows, heads
    )
    attn_cols_all = d_qkv.shape[1] + head_cols
    attn_part = outer(
        [(inputs, [d_qkv]), (d_mids, [mixed])],
        256,
        (pair_far, middle_out, *down_rows),
        pl.CostEstimate(
            flops=4 * d_qkv.shape[0] * width * attn_cols_all,
            transcendentals=0,
            bytes_accessed=8 * d_qkv.shape[0] * width,
        ),
    )
    attn_far = far_scatter(attn_part)
    pair_rows = to_rows(pair_far)
    product = plain(after(d_qkv, attn_part, *pair_rows), in_w)
    back_mine = own_side(product, send_half(product))
    back_a = scatter(back_mine)
    layer_out = both_halves(middle_out)
    input_grad = d_middle + through_norm(back_a, own_f * inverse_rms(own_f))
    input_grad = both_halves(input_grad)

    one = jnp.ones_like(col_gain_a)
    (grad_down,) = unpack(
        [after(piece, back_mine) for piece in down_rows], [units], [RESIDUAL]
    )
    grad_gate, grad_up = unpack(
        [after(piece, back_mine) for piece in pair_rows], [units, units], [one, one], parts=units // block
    )
    grad_query, grad_key, grad_value, grad_out = unpack(
        to_rows(after(attn_far, back_a)),
        [head_cols, HD, HD, head_cols],
        [one, one, one, RESIDUAL],
    )

    def row_sum(*pairs):
        return sum(jnp.sum(weight.astype(jnp.float32) * grad, axis=1) for weight, grad in pairs)

    gain_grads = jnp.stack(
        [
            row_sum(
                (query_weight, grad_query), (key_weight, grad_key), (value_weight, grad_value)
            ),
            row_sum((gate_weight, grad_gate), (up_weight, grad_up)),
        ]
    )
    gain_grads = gain_grads + swap_core(gain_grads)
    return (
        layer_out.reshape(hidden_in.shape),
        input_grad.reshape(hidden_in.shape),
        gain_grads[0],
        grad_query * col_gain_a,
        grad_key * col_gain_a,
        grad_value * col_gain_a,
        grad_out,
        gain_grads[1],
        grad_gate * col_gain_f,
        grad_up * col_gain_f,
        grad_down,
    )


def solution(mesh):
    sizes = dict(mesh.shape)
    fsdp, ctx, tp = sizes["fsdp"], sizes["ctx"], sizes["tp"]
    near = KVH // (ctx * tp)
    group = near * ctx
    fits = (
        tuple(mesh.axis_names) == ("fsdp", "ctx", "tp")
        and tp == 2
        and near > 0
        and group * tp == KVH
        and fsdp % near == 0
        and near == ctx == 2
    )
    if fits:
        mesh = Mesh(
            mesh.devices.reshape(fsdp // near, near, ctx, tp), ("far", "near", "ctx", "tp")
        )
        body, data = functools.partial(group_shards, group, tp), ("far", "near")
    else:
        body, data = generic_shards, ("fsdp",)
    owner = (*data, "ctx")
    weight, gain, tokens = P(owner, "tp"), P(owner), P(data, "ctx", None)
    in_specs = (
        tokens,
        P(data, None),
        gain,
        weight,
        weight,
        weight,
        weight,
        gain,
        weight,
        weight,
        weight,
        tokens,
    )
    out_specs = (
        tokens,
        tokens,
        gain,
        weight,
        weight,
        weight,
        weight,
        gain,
        weight,
        weight,
        weight,
    )
    return jax.shard_map(body, mesh=mesh, in_specs=in_specs, out_specs=out_specs, check_vma=False)
```

```python
import functools

import jax
import jax.numpy as jnp
from jax import lax
from jax.experimental import pallas as pl
from jax.experimental.pallas import tpu as pltpu
from jax.sharding import Mesh
from jax.sharding import PartitionSpec as P

HQ = 32
KVH = 8
HD = 64


EPSILON = 1e-05
SCALE = 0.015625
RESIDUAL = 0.22
THETA = 10000000.0


def rotate_pairs(values, cosine, sine):
    half = values.shape[-1] // 2
    swapped = jnp.concatenate([-values[..., half:], values[..., :half]], axis=-1)
    return values * cosine + swapped * sine


def matmul_low(left, right):
    return jnp.dot(left, right, preferred_element_type=jnp.float32)


def matmul_trans(left, right):
    return lax.dot_general(
        left, right, (((1,), (1,)), ((), ())), preferred_element_type=jnp.float32
    )


def matmul_outer(left, right):
    return lax.dot_general(
        left, right, (((0,), (0,)), ((), ())), preferred_element_type=jnp.float32
    )


def norm_back(grad_normed, gain, unit_rows, inv_rms):
    scaled = grad_normed * gain
    return inv_rms * (scaled - unit_rows * jnp.mean(scaled * unit_rows, axis=-1, keepdims=True))


def reduce_low(grad):
    low = lax.psum_scatter(
        grad.astype(jnp.bfloat16), ("fsdp", "ctx"), scatter_dimension=0, tiled=True
    )
    return low.astype(jnp.float32)


def generic_shards(
    hidden_in,
    segments,
    gain_attn,
    query_weight,
    key_weight,
    value_weight,
    out_weight,
    gain_ffn,
    gate_weight,
    up_weight,
    down_weight,
    cotangent,
):
    seqs_here, rows_here, width = hidden_in.shape
    length = segments.shape[1]
    tokens = seqs_here * rows_here
    kv_local = key_weight.shape[1] // HD
    group_size = HQ // KVH
    head_cols = kv_local * group_size * HD
    bfloat = jnp.bfloat16
    first_row = lax.axis_index("ctx") * rows_here
    own_seg = lax.dynamic_slice_in_dim(segments, first_row, rows_here, 1)
    before = jnp.sum((segments[:, None, :] < own_seg[:, :, None]).astype(jnp.int32), axis=2)
    own_place = first_row + jnp.arange(rows_here, dtype=jnp.int32)
    places = (own_place[None, :] - before).astype(jnp.float32)
    freqs = THETA ** (-jnp.arange(0, HD, 2, dtype=jnp.float32) / HD)
    phase = places[:, :, None] * freqs
    phase = jnp.concatenate([phase, phase], axis=-1)
    cosine = jnp.cos(phase)
    sine = jnp.sin(phase)
    key_place = jnp.arange(length, dtype=jnp.int32)
    allowed = (own_seg[:, :, None] == segments[:, None, :]) & (
        key_place[None, None, :] <= own_place[None, :, None]
    )
    allowed = allowed[:, None, None, :, :]
    attn_full = (
        lax.all_gather(gain_attn.astype(jnp.bfloat16), ("fsdp", "ctx"), axis=0, tiled=True).astype(
            gain_attn.dtype
        ),
        lax.all_gather(query_weight, ("fsdp", "ctx"), axis=0, tiled=True),
        lax.all_gather(key_weight, ("fsdp", "ctx"), axis=0, tiled=True),
        lax.all_gather(value_weight, ("fsdp", "ctx"), axis=0, tiled=True),
        lax.all_gather(out_weight, ("fsdp", "ctx"), axis=0, tiled=True),
    )
    gain_a, query_full, key_full, value_full, out_full = attn_full
    inputs_f = hidden_in.reshape(tokens, width).astype(jnp.float32)
    inv_a = lax.rsqrt(jnp.mean(inputs_f * inputs_f, axis=-1, keepdims=True) + EPSILON)
    unit_a = inputs_f * inv_a
    normed_a = (unit_a * gain_a).astype(bfloat)
    query_raw = matmul_low(normed_a, query_full).reshape(
        seqs_here, rows_here, kv_local, group_size, HD
    )
    key_raw = matmul_low(normed_a, key_full).reshape(seqs_here, rows_here, kv_local, HD)
    value_low = (
        matmul_low(normed_a, value_full).astype(bfloat).reshape(seqs_here, rows_here, kv_local * HD)
    )
    query_rot = rotate_pairs(
        query_raw, cosine[:, :, None, None, :], sine[:, :, None, None, :]
    ).astype(bfloat)
    key_rot = rotate_pairs(key_raw, cosine[:, :, None, :], sine[:, :, None, :]).astype(bfloat)
    key_rot = key_rot.reshape(seqs_here, rows_here, kv_local * HD)
    key_all, value_all = (
        lax.all_gather(key_rot, "ctx", axis=1, tiled=True),
        lax.all_gather(value_low, "ctx", axis=1, tiled=True),
    )
    key_all = key_all.reshape(seqs_here, length, kv_local, HD)
    value_all = value_all.reshape(seqs_here, length, kv_local, HD)

    def masked_scores():
        scores = (
            jnp.einsum("srngd,slnd->sngrl", query_rot, key_all, preferred_element_type=jnp.float32)
            * SCALE
        )
        return jnp.where(allowed, scores, -1e30)

    scores = masked_scores()
    highest = jnp.max(scores, axis=-1, keepdims=True)
    raised = jnp.exp(scores - highest)
    totals = jnp.sum(raised, axis=-1, keepdims=True)
    log_total = highest + jnp.log(totals)
    probs_low = (raised / totals).astype(bfloat)
    mixed = jnp.einsum(
        "sngrl,slnd->srngd", probs_low, value_all, preferred_element_type=jnp.float32
    )
    mixed = mixed.astype(bfloat).reshape(tokens, head_cols)
    branch_a = lax.psum(matmul_trans(mixed, out_full).astype(jnp.bfloat16), "tp").astype(
        jnp.float32
    )
    middle = inputs_f + RESIDUAL * branch_a
    ffn_full = (
        lax.all_gather(gain_ffn.astype(jnp.bfloat16), ("fsdp", "ctx"), axis=0, tiled=True).astype(
            gain_ffn.dtype
        ),
        lax.all_gather(gate_weight, ("fsdp", "ctx"), axis=0, tiled=True),
        lax.all_gather(up_weight, ("fsdp", "ctx"), axis=0, tiled=True),
        lax.all_gather(down_weight, ("fsdp", "ctx"), axis=0, tiled=True),
    )
    gain_f, gate_full, up_full, down_full = ffn_full
    inv_f = lax.rsqrt(jnp.mean(middle * middle, axis=-1, keepdims=True) + EPSILON)
    unit_f = middle * inv_f
    normed_f = (unit_f * gain_f).astype(bfloat)
    gate_pre = matmul_low(normed_f, gate_full)
    upward = matmul_low(normed_f, up_full)
    sigma = jax.nn.sigmoid(gate_pre)
    active = gate_pre * sigma
    hidden = (active * upward).astype(bfloat)
    branch_f = lax.psum(matmul_trans(hidden, down_full).astype(jnp.bfloat16), "tp").astype(
        jnp.float32
    )
    layer_out = (middle + RESIDUAL * branch_f).astype(bfloat).reshape(seqs_here, rows_here, width)
    gain_fb, gate_back, up_back, down_back = (
        lax.all_gather(gain_ffn.astype(jnp.bfloat16), ("fsdp", "ctx"), axis=0, tiled=True).astype(
            gain_ffn.dtype
        ),
        lax.all_gather(gate_weight, ("fsdp", "ctx"), axis=0, tiled=True),
        lax.all_gather(up_weight, ("fsdp", "ctx"), axis=0, tiled=True),
        lax.all_gather(down_weight, ("fsdp", "ctx"), axis=0, tiled=True),
    )
    grad_y = cotangent.reshape(tokens, width).astype(jnp.float32)
    d_branch_f = (RESIDUAL * grad_y).astype(bfloat)
    grad_down = matmul_outer(d_branch_f, hidden)
    d_hidden = matmul_low(d_branch_f, down_back)
    d_gate = (d_hidden * upward * sigma * (1.0 + gate_pre * (1.0 - sigma))).astype(bfloat)
    d_up = (d_hidden * active).astype(bfloat)
    grad_gate = matmul_outer(normed_f, d_gate)
    grad_up = matmul_outer(normed_f, d_up)
    d_normed_f = lax.psum(
        (matmul_trans(d_gate, gate_back) + matmul_trans(d_up, up_back)).astype(jnp.bfloat16), "tp"
    ).astype(jnp.float32)
    grad_gain_ffn = jnp.sum(d_normed_f * unit_f, axis=0)
    d_middle = grad_y + norm_back(d_normed_f, gain_fb, unit_f, inv_f)
    ffn_grads = (
        lax.psum_scatter(grad_gain_ffn, ("fsdp", "ctx"), scatter_dimension=0, tiled=True),
        reduce_low(grad_gate),
        reduce_low(grad_up),
        reduce_low(grad_down),
    )
    gain_ab, query_back, key_back, value_back, out_back = (
        lax.all_gather(gain_attn.astype(jnp.bfloat16), ("fsdp", "ctx"), axis=0, tiled=True).astype(
            gain_attn.dtype
        ),
        lax.all_gather(query_weight, ("fsdp", "ctx"), axis=0, tiled=True),
        lax.all_gather(key_weight, ("fsdp", "ctx"), axis=0, tiled=True),
        lax.all_gather(value_weight, ("fsdp", "ctx"), axis=0, tiled=True),
        lax.all_gather(out_weight, ("fsdp", "ctx"), axis=0, tiled=True),
    )
    d_branch_a = (RESIDUAL * d_middle).astype(bfloat)
    grad_out = matmul_outer(d_branch_a, mixed)
    d_mixed = (
        matmul_low(d_branch_a, out_back)
        .astype(bfloat)
        .reshape(seqs_here, rows_here, kv_local, group_size, HD)
    )
    probs_again = jnp.exp(masked_scores() - log_total)
    probs_again_low = probs_again.astype(bfloat)
    d_probs = jnp.einsum(
        "srngd,slnd->sngrl", d_mixed, value_all, preferred_element_type=jnp.float32
    )
    inner = jnp.sum(probs_again * d_probs, axis=-1, keepdims=True)
    d_scores = (probs_again * (d_probs - inner)).astype(bfloat)
    d_query_rot = (
        jnp.einsum("sngrl,slnd->srngd", d_scores, key_all, preferred_element_type=jnp.float32)
        * SCALE
    )
    d_key_all = (
        jnp.einsum("sngrl,srngd->slnd", d_scores, query_rot, preferred_element_type=jnp.float32)
        * SCALE
    )
    d_value_all = jnp.einsum(
        "sngrl,srngd->slnd", probs_again_low, d_mixed, preferred_element_type=jnp.float32
    )
    d_key_own, d_value_own = (
        lax.psum_scatter(
            d_key_all.reshape(seqs_here, length, kv_local * HD).astype(jnp.bfloat16),
            "ctx",
            scatter_dimension=1,
            tiled=True,
        ).astype(jnp.float32),
        lax.psum_scatter(
            d_value_all.reshape(seqs_here, length, kv_local * HD).astype(jnp.bfloat16),
            "ctx",
            scatter_dimension=1,
            tiled=True,
        ).astype(jnp.float32),
    )
    d_query = (
        rotate_pairs(d_query_rot, cosine[:, :, None, None, :], -sine[:, :, None, None, :])
        .astype(bfloat)
        .reshape(tokens, head_cols)
    )
    d_key = rotate_pairs(
        d_key_own.reshape(seqs_here, rows_here, kv_local, HD),
        cosine[:, :, None, :],
        -sine[:, :, None, :],
    )
    d_key = d_key.astype(bfloat).reshape(tokens, kv_local * HD)
    d_value = d_value_own.reshape(tokens, kv_local * HD).astype(bfloat)
    grad_query = matmul_outer(normed_a, d_query)
    grad_key = matmul_outer(normed_a, d_key)
    grad_value = matmul_outer(normed_a, d_value)
    d_normed_part = (
        matmul_trans(d_query, query_back)
        + matmul_trans(d_key, key_back)
        + matmul_trans(d_value, value_back)
    )
    d_normed_a = lax.psum(d_normed_part.astype(jnp.bfloat16), "tp").astype(jnp.float32)
    grad_gain_attn = jnp.sum(d_normed_a * unit_a, axis=0)
    input_grad = (d_middle + norm_back(d_normed_a, gain_ab, unit_a, inv_a)).reshape(
        seqs_here, rows_here, width
    )
    attn_grads = (
        lax.psum_scatter(grad_gain_attn, ("fsdp", "ctx"), scatter_dimension=0, tiled=True),
        reduce_low(grad_query),
        reduce_low(grad_key),
        reduce_low(grad_value),
        reduce_low(grad_out),
    )
    return (
        layer_out,
        input_grad,
        attn_grads[0],
        attn_grads[1],
        attn_grads[2],
        attn_grads[3],
        attn_grads[4],
        ffn_grads[0],
        ffn_grads[1],
        ffn_grads[2],
        ffn_grads[3],
    )


MAX_DOC = 512
LANES = 128
NEG = -1e30


def half_lanes(rows):
    lane = lax.broadcasted_iota(jnp.int32, (rows, LANES), 1)
    return lane % HD < HD // 2, lane < HD


def turn(slab, cosine, sine_signed):
    first, _ = half_lanes(slab.shape[0])
    swapped = jnp.where(
        first,
        pltpu.roll(slab, LANES - HD // 2, 1),
        pltpu.roll(slab, HD // 2, 1),
    )
    return slab * cosine + swapped * sine_signed


def dot_nt(left, right):
    return lax.dot_general(left, right, (((1,), (1,)), ((), ())), preferred_element_type=jnp.float32)


def dot_tn(left, right):
    return lax.dot_general(left, right, (((0,), (0,)), ((), ())), preferred_element_type=jnp.float32)


def window_mask(start, first_query, first_key, rows, keys):
    query = first_query + lax.broadcasted_iota(jnp.int32, (rows, keys), 0)
    key = first_key + lax.broadcasted_iota(jnp.int32, (rows, keys), 1)
    return (key <= query) & (key >= start)


def each_window(step, rows, window, body):
    last = window // rows - 1
    for early in range(last):
        pl.when(step == early)(functools.partial(body, (early + 1) * rows, 0))
    first = pl.multiple_of(jnp.maximum(step - last, 0) * rows, rows)
    pl.when(step >= last)(functools.partial(body, window, first))


def attend_kernel(
    rows, window, heads, place_ref, qkv_ref, cos_ref, sin_ref, start_ref, *rest,
):
    query_ref, kv_ref, mixed_ref, lse_ref, keys, values = rest[-6:]
    step = pl.program_id(1)
    _, low_half = half_lanes(rows)
    cosine, sine = cos_ref[...], sin_ref[...]

    @pl.when(step == 0)
    def _():
        keys[...] = jnp.zeros_like(keys)
        values[...] = jnp.zeros_like(values)

    width = heads * HD
    raw = qkv_ref[:, width:]
    kv = jnp.where(low_half, turn(raw, cosine, sine), raw)
    kv_ref[...] = kv.astype(jnp.bfloat16)
    moved = pltpu.roll(kv, HD, 1)
    own = pl.ds(pl.multiple_of(step * rows, rows), rows)
    keys[own, :] = jnp.where(low_half, kv, moved).astype(jnp.bfloat16)
    values[own, :] = jnp.where(low_half, moved, kv).astype(jnp.bfloat16)

    def windowed(count, first_key):
        keys_w = keys[pl.ds(first_key, count), :]
        values_w = values[pl.ds(first_key, count), :]
        allowed = window_mask(start_ref[...], step * rows, first_key, rows, count)
        for slab in range(width // LANES):
            at = slice(slab * LANES, (slab + 1) * LANES)
            rot = turn(qkv_ref[:, at], cosine, sine).astype(jnp.bfloat16)
            query_ref[:, at] = rot
            both = []
            for part in range(2):
                mine = low_half if part == 0 else jnp.logical_not(low_half)
                one = jnp.where(mine, rot, jnp.zeros_like(rot))
                scores = jnp.where(allowed, dot_nt(one, keys_w) * SCALE, NEG)
                highest = jnp.max(scores, axis=1, keepdims=True)
                raised = jnp.exp(scores - highest)
                total = jnp.sum(raised, axis=1, keepdims=True)
                mixed = jnp.dot(
                    raised.astype(jnp.bfloat16), values_w, preferred_element_type=jnp.float32
                )
                both.append(mixed / total)
                head = slab * 2 + part
                lse_ref[:, head : head + 1] = highest + jnp.log(total)
            mixed_ref[:, at] = jnp.where(low_half, both[0], both[1]).astype(jnp.bfloat16)

    each_window(step, rows, window, windowed)


def attend_back_kernel(
    rows, window, heads, blocks, place_ref, query_ref, kv_ref, lse_ref, grad_ref, inv_ref, cos_ref, sin_ref, start_ref,
    out_ref, keys, values, d_keys, d_values,
):
    seq = pl.program_id(0)
    step = blocks - 1 - pl.program_id(1)
    _, low_half = half_lanes(rows)
    inv = inv_ref[...]
    cosine, sine = cos_ref[...], sin_ref[...]

    @pl.when(step == blocks - 1)
    def _():
        for block in range(blocks):
            source = pl.multiple_of(place_ref[seq * blocks + block] * rows, rows)
            kv = kv_ref[pl.ds(source, rows), :].astype(jnp.float32)
            moved = pltpu.roll(kv, HD, 1)
            at = slice(block * rows, (block + 1) * rows)
            keys[at, :] = jnp.where(low_half, kv, moved).astype(jnp.bfloat16)
            values[at, :] = jnp.where(low_half, moved, kv).astype(jnp.bfloat16)
        d_keys[...] = jnp.zeros_like(d_keys)
        d_values[...] = jnp.zeros_like(d_values)

    width = heads * HD

    def windowed(count, first_key):
        span = pl.ds(first_key, count)
        keys_w = keys[span, :]
        values_w = values[span, :]
        allowed = window_mask(start_ref[...], step * rows, first_key, rows, count)
        d_keys_w = jnp.zeros((count, LANES), jnp.float32)
        d_values_w = jnp.zeros((count, LANES), jnp.float32)
        for slab in range(width // LANES):
            at = slice(slab * LANES, (slab + 1) * LANES)
            query, grad = query_ref[:, at], grad_ref[:, at]
            both = []
            for part in range(2):
                mine = low_half if part == 0 else jnp.logical_not(low_half)
                head = slab * 2 + part
                one = jnp.where(mine, query, jnp.zeros_like(query))
                one_grad = jnp.where(mine, grad, jnp.zeros_like(grad))
                scores = dot_nt(one, keys_w) * SCALE - lse_ref[:, head : head + 1]
                probs = jnp.exp(jnp.where(allowed, scores, NEG))
                d_probs = dot_nt(one_grad, values_w)
                inner = jnp.sum(probs * d_probs, axis=1, keepdims=True)
                d_scores = (probs * (d_probs - inner)).astype(jnp.bfloat16)
                both.append(jnp.dot(d_scores, keys_w, preferred_element_type=jnp.float32))
                d_keys_w = d_keys_w + dot_tn(d_scores, one)
                d_values_w = d_values_w + dot_tn(probs.astype(jnp.bfloat16), one_grad)
            d_query = jnp.where(low_half, both[0], both[1]) * SCALE
            out_ref[:, at] = (turn(d_query, cosine, -sine) * inv).astype(jnp.bfloat16)
        d_keys[span, :] += d_keys_w
        d_values[span, :] += d_values_w

    each_window(step, rows, window, windowed)
    own = pl.ds(pl.multiple_of(step * rows, rows), rows)
    d_key = d_keys[own, :] * SCALE
    d_key = turn(d_key + pltpu.roll(d_key, HD, 1), cosine, -sine)
    d_value = d_values[own, :]
    d_value = d_value + pltpu.roll(d_value, HD, 1)
    out_ref[:, width:] = (jnp.where(low_half, d_key, d_value) * inv).astype(jnp.bfloat16)


def attend(place, qkv, cosine, sine, start, seqs, blocks, rows, heads, others):
    tokens = qkv.shape[0]
    width = heads * HD
    window = min(blocks * rows, rows + -(-MAX_DOC // rows) * rows)

    def placed(cols):
        return pl.BlockSpec((rows, cols), lambda s, i, place: (place[s * blocks + i], 0))

    def natural(cols):
        return pl.BlockSpec((rows, cols), lambda s, i, place: (s * blocks + i, 0))

    return pl.pallas_call(
        functools.partial(attend_kernel, rows, window, heads),
        out_shape=(
            jax.ShapeDtypeStruct((tokens, width), jnp.bfloat16),
            jax.ShapeDtypeStruct((tokens, LANES), jnp.bfloat16),
            jax.ShapeDtypeStruct((tokens, width), jnp.bfloat16),
            jax.ShapeDtypeStruct((tokens, heads), jnp.float32),
        ),
        grid_spec=pltpu.PrefetchScalarGridSpec(
            num_scalar_prefetch=1,
            grid=(seqs, blocks),
            in_specs=[placed(width + LANES), natural(LANES), natural(LANES), natural(1)]
            + [ANYWHERE] * len(others),
            out_specs=[placed(width), placed(LANES), placed(width), placed(heads)],
            scratch_shapes=[pltpu.VMEM((blocks * rows, LANES), jnp.bfloat16)] * 2,
        ),
        compiler_params=pltpu.CompilerParams(vmem_limit_bytes=48 << 20),
        name="attend",
    )(place, qkv, cosine, sine, start, *others)


def attend_back(place, query, kv, lse, grad, inv, cosine, sine, start, seqs, blocks, rows, heads):
    tokens = query.shape[0]
    width = heads * HD
    window = min(blocks * rows, rows + -(-MAX_DOC // rows) * rows)

    def placed(cols):
        return pl.BlockSpec(
            (rows, cols), lambda s, i, place: (place[s * blocks + blocks - 1 - i], 0)
        )

    def natural(cols):
        return pl.BlockSpec((rows, cols), lambda s, i, place: (s * blocks + blocks - 1 - i, 0))

    return pl.pallas_call(
        functools.partial(attend_back_kernel, rows, window, heads, blocks),
        out_shape=jax.ShapeDtypeStruct((tokens, width + LANES), jnp.bfloat16),
        grid_spec=pltpu.PrefetchScalarGridSpec(
            num_scalar_prefetch=1,
            grid=(seqs, blocks),
            in_specs=[
                placed(width),
                pl.BlockSpec((tokens, LANES), lambda s, i, place: (0, 0)),
                placed(heads),
                placed(width),
                placed(1),
                natural(LANES),
                natural(LANES),
                natural(1),
            ],
            out_specs=placed(width + LANES),
            scratch_shapes=[pltpu.VMEM((blocks * rows, LANES), jnp.bfloat16)] * 2
            + [pltpu.VMEM((blocks * rows, LANES), jnp.float32)] * 2,
        ),
        compiler_params=pltpu.CompilerParams(vmem_limit_bytes=48 << 20),
        cost_estimate=pl.CostEstimate(
            flops=48 * tokens * window * heads * LANES,
            transcendentals=tokens * window * heads,
            bytes_accessed=tokens * (8 * width + 12 * LANES),
        ),
        name="attend_back",
    )(place, query, kv, lse, grad, inv, cosine, sine, start)


VMEM_LIMIT = 56 << 20
ANYWHERE = pl.BlockSpec(memory_space=pl.ANY)


def fetch(pieces, whole, sems):
    copies, at = [], 0
    for n, piece in enumerate(pieces):
        span = slice(at, at + piece.shape[0])
        copy = pltpu.make_async_copy(piece, whole.at[span, :], sems.at[n])
        copy.start()
        copies.append((copy, span))
        at += piece.shape[0]
    return copies


def inverse_rms(values):
    values = values.astype(jnp.float32)
    return lax.rsqrt(jnp.mean(values * values, axis=-1, keepdims=True) + EPSILON)


def rows_of(pieces):
    return sum(piece.shape[0] for piece in pieces)


def project_kernel(count, tokens, normed, factor, *refs):
    pieces, rest = refs[:count], refs[count + tokens :]
    weight_ref, out_ref = rest[:2]
    whole, sems = rest[-2:]
    for copy, span in fetch(pieces, whole, sems):
        copy.wait()
        values = whole[span, :]
        product = jnp.dot(values, weight_ref[...], preferred_element_type=jnp.float32)
        if normed:
            inv = inverse_rms(values)
            rest[2][span, :] = inv
            product = product * inv
        else:
            product = product * factor
        out_ref[span, :] = product.astype(out_ref.dtype)


def project(pieces, weight, normed, factor, dtype, tokens=()):
    count, width = rows_of(pieces), pieces[0].shape[1]
    out_shape = [jax.ShapeDtypeStruct((count, weight.shape[1]), dtype)]
    if normed:
        out_shape.append(jax.ShapeDtypeStruct((count, 1), jnp.float32))
    vmem = pl.BlockSpec(memory_space=pltpu.VMEM)
    return pl.pallas_call(
        functools.partial(project_kernel, len(pieces), len(tokens), normed, factor),
        out_shape=out_shape,
        in_specs=[ANYWHERE] * (len(pieces) + len(tokens)) + [vmem],
        out_specs=[vmem] * len(out_shape),
        scratch_shapes=[
            pltpu.VMEM((count, width), jnp.bfloat16),
            pltpu.SemaphoreType.DMA((len(pieces),)),
        ],
        compiler_params=pltpu.CompilerParams(vmem_limit_bytes=VMEM_LIMIT),
        cost_estimate=pl.CostEstimate(
            flops=4 * count * width * weight.shape[1],
            transcendentals=0,
            bytes_accessed=2 * count * width,
        ),
        name="project",
    )(*pieces, *tokens, weight)


def gated_kernel(count, chunk, *refs):
    pieces, rest = refs[:count], refs[count:]
    pair_w, gate_ref, up_ref, hidden_ref, inv_ref, whole, sems = rest
    block = gate_ref.shape[1]

    @pl.when(pl.program_id(0) == 0)
    def _():
        for copy, span in fetch(pieces, whole, sems):
            copy.wait()
            inv_ref[span, :] = inverse_rms(whole[span, :])

    for at in range(0, whole.shape[0], chunk):
        span = slice(at, at + chunk)
        both = jnp.dot(whole[span, :], pair_w[...], preferred_element_type=jnp.float32)
        both = both * inv_ref[span, :]
        gate, up = both[:, :block], both[:, block:]
        gate_ref[span, :] = gate.astype(jnp.bfloat16)
        up_ref[span, :] = up.astype(jnp.bfloat16)
        hidden_ref[span, :] = (gate * lax.logistic(gate) * up).astype(jnp.bfloat16)


def gated(pieces, pair_w, block, chunk):
    tokens, width = rows_of(pieces), pieces[0].shape[1]
    units = pair_w.shape[1] // 2
    low = jax.ShapeDtypeStruct((tokens, units), jnp.bfloat16)
    out = pl.BlockSpec((tokens, block), lambda j: (0, j))
    return pl.pallas_call(
        functools.partial(gated_kernel, len(pieces), chunk),
        out_shape=[low, low, low, jax.ShapeDtypeStruct((tokens, 1), jnp.float32)],
        grid=(units // block,),
        in_specs=[ANYWHERE] * len(pieces)
        + [pl.BlockSpec((width, 2 * block), lambda j: (0, j))],
        out_specs=[out, out, out, pl.BlockSpec((tokens, 1), lambda j: (0, 0))],
        scratch_shapes=[
            pltpu.VMEM((tokens, width), jnp.bfloat16),
            pltpu.SemaphoreType.DMA((len(pieces),)),
        ],
        compiler_params=pltpu.CompilerParams(vmem_limit_bytes=VMEM_LIMIT),
        name="gated",
    )(*pieces, pair_w)


def gated_back_kernel(count, tokens, chunk, *refs):
    pieces, rest = refs[:count], refs[count + tokens :]
    down_w, gate_ref, up_ref, inv_ref, out_ref, whole, sems = rest
    block = gate_ref.shape[1]

    @pl.when(pl.program_id(0) == 0)
    def _():
        for copy, _ in fetch(pieces, whole, sems):
            copy.wait()

    for at in range(0, whole.shape[0], chunk):
        span = slice(at, at + chunk)
        d_hidden = jnp.dot(whole[span, :], down_w[...], preferred_element_type=jnp.float32)
        d_hidden = d_hidden * (RESIDUAL * inv_ref[span, :])
        gate = gate_ref[span, :].astype(jnp.float32)
        up = up_ref[span, :].astype(jnp.float32)
        sigma = lax.logistic(gate)
        out_ref[span, :block] = (d_hidden * up * sigma * (1.0 + gate * (1.0 - sigma))).astype(
            jnp.bfloat16
        )
        out_ref[span, block:] = (d_hidden * gate * sigma).astype(jnp.bfloat16)


def gated_back(pieces, down_w, gate, up, inv, block, chunk, others):
    tokens, width = rows_of(pieces), pieces[0].shape[1]
    units = down_w.shape[1]
    tall = pl.BlockSpec((tokens, block), lambda j: (0, j))
    return pl.pallas_call(
        functools.partial(gated_back_kernel, len(pieces), len(others), chunk),
        out_shape=jax.ShapeDtypeStruct((tokens, 2 * units), jnp.bfloat16),
        grid=(units // block,),
        in_specs=[ANYWHERE] * (len(pieces) + len(others))
        + [
            pl.BlockSpec((width, block), lambda j: (0, j)),
            tall,
            tall,
            pl.BlockSpec((tokens, 1), lambda j: (0, 0)),
        ],
        out_specs=pl.BlockSpec((tokens, 2 * block), lambda j: (0, j)),
        scratch_shapes=[
            pltpu.VMEM((tokens, width), jnp.bfloat16),
            pltpu.SemaphoreType.DMA((len(pieces),)),
        ],
        compiler_params=pltpu.CompilerParams(vmem_limit_bytes=VMEM_LIMIT),
        name="gated_back",
    )(*pieces, *others, down_w, gate, up, inv)


def outer_kernel(counts, tokens, block, *refs):
    sources, at = [], 0
    for count, rights in counts:
        sources.append((refs[at : at + count], refs[at + count : at + count + rights]))
        at += count + rights
    out_ref, scratch = refs[at + tokens], refs[at + tokens + 1 :]
    step = pl.program_id(0)

    @pl.when(step == 0)
    def _():
        copies = []
        for n, (pieces, _) in enumerate(sources):
            copies += fetch(pieces, scratch[2 * n], scratch[2 * n + 1])
        for copy, _ in copies:
            copy.wait()

    first = 0
    columns = pl.ds(pl.multiple_of(step * block, block), block)
    for n, (_, rights) in enumerate(sources):
        left = scratch[2 * n][:, columns]
        for right in rights:
            out_ref[:, first : first + right.shape[1]] = dot_tn(left, right[...]).astype(
                out_ref.dtype
            )
            first += right.shape[1]


def outer(sources, block, tokens=(), cost=None):
    operands, in_specs, scratch, counts, total = [], [], [], [], 0
    for pieces, rights in sources:
        count, width = rows_of(pieces), pieces[0].shape[1]
        operands += [*pieces, *rights]
        in_specs += [ANYWHERE] * len(pieces)
        in_specs += [pl.BlockSpec(right.shape, lambda j: (0, 0)) for right in rights]
        scratch += [
            pltpu.VMEM((count, width), jnp.bfloat16),
            pltpu.SemaphoreType.DMA((len(pieces),)),
        ]
        counts.append((len(pieces), len(rights)))
        total += sum(right.shape[1] for right in rights)
    return pl.pallas_call(
        functools.partial(outer_kernel, counts, len(tokens), block),
        out_shape=jax.ShapeDtypeStruct((width, total), jnp.bfloat16),
        grid=(width // block,),
        in_specs=in_specs + [ANYWHERE] * len(tokens),
        out_specs=pl.BlockSpec((block, total), lambda j: (j, 0)),
        scratch_shapes=scratch,
        compiler_params=pltpu.CompilerParams(vmem_limit_bytes=VMEM_LIMIT),
        cost_estimate=cost,
        name="outer",
    )(*operands, *tokens)


def rows_kernel(added, left_ref, weight_ref, *rest):
    product = dot_nt(left_ref[...], weight_ref[...])
    if added:
        product = product + rest[0][...].astype(jnp.float32)
    rest[-1][...] = product.astype(rest[-1].dtype)


def rows_product(left, weight, first, size, add, block):
    width, depth = weight.shape
    out = pl.BlockSpec((size, block), lambda j: (0, j))
    extra = [] if add is None else [add]
    return pl.pallas_call(
        functools.partial(rows_kernel, len(extra)),
        out_shape=jax.ShapeDtypeStruct((size, width), jnp.bfloat16),
        grid=(width // block,),
        in_specs=[
            pl.BlockSpec((size, depth), lambda j: (first // size, 0)),
            pl.BlockSpec((block, depth), lambda j: (j, 0)),
        ]
        + [out] * len(extra),
        out_specs=out,
        compiler_params=pltpu.CompilerParams(vmem_limit_bytes=VMEM_LIMIT),
        name="rows_product",
    )(left, weight, *extra)


def fold_kernel(tokens, mine, from_near, from_ctx, *rest):
    to_ctx, to_near = rest[tokens:]
    rows, half = mine.shape[0] // 4, mine.shape[0] // 8
    ctx_first, near_last = slice(rows, rows + half), slice(2 * rows + half, 3 * rows)
    to_ctx[...] = (
        mine[ctx_first, :].astype(jnp.float32) + from_near[...].astype(jnp.float32)
    ).astype(jnp.bfloat16)
    to_near[...] = (
        mine[near_last, :].astype(jnp.float32) + from_ctx[...].astype(jnp.float32)
    ).astype(jnp.bfloat16)


def fold(mine, from_near, from_ctx, tokens):
    half = jax.ShapeDtypeStruct(from_near.shape, jnp.bfloat16)
    vmem = pl.BlockSpec(memory_space=pltpu.VMEM)
    return pl.pallas_call(
        functools.partial(fold_kernel, len(tokens)),
        out_shape=[half, half],
        in_specs=[vmem] * 3 + [ANYWHERE] * len(tokens),
        out_specs=[vmem] * 2,
        compiler_params=pltpu.CompilerParams(vmem_limit_bytes=VMEM_LIMIT),
        name="fold",
    )(mine, from_near, from_ctx, *tokens)


def after_kernel(*refs):
    del refs


def after(value, *tokens):
    return pl.pallas_call(
        after_kernel,
        out_shape=jax.ShapeDtypeStruct(value.shape, value.dtype),
        in_specs=[ANYWHERE] * (1 + len(tokens)),
        out_specs=ANYWHERE,
        input_output_aliases={0: 0},
        name="after",
    )(value, *tokens)


def group_shards(
    group, cores,
    hidden_in, segments, gain_attn, query_weight, key_weight, value_weight, out_weight,
    gain_ffn, gate_weight, up_weight, down_weight, cotangent,
):
    bfloat = jnp.bfloat16
    seqs_here, rows_here, width = hidden_in.shape
    length = segments.shape[1]
    rows = rows_here // cores
    near = group // (length // rows_here)
    blocks = length // rows
    heads = HQ // KVH
    me = lax.axis_index(("near", "ctx")).astype(jnp.uint32)
    me_core = lax.axis_index("tp").astype(jnp.uint32)

    def swap(value, m):
        return lax.ppermute(value, ("near", "ctx"), [(i, i ^ m) for i in range(group)])

    def swap_core(value):
        return lax.ppermute(value, "tp", [(0, 1), (1, 0)])

    def gather(own, later=()):
        half = own.shape[0] // 2
        by_ctx, by_near = swap(own, 1), swap(own, 2)
        if later:
            by_ctx, by_near = after(by_ctx, *later), after(by_near, *later)
        opposite = [swap(by_ctx[:half], 2), swap(by_near[half:], 1)]
        same = [own, by_ctx, by_near, *opposite]
        return same + [swap_core(v) for v in same]

    def other_side(product):
        return product(group * rows, group * rows, None)

    def own_side(product, other):
        return product(0, group * rows, other)

    def scatter(mine, *tokens):
        half = rows // 2
        ctx_low, near_low, opposite = (mine[m * rows : (m + 1) * rows] for m in range(1, group))
        from_near, from_ctx = swap(opposite[:half], 2), swap(opposite[half:], 1)
        near_first, ctx_last = swap(near_low[:half], 2), swap(ctx_low[half:], 1)
        to_ctx, to_near = fold(mine, from_near, from_ctx, tokens)
        ctx_first, near_last = swap(to_ctx, 1), swap(to_near, 2)
        total = jnp.concatenate(
            [
                mine[:half].astype(jnp.float32)
                + ctx_first.astype(jnp.float32)
                + near_first.astype(jnp.float32),
                mine[half:rows].astype(jnp.float32)
                + ctx_last.astype(jnp.float32)
                + near_last.astype(jnp.float32),
            ]
        )
        return total, to_ctx

    def scatter_direct(mine):
        total = mine[:rows].astype(jnp.float32)
        for m in range(1, group):
            total = total + swap(mine[m * rows : (m + 1) * rows], m).astype(jnp.float32)
        return total

    def plain(left, weight):
        return lambda first, size, add: rows_product(left, weight, first, size, add, 512)

    def narrow(left, weight):
        def product(first, size, add):
            out = matmul_trans(left[first : first + size], weight)
            return (out if add is None else out + add.astype(jnp.float32)).astype(bfloat)

        return product

    def own_half(value):
        return cut(value, me_core, rows, 0)

    def both_halves(own):
        other = swap_core(own)
        whole = jnp.zeros((rows_here, own.shape[1]), own.dtype)
        whole = put(whole, own, me_core, 0)
        return put(whole, other, me_core ^ jnp.uint32(1), 0)

    def cut(value, index, size, axis):
        starts = [jnp.uint32(0)] * value.ndim
        starts[axis] = index * jnp.uint32(size)
        sizes = list(value.shape)
        sizes[axis] = size
        return lax.dynamic_slice(value, starts, sizes)

    def put(whole, piece, index, axis):
        starts = [jnp.uint32(0)] * whole.ndim
        starts[axis] = index * jnp.uint32(piece.shape[axis])
        return lax.dynamic_update_slice(whole, piece, starts)

    def to_columns(*weights, parts=1):
        whole = None
        for m in range(group):
            there = me ^ jnp.uint32(m)
            own = [cut(w, there, w.shape[1] // group, 1) for w in weights]
            sizes = [w.shape[1] // parts for w in own]
            piece = jnp.concatenate(
                [w[:, n * size : (n + 1) * size] for n in range(parts) for w, size in zip(own, sizes)],
                axis=1,
            )
            piece = swap(piece, m) if m else piece
            if whole is None:
                whole = jnp.zeros((group * piece.shape[0], piece.shape[1]), piece.dtype)
            whole = put(whole, piece, there, 0)
        return whole

    def to_rows(grad):
        deep = grad.shape[0] // group
        pieces = [cut(grad, me ^ jnp.uint32(m), deep, 0) for m in range(group)]
        return [swap(piece, m) if m else piece for m, piece in enumerate(pieces)]

    def unpack(pieces, widths, factors, parts=1):
        first, wholes, turn_width = 0, [], sum(widths) // parts
        for cols, factor in zip(widths, factors):
            size = cols // parts
            whole = jnp.zeros((pieces[0].shape[0], group * cols), jnp.float32)
            for m, piece in enumerate(pieces):
                part = jnp.concatenate(
                    [
                        piece[:, n * turn_width + first : n * turn_width + first + size]
                        for n in range(parts)
                    ],
                    axis=1,
                )
                part = part.astype(jnp.float32) * factor
                whole = put(whole, part, me ^ jnp.uint32(m), 1)
            first += size
            wholes.append(whole)
        return wholes

    def far_gather(weight):
        return lax.all_gather(weight, "far", axis=0, tiled=True)

    def far_scatter(grad):
        return lax.psum_scatter(grad.astype(bfloat), "far", scatter_dimension=0, tiled=True)

    deep = query_weight.shape[0]
    col_gain_a, col_gain_f = gain_attn[:, None], gain_ffn[:, None]

    def scaled(weight, gain):
        return (weight.astype(jnp.float32) * gain).astype(bfloat)

    attn_cols = to_columns(
        scaled(query_weight, col_gain_a),
        scaled(key_weight, col_gain_a),
        scaled(value_weight, col_gain_a),
        out_weight,
    )
    attn_w = far_gather(attn_cols)
    head_cols = heads * HD
    in_w, out_w = attn_w[:, : head_cols + 2 * HD], attn_w[:, head_cols + 2 * HD :]

    gain_later = after(col_gain_f, attn_cols)
    units = down_weight.shape[1] // group
    block = min(units, 256)
    pair_cols = to_columns(
        scaled(gate_weight, gain_later), scaled(up_weight, gain_later), parts=units // block
    )
    seg_others = [swap(segments, n * (group // near)) for n in range(1, near)]
    own_in = after(own_half(hidden_in.reshape(rows_here, width)), pair_cols, *seg_others)
    inputs = gather(own_in)
    pair_w = far_gather(pair_cols)
    own_cot = own_half(cotangent.reshape(rows_here, width))

    seg_all = jnp.concatenate(
        [segments] + seg_others,
        axis=0,
    )
    start = jnp.sum((seg_all[:, None, :] < seg_all[:, :, None]).astype(jnp.int32), axis=2)
    places = (jnp.arange(length, dtype=jnp.int32)[None, :] - start).astype(jnp.float32)
    freqs = THETA ** (-jnp.arange(0, HD, 2, dtype=jnp.float32) / HD)
    phase = places.reshape(-1)[:, None] * freqs
    cosine, sine = jnp.cos(phase), jnp.sin(phase)
    cosine = jnp.concatenate([cosine, cosine, cosine, cosine], axis=1)
    sine = jnp.concatenate([-sine, sine, -sine, sine], axis=1)
    start = start.reshape(-1)[:, None]
    at = jnp.arange(near * blocks, dtype=jnp.int32)
    in_seq = at % blocks
    here_ctx = lax.axis_index("ctx")
    place = (
        ((in_seq % cores) ^ lax.axis_index("tp")) * group
        + (at // blocks) * (group // near)
        + ((in_seq // cores) ^ here_ctx)
    ).astype(jnp.int32)

    qkv, inv_a = project(inputs, in_w, True, None, jnp.float32)
    down_cols = to_columns(after(down_weight, inv_a))
    down_w = far_gather(down_cols)
    query, kv, mixed, lse = attend(
        place, qkv, cosine, sine, start, near, blocks, rows, heads, ()
    )
    product = narrow(after(mixed, down_cols), out_w)
    branch_a, _ = scatter(own_side(product, swap_core(other_side(product))))
    own_f = own_in.astype(jnp.float32)
    middle = own_f + RESIDUAL * branch_a

    mids = gather(middle.astype(bfloat))
    gate_pre, upward, hidden, inv_f = gated(mids, pair_w, block, 512)
    cots = gather(after(own_cot, *mids[1 : len(mids) // 2]), (inv_f,))
    down_part = outer([(cots, [hidden])], 256)
    down_far = far_scatter(down_part)
    d_both = gated_back(cots, down_w, gate_pre, upward, inv_f, block, 512, (down_part,))
    product = plain(d_both, pair_w)
    other = other_side(product)
    pair_part = outer([(mids, [d_both])], 256, (other,))
    pair_far = far_scatter(pair_part)
    back_mine = own_side(product, after(swap_core(other), pair_part))
    product = plain(after(hidden, back_mine), down_w)
    other = other_side(product)
    back_f, _ = scatter(back_mine, other, down_far)
    branch_mine = own_side(product, swap_core(other))

    def through_norm(grad, unit):
        return grad - unit * jnp.mean(grad * unit, axis=-1, keepdims=True)

    d_middle = own_cot.astype(jnp.float32) + through_norm(back_f, middle * inverse_rms(middle))

    d_mids = gather(after(d_middle.astype(bfloat), branch_mine))
    branch_f = scatter_direct(after(branch_mine, *d_mids[1 : len(d_mids) // 2]))
    middle_out = (middle + RESIDUAL * branch_f).astype(bfloat)
    (d_mixed,) = project(d_mids, out_w, False, RESIDUAL, bfloat)
    down_rows = to_rows(after(down_far, d_mixed))
    d_qkv = attend_back(
        place, query, kv, lse, d_mixed, inv_a, cosine, sine, start, near, blocks, rows, heads
    )
    attn_cols_all = d_qkv.shape[1] + head_cols
    attn_part = outer(
        [(inputs, [d_qkv]), (d_mids, [mixed])],
        256,
        (pair_far,),
        pl.CostEstimate(
            flops=4 * d_qkv.shape[0] * width * attn_cols_all,
            transcendentals=0,
            bytes_accessed=8 * d_qkv.shape[0] * width,
        ),
    )
    attn_far = far_scatter(attn_part)
    pair_rows = to_rows(pair_far)
    product = narrow(after(d_qkv, attn_part, middle_out, *down_rows, *pair_rows), in_w)
    back_mine = own_side(product, swap_core(other_side(product)))
    back_a, _ = scatter(back_mine)
    layer_out = both_halves(after(middle_out, back_mine))
    input_grad = d_middle + through_norm(back_a, own_f * inverse_rms(own_f))
    input_grad = both_halves(input_grad)

    one = jnp.ones_like(col_gain_a)
    (grad_down,) = unpack(
        [after(piece, back_mine) for piece in down_rows], [units], [RESIDUAL]
    )
    grad_gate, grad_up = unpack(
        [after(piece, back_mine) for piece in pair_rows], [units, units], [one, one], parts=units // block
    )
    grad_query, grad_key, grad_value, grad_out = unpack(
        to_rows(after(attn_far, back_a)),
        [head_cols, HD, HD, head_cols],
        [one, one, one, RESIDUAL],
    )

    def row_sum(*pairs):
        return sum(jnp.sum(weight.astype(jnp.float32) * grad, axis=1) for weight, grad in pairs)

    gain_grads = jnp.stack(
        [
            row_sum(
                (query_weight, grad_query), (key_weight, grad_key), (value_weight, grad_value)
            ),
            row_sum((gate_weight, grad_gate), (up_weight, grad_up)),
        ]
    )
    gain_grads = gain_grads + swap_core(gain_grads)
    return (
        layer_out.reshape(hidden_in.shape),
        input_grad.reshape(hidden_in.shape),
        gain_grads[0],
        grad_query * col_gain_a,
        grad_key * col_gain_a,
        grad_value * col_gain_a,
        grad_out,
        gain_grads[1],
        grad_gate * col_gain_f,
        grad_up * col_gain_f,
        grad_down,
    )


def solution(mesh):
    sizes = dict(mesh.shape)
    fsdp, ctx, tp = sizes["fsdp"], sizes["ctx"], sizes["tp"]
    near = KVH // (ctx * tp)
    group = near * ctx
    fits = (
        tuple(mesh.axis_names) == ("fsdp", "ctx", "tp")
        and tp == 2
        and near > 0
        and group * tp == KVH
        and fsdp % near == 0
        and near == ctx == 2
    )
    if fits:
        mesh = Mesh(
            mesh.devices.reshape(fsdp // near, near, ctx, tp), ("far", "near", "ctx", "tp")
        )
        body, data = functools.partial(group_shards, group, tp), ("far", "near")
    else:
        body, data = generic_shards, ("fsdp",)
    owner = (*data, "ctx")
    weight, gain, tokens = P(owner, "tp"), P(owner), P(data, "ctx", None)
    in_specs = (
        tokens,
        P(data, None),
        gain,
        weight,
        weight,
        weight,
        weight,
        gain,
        weight,
        weight,
        weight,
        tokens,
    )
    out_specs = (
        tokens,
        tokens,
        gain,
        weight,
        weight,
        weight,
        weight,
        gain,
        weight,
        weight,
        weight,
    )
    return jax.shard_map(body, mesh=mesh, in_specs=in_specs, out_specs=out_specs, check_vma=False)
```

```python
import functools

import jax
import jax.numpy as jnp
from jax import lax
from jax.experimental import pallas as pl
from jax.experimental.pallas import tpu as pltpu
from jax.sharding import Mesh
from jax.sharding import PartitionSpec as P

HQ = 32
KVH = 8
HD = 64


EPSILON = 1e-05
SCALE = 0.015625
RESIDUAL = 0.22
THETA = 10000000.0


def rotate_pairs(values, cosine, sine):
    half = values.shape[-1] // 2
    swapped = jnp.concatenate([-values[..., half:], values[..., :half]], axis=-1)
    return values * cosine + swapped * sine


def matmul_low(left, right):
    return jnp.dot(left, right, preferred_element_type=jnp.float32)


def matmul_trans(left, right):
    return lax.dot_general(
        left, right, (((1,), (1,)), ((), ())), preferred_element_type=jnp.float32
    )


def matmul_outer(left, right):
    return lax.dot_general(
        left, right, (((0,), (0,)), ((), ())), preferred_element_type=jnp.float32
    )


def norm_back(grad_normed, gain, unit_rows, inv_rms):
    scaled = grad_normed * gain
    return inv_rms * (scaled - unit_rows * jnp.mean(scaled * unit_rows, axis=-1, keepdims=True))


def reduce_low(grad):
    low = lax.psum_scatter(
        grad.astype(jnp.bfloat16), ("fsdp", "ctx"), scatter_dimension=0, tiled=True
    )
    return low.astype(jnp.float32)


def generic_shards(
    hidden_in,
    segments,
    gain_attn,
    query_weight,
    key_weight,
    value_weight,
    out_weight,
    gain_ffn,
    gate_weight,
    up_weight,
    down_weight,
    cotangent,
):
    seqs_here, rows_here, width = hidden_in.shape
    length = segments.shape[1]
    tokens = seqs_here * rows_here
    kv_local = key_weight.shape[1] // HD
    group_size = HQ // KVH
    head_cols = kv_local * group_size * HD
    bfloat = jnp.bfloat16
    first_row = lax.axis_index("ctx") * rows_here
    own_seg = lax.dynamic_slice_in_dim(segments, first_row, rows_here, 1)
    before = jnp.sum((segments[:, None, :] < own_seg[:, :, None]).astype(jnp.int32), axis=2)
    own_place = first_row + jnp.arange(rows_here, dtype=jnp.int32)
    places = (own_place[None, :] - before).astype(jnp.float32)
    freqs = THETA ** (-jnp.arange(0, HD, 2, dtype=jnp.float32) / HD)
    phase = places[:, :, None] * freqs
    phase = jnp.concatenate([phase, phase], axis=-1)
    cosine = jnp.cos(phase)
    sine = jnp.sin(phase)
    key_place = jnp.arange(length, dtype=jnp.int32)
    allowed = (own_seg[:, :, None] == segments[:, None, :]) & (
        key_place[None, None, :] <= own_place[None, :, None]
    )
    allowed = allowed[:, None, None, :, :]
    attn_full = (
        lax.all_gather(gain_attn.astype(jnp.bfloat16), ("fsdp", "ctx"), axis=0, tiled=True).astype(
            gain_attn.dtype
        ),
        lax.all_gather(query_weight, ("fsdp", "ctx"), axis=0, tiled=True),
        lax.all_gather(key_weight, ("fsdp", "ctx"), axis=0, tiled=True),
        lax.all_gather(value_weight, ("fsdp", "ctx"), axis=0, tiled=True),
        lax.all_gather(out_weight, ("fsdp", "ctx"), axis=0, tiled=True),
    )
    gain_a, query_full, key_full, value_full, out_full = attn_full
    inputs_f = hidden_in.reshape(tokens, width).astype(jnp.float32)
    inv_a = lax.rsqrt(jnp.mean(inputs_f * inputs_f, axis=-1, keepdims=True) + EPSILON)
    unit_a = inputs_f * inv_a
    normed_a = (unit_a * gain_a).astype(bfloat)
    query_raw = matmul_low(normed_a, query_full).reshape(
        seqs_here, rows_here, kv_local, group_size, HD
    )
    key_raw = matmul_low(normed_a, key_full).reshape(seqs_here, rows_here, kv_local, HD)
    value_low = (
        matmul_low(normed_a, value_full).astype(bfloat).reshape(seqs_here, rows_here, kv_local * HD)
    )
    query_rot = rotate_pairs(
        query_raw, cosine[:, :, None, None, :], sine[:, :, None, None, :]
    ).astype(bfloat)
    key_rot = rotate_pairs(key_raw, cosine[:, :, None, :], sine[:, :, None, :]).astype(bfloat)
    key_rot = key_rot.reshape(seqs_here, rows_here, kv_local * HD)
    key_all, value_all = (
        lax.all_gather(key_rot, "ctx", axis=1, tiled=True),
        lax.all_gather(value_low, "ctx", axis=1, tiled=True),
    )
    key_all = key_all.reshape(seqs_here, length, kv_local, HD)
    value_all = value_all.reshape(seqs_here, length, kv_local, HD)

    def masked_scores():
        scores = (
            jnp.einsum("srngd,slnd->sngrl", query_rot, key_all, preferred_element_type=jnp.float32)
            * SCALE
        )
        return jnp.where(allowed, scores, -1e30)

    scores = masked_scores()
    highest = jnp.max(scores, axis=-1, keepdims=True)
    raised = jnp.exp(scores - highest)
    totals = jnp.sum(raised, axis=-1, keepdims=True)
    log_total = highest + jnp.log(totals)
    probs_low = (raised / totals).astype(bfloat)
    mixed = jnp.einsum(
        "sngrl,slnd->srngd", probs_low, value_all, preferred_element_type=jnp.float32
    )
    mixed = mixed.astype(bfloat).reshape(tokens, head_cols)
    branch_a = lax.psum(matmul_trans(mixed, out_full).astype(jnp.bfloat16), "tp").astype(
        jnp.float32
    )
    middle = inputs_f + RESIDUAL * branch_a
    ffn_full = (
        lax.all_gather(gain_ffn.astype(jnp.bfloat16), ("fsdp", "ctx"), axis=0, tiled=True).astype(
            gain_ffn.dtype
        ),
        lax.all_gather(gate_weight, ("fsdp", "ctx"), axis=0, tiled=True),
        lax.all_gather(up_weight, ("fsdp", "ctx"), axis=0, tiled=True),
        lax.all_gather(down_weight, ("fsdp", "ctx"), axis=0, tiled=True),
    )
    gain_f, gate_full, up_full, down_full = ffn_full
    inv_f = lax.rsqrt(jnp.mean(middle * middle, axis=-1, keepdims=True) + EPSILON)
    unit_f = middle * inv_f
    normed_f = (unit_f * gain_f).astype(bfloat)
    gate_pre = matmul_low(normed_f, gate_full)
    upward = matmul_low(normed_f, up_full)
    sigma = jax.nn.sigmoid(gate_pre)
    active = gate_pre * sigma
    hidden = (active * upward).astype(bfloat)
    branch_f = lax.psum(matmul_trans(hidden, down_full).astype(jnp.bfloat16), "tp").astype(
        jnp.float32
    )
    layer_out = (middle + RESIDUAL * branch_f).astype(bfloat).reshape(seqs_here, rows_here, width)
    gain_fb, gate_back, up_back, down_back = (
        lax.all_gather(gain_ffn.astype(jnp.bfloat16), ("fsdp", "ctx"), axis=0, tiled=True).astype(
            gain_ffn.dtype
        ),
        lax.all_gather(gate_weight, ("fsdp", "ctx"), axis=0, tiled=True),
        lax.all_gather(up_weight, ("fsdp", "ctx"), axis=0, tiled=True),
        lax.all_gather(down_weight, ("fsdp", "ctx"), axis=0, tiled=True),
    )
    grad_y = cotangent.reshape(tokens, width).astype(jnp.float32)
    d_branch_f = (RESIDUAL * grad_y).astype(bfloat)
    grad_down = matmul_outer(d_branch_f, hidden)
    d_hidden = matmul_low(d_branch_f, down_back)
    d_gate = (d_hidden * upward * sigma * (1.0 + gate_pre * (1.0 - sigma))).astype(bfloat)
    d_up = (d_hidden * active).astype(bfloat)
    grad_gate = matmul_outer(normed_f, d_gate)
    grad_up = matmul_outer(normed_f, d_up)
    d_normed_f = lax.psum(
        (matmul_trans(d_gate, gate_back) + matmul_trans(d_up, up_back)).astype(jnp.bfloat16), "tp"
    ).astype(jnp.float32)
    grad_gain_ffn = jnp.sum(d_normed_f * unit_f, axis=0)
    d_middle = grad_y + norm_back(d_normed_f, gain_fb, unit_f, inv_f)
    ffn_grads = (
        lax.psum_scatter(grad_gain_ffn, ("fsdp", "ctx"), scatter_dimension=0, tiled=True),
        reduce_low(grad_gate),
        reduce_low(grad_up),
        reduce_low(grad_down),
    )
    gain_ab, query_back, key_back, value_back, out_back = (
        lax.all_gather(gain_attn.astype(jnp.bfloat16), ("fsdp", "ctx"), axis=0, tiled=True).astype(
            gain_attn.dtype
        ),
        lax.all_gather(query_weight, ("fsdp", "ctx"), axis=0, tiled=True),
        lax.all_gather(key_weight, ("fsdp", "ctx"), axis=0, tiled=True),
        lax.all_gather(value_weight, ("fsdp", "ctx"), axis=0, tiled=True),
        lax.all_gather(out_weight, ("fsdp", "ctx"), axis=0, tiled=True),
    )
    d_branch_a = (RESIDUAL * d_middle).astype(bfloat)
    grad_out = matmul_outer(d_branch_a, mixed)
    d_mixed = (
        matmul_low(d_branch_a, out_back)
        .astype(bfloat)
        .reshape(seqs_here, rows_here, kv_local, group_size, HD)
    )
    probs_again = jnp.exp(masked_scores() - log_total)
    probs_again_low = probs_again.astype(bfloat)
    d_probs = jnp.einsum(
        "srngd,slnd->sngrl", d_mixed, value_all, preferred_element_type=jnp.float32
    )
    inner = jnp.sum(probs_again * d_probs, axis=-1, keepdims=True)
    d_scores = (probs_again * (d_probs - inner)).astype(bfloat)
    d_query_rot = (
        jnp.einsum("sngrl,slnd->srngd", d_scores, key_all, preferred_element_type=jnp.float32)
        * SCALE
    )
    d_key_all = (
        jnp.einsum("sngrl,srngd->slnd", d_scores, query_rot, preferred_element_type=jnp.float32)
        * SCALE
    )
    d_value_all = jnp.einsum(
        "sngrl,srngd->slnd", probs_again_low, d_mixed, preferred_element_type=jnp.float32
    )
    d_key_own, d_value_own = (
        lax.psum_scatter(
            d_key_all.reshape(seqs_here, length, kv_local * HD).astype(jnp.bfloat16),
            "ctx",
            scatter_dimension=1,
            tiled=True,
        ).astype(jnp.float32),
        lax.psum_scatter(
            d_value_all.reshape(seqs_here, length, kv_local * HD).astype(jnp.bfloat16),
            "ctx",
            scatter_dimension=1,
            tiled=True,
        ).astype(jnp.float32),
    )
    d_query = (
        rotate_pairs(d_query_rot, cosine[:, :, None, None, :], -sine[:, :, None, None, :])
        .astype(bfloat)
        .reshape(tokens, head_cols)
    )
    d_key = rotate_pairs(
        d_key_own.reshape(seqs_here, rows_here, kv_local, HD),
        cosine[:, :, None, :],
        -sine[:, :, None, :],
    )
    d_key = d_key.astype(bfloat).reshape(tokens, kv_local * HD)
    d_value = d_value_own.reshape(tokens, kv_local * HD).astype(bfloat)
    grad_query = matmul_outer(normed_a, d_query)
    grad_key = matmul_outer(normed_a, d_key)
    grad_value = matmul_outer(normed_a, d_value)
    d_normed_part = (
        matmul_trans(d_query, query_back)
        + matmul_trans(d_key, key_back)
        + matmul_trans(d_value, value_back)
    )
    d_normed_a = lax.psum(d_normed_part.astype(jnp.bfloat16), "tp").astype(jnp.float32)
    grad_gain_attn = jnp.sum(d_normed_a * unit_a, axis=0)
    input_grad = (d_middle + norm_back(d_normed_a, gain_ab, unit_a, inv_a)).reshape(
        seqs_here, rows_here, width
    )
    attn_grads = (
        lax.psum_scatter(grad_gain_attn, ("fsdp", "ctx"), scatter_dimension=0, tiled=True),
        reduce_low(grad_query),
        reduce_low(grad_key),
        reduce_low(grad_value),
        reduce_low(grad_out),
    )
    return (
        layer_out,
        input_grad,
        attn_grads[0],
        attn_grads[1],
        attn_grads[2],
        attn_grads[3],
        attn_grads[4],
        ffn_grads[0],
        ffn_grads[1],
        ffn_grads[2],
        ffn_grads[3],
    )


MAX_DOC = 512
LANES = 128
NEG = -1e30


def half_lanes(rows):
    lane = lax.broadcasted_iota(jnp.int32, (rows, LANES), 1)
    return lane % HD < HD // 2, lane < HD


def turn(slab, cosine, sine_signed):
    first, _ = half_lanes(slab.shape[0])
    swapped = jnp.where(
        first,
        pltpu.roll(slab, LANES - HD // 2, 1),
        pltpu.roll(slab, HD // 2, 1),
    )
    return slab * cosine + swapped * sine_signed


def dot_nt(left, right):
    return lax.dot_general(left, right, (((1,), (1,)), ((), ())), preferred_element_type=jnp.float32)


def dot_tn(left, right):
    return lax.dot_general(left, right, (((0,), (0,)), ((), ())), preferred_element_type=jnp.float32)


def window_mask(start, first_query, first_key, rows, keys):
    query = first_query + lax.broadcasted_iota(jnp.int32, (rows, keys), 0)
    key = first_key + lax.broadcasted_iota(jnp.int32, (rows, keys), 1)
    return (key <= query) & (key >= start)


def each_window(step, rows, window, body):
    last = window // rows - 1
    for early in range(last):
        pl.when(step == early)(functools.partial(body, (early + 1) * rows, 0))
    first = pl.multiple_of(jnp.maximum(step - last, 0) * rows, rows)
    pl.when(step >= last)(functools.partial(body, window, first))


def attend_kernel(
    rows, window, heads, place_ref, qkv_ref, cos_ref, sin_ref, start_ref, *rest,
):
    query_ref, kv_ref, mixed_ref, lse_ref, keys, values = rest[-6:]
    step = pl.program_id(1)
    _, low_half = half_lanes(rows)
    cosine, sine = cos_ref[...], sin_ref[...]

    @pl.when(step == 0)
    def _():
        keys[...] = jnp.zeros_like(keys)
        values[...] = jnp.zeros_like(values)

    width = heads * HD
    raw = qkv_ref[:, width:]
    kv = jnp.where(low_half, turn(raw, cosine, sine), raw)
    kv_ref[...] = kv.astype(jnp.bfloat16)
    moved = pltpu.roll(kv, HD, 1)
    own = pl.ds(pl.multiple_of(step * rows, rows), rows)
    keys[own, :] = jnp.where(low_half, kv, moved).astype(jnp.bfloat16)
    values[own, :] = jnp.where(low_half, moved, kv).astype(jnp.bfloat16)

    def windowed(count, first_key):
        keys_w = keys[pl.ds(first_key, count), :]
        values_w = values[pl.ds(first_key, count), :]
        allowed = window_mask(start_ref[...], step * rows, first_key, rows, count)
        for slab in range(width // LANES):
            at = slice(slab * LANES, (slab + 1) * LANES)
            rot = turn(qkv_ref[:, at], cosine, sine).astype(jnp.bfloat16)
            query_ref[:, at] = rot
            both = []
            for part in range(2):
                mine = low_half if part == 0 else jnp.logical_not(low_half)
                one = jnp.where(mine, rot, jnp.zeros_like(rot))
                scores = jnp.where(allowed, dot_nt(one * SCALE, keys_w), NEG)
                highest = jnp.max(scores, axis=1, keepdims=True)
                raised = jnp.exp(scores - highest)
                total = jnp.sum(raised, axis=1, keepdims=True)
                mixed = jnp.dot(
                    raised.astype(jnp.bfloat16), values_w, preferred_element_type=jnp.float32
                )
                both.append(mixed / total)
                head = slab * 2 + part
                lse_ref[:, head : head + 1] = highest + jnp.log(total)
            mixed_ref[:, at] = jnp.where(low_half, both[0], both[1]).astype(jnp.bfloat16)

    each_window(step, rows, window, windowed)


def attend_back_kernel(
    rows, window, heads, blocks, place_ref, query_ref, kv_ref, lse_ref, grad_ref, inv_ref, cos_ref, sin_ref, start_ref,
    out_ref, keys, values, d_keys, d_values,
):
    seq = pl.program_id(0)
    step = blocks - 1 - pl.program_id(1)
    _, low_half = half_lanes(rows)
    inv = inv_ref[...]
    cosine, sine = cos_ref[...], sin_ref[...]

    @pl.when(step == blocks - 1)
    def _():
        for block in range(blocks):
            source = pl.multiple_of(place_ref[seq * blocks + block] * rows, rows)
            kv = kv_ref[pl.ds(source, rows), :].astype(jnp.float32)
            moved = pltpu.roll(kv, HD, 1)
            at = slice(block * rows, (block + 1) * rows)
            keys[at, :] = jnp.where(low_half, kv, moved).astype(jnp.bfloat16)
            values[at, :] = jnp.where(low_half, moved, kv).astype(jnp.bfloat16)
        d_keys[...] = jnp.zeros_like(d_keys)
        d_values[...] = jnp.zeros_like(d_values)

    width = heads * HD

    def windowed(count, first_key):
        span = pl.ds(first_key, count)
        keys_w = keys[span, :]
        values_w = values[span, :]
        allowed = window_mask(start_ref[...], step * rows, first_key, rows, count)
        d_keys_w = jnp.zeros((count, LANES), jnp.float32)
        d_values_w = jnp.zeros((count, LANES), jnp.float32)
        for slab in range(width // LANES):
            at = slice(slab * LANES, (slab + 1) * LANES)
            query, grad = query_ref[:, at], grad_ref[:, at]
            both = []
            for part in range(2):
                mine = low_half if part == 0 else jnp.logical_not(low_half)
                head = slab * 2 + part
                one = jnp.where(mine, query, jnp.zeros_like(query)) * SCALE
                one_grad = jnp.where(mine, grad, jnp.zeros_like(grad))
                scores = dot_nt(one, keys_w) - lse_ref[:, head : head + 1]
                probs = jnp.exp(jnp.where(allowed, scores, NEG))
                d_probs = dot_nt(one_grad, values_w)
                inner = jnp.sum(probs * d_probs, axis=1, keepdims=True)
                d_scores = (probs * (d_probs - inner)).astype(jnp.bfloat16)
                both.append(jnp.dot(d_scores, keys_w, preferred_element_type=jnp.float32))
                d_keys_w = d_keys_w + dot_tn(d_scores, one)
                d_values_w = d_values_w + dot_tn(probs.astype(jnp.bfloat16), one_grad)
            d_query = jnp.where(low_half, both[0], both[1]) * SCALE
            out_ref[:, at] = (turn(d_query, cosine, -sine) * inv).astype(jnp.bfloat16)
        d_keys[span, :] += d_keys_w
        d_values[span, :] += d_values_w

    each_window(step, rows, window, windowed)
    own = pl.ds(pl.multiple_of(step * rows, rows), rows)
    d_key = d_keys[own, :]
    d_key = turn(d_key + pltpu.roll(d_key, HD, 1), cosine, -sine)
    d_value = d_values[own, :]
    d_value = d_value + pltpu.roll(d_value, HD, 1)
    out_ref[:, width:] = (jnp.where(low_half, d_key, d_value) * inv).astype(jnp.bfloat16)


def attend(place, qkv, cosine, sine, start, seqs, blocks, rows, heads, others):
    tokens = qkv.shape[0]
    width = heads * HD
    window = min(blocks * rows, rows + -(-MAX_DOC // rows) * rows)

    def placed(cols):
        return pl.BlockSpec((rows, cols), lambda s, i, place: (place[s * blocks + i], 0))

    def natural(cols):
        return pl.BlockSpec((rows, cols), lambda s, i, place: (s * blocks + i, 0))

    return pl.pallas_call(
        functools.partial(attend_kernel, rows, window, heads),
        out_shape=(
            jax.ShapeDtypeStruct((tokens, width), jnp.bfloat16),
            jax.ShapeDtypeStruct((tokens, LANES), jnp.bfloat16),
            jax.ShapeDtypeStruct((tokens, width), jnp.bfloat16),
            jax.ShapeDtypeStruct((tokens, heads), jnp.float32),
        ),
        grid_spec=pltpu.PrefetchScalarGridSpec(
            num_scalar_prefetch=1,
            grid=(seqs, blocks),
            in_specs=[placed(width + LANES), natural(LANES), natural(LANES), natural(1)]
            + [ANYWHERE] * len(others),
            out_specs=[placed(width), placed(LANES), placed(width), placed(heads)],
            scratch_shapes=[pltpu.VMEM((blocks * rows, LANES), jnp.bfloat16)] * 2,
        ),
        compiler_params=pltpu.CompilerParams(vmem_limit_bytes=48 << 20),
        name="attend",
    )(place, qkv, cosine, sine, start, *others)


def attend_back(place, query, kv, lse, grad, inv, cosine, sine, start, seqs, blocks, rows, heads):
    tokens = query.shape[0]
    width = heads * HD
    window = min(blocks * rows, rows + -(-MAX_DOC // rows) * rows)

    def placed(cols):
        return pl.BlockSpec(
            (rows, cols), lambda s, i, place: (place[s * blocks + blocks - 1 - i], 0)
        )

    def natural(cols):
        return pl.BlockSpec((rows, cols), lambda s, i, place: (s * blocks + blocks - 1 - i, 0))

    return pl.pallas_call(
        functools.partial(attend_back_kernel, rows, window, heads, blocks),
        out_shape=jax.ShapeDtypeStruct((tokens, width + LANES), jnp.bfloat16),
        grid_spec=pltpu.PrefetchScalarGridSpec(
            num_scalar_prefetch=1,
            grid=(seqs, blocks),
            in_specs=[
                placed(width),
                pl.BlockSpec((tokens, LANES), lambda s, i, place: (0, 0)),
                placed(heads),
                placed(width),
                placed(1),
                natural(LANES),
                natural(LANES),
                natural(1),
            ],
            out_specs=placed(width + LANES),
            scratch_shapes=[pltpu.VMEM((blocks * rows, LANES), jnp.bfloat16)] * 2
            + [pltpu.VMEM((blocks * rows, LANES), jnp.float32)] * 2,
        ),
        compiler_params=pltpu.CompilerParams(vmem_limit_bytes=48 << 20),
        cost_estimate=pl.CostEstimate(
            flops=48 * tokens * window * heads * LANES,
            transcendentals=tokens * window * heads,
            bytes_accessed=tokens * (8 * width + 12 * LANES),
        ),
        name="attend_back",
    )(place, query, kv, lse, grad, inv, cosine, sine, start)


VMEM_LIMIT = 56 << 20
ANYWHERE = pl.BlockSpec(memory_space=pl.ANY)


def fetch(pieces, whole, sems):
    copies, at = [], 0
    for n, piece in enumerate(pieces):
        span = slice(at, at + piece.shape[0])
        copy = pltpu.make_async_copy(piece, whole.at[span, :], sems.at[n])
        copy.start()
        copies.append((copy, span))
        at += piece.shape[0]
    return copies


def inverse_rms(values):
    values = values.astype(jnp.float32)
    return lax.rsqrt(jnp.mean(values * values, axis=-1, keepdims=True) + EPSILON)


def rows_of(pieces):
    return sum(piece.shape[0] for piece in pieces)


def project_kernel(count, tokens, normed, factor, *refs):
    pieces, rest = refs[:count], refs[count + tokens :]
    weight_ref, out_ref = rest[:2]
    whole, sems = rest[-2:]
    for copy, span in fetch(pieces, whole, sems):
        copy.wait()
        values = whole[span, :]
        product = jnp.dot(values, weight_ref[...], preferred_element_type=jnp.float32)
        if normed:
            inv = inverse_rms(values)
            rest[2][span, :] = inv
            product = product * inv
        else:
            product = product * factor
        out_ref[span, :] = product.astype(out_ref.dtype)


def project(pieces, weight, normed, factor, dtype, tokens=()):
    count, width = rows_of(pieces), pieces[0].shape[1]
    out_shape = [jax.ShapeDtypeStruct((count, weight.shape[1]), dtype)]
    if normed:
        out_shape.append(jax.ShapeDtypeStruct((count, 1), jnp.float32))
    vmem = pl.BlockSpec(memory_space=pltpu.VMEM)
    return pl.pallas_call(
        functools.partial(project_kernel, len(pieces), len(tokens), normed, factor),
        out_shape=out_shape,
        in_specs=[ANYWHERE] * (len(pieces) + len(tokens)) + [vmem],
        out_specs=[vmem] * len(out_shape),
        scratch_shapes=[
            pltpu.VMEM((count, width), jnp.bfloat16),
            pltpu.SemaphoreType.DMA((len(pieces),)),
        ],
        compiler_params=pltpu.CompilerParams(vmem_limit_bytes=VMEM_LIMIT),
        cost_estimate=pl.CostEstimate(
            flops=4 * count * width * weight.shape[1],
            transcendentals=0,
            bytes_accessed=2 * count * width,
        ),
        name="project",
    )(*pieces, *tokens, weight)


def gated_kernel(count, chunk, *refs):
    pieces, rest = refs[:count], refs[count:]
    pair_w, gate_ref, up_ref, hidden_ref, inv_ref, whole, sems = rest
    block = gate_ref.shape[1]

    @pl.when(pl.program_id(0) == 0)
    def _():
        for copy, span in fetch(pieces, whole, sems):
            copy.wait()
            inv_ref[span, :] = inverse_rms(whole[span, :])

    for at in range(0, whole.shape[0], chunk):
        span = slice(at, at + chunk)
        both = jnp.dot(whole[span, :], pair_w[...], preferred_element_type=jnp.float32)
        both = both * inv_ref[span, :]
        gate, up = both[:, :block], both[:, block:]
        gate_ref[span, :] = gate.astype(jnp.bfloat16)
        up_ref[span, :] = up.astype(jnp.bfloat16)
        hidden_ref[span, :] = (gate * lax.logistic(gate) * up).astype(jnp.bfloat16)


def gated(pieces, pair_w, block, chunk):
    tokens, width = rows_of(pieces), pieces[0].shape[1]
    units = pair_w.shape[1] // 2
    low = jax.ShapeDtypeStruct((tokens, units), jnp.bfloat16)
    out = pl.BlockSpec((tokens, block), lambda j: (0, j))
    return pl.pallas_call(
        functools.partial(gated_kernel, len(pieces), chunk),
        out_shape=[low, low, low, jax.ShapeDtypeStruct((tokens, 1), jnp.float32)],
        grid=(units // block,),
        in_specs=[ANYWHERE] * len(pieces)
        + [pl.BlockSpec((width, 2 * block), lambda j: (0, j))],
        out_specs=[out, out, out, pl.BlockSpec((tokens, 1), lambda j: (0, 0))],
        scratch_shapes=[
            pltpu.VMEM((tokens, width), jnp.bfloat16),
            pltpu.SemaphoreType.DMA((len(pieces),)),
        ],
        compiler_params=pltpu.CompilerParams(vmem_limit_bytes=VMEM_LIMIT),
        name="gated",
    )(*pieces, pair_w)


def gated_back_kernel(count, tokens, chunk, *refs):
    pieces, rest = refs[:count], refs[count + tokens :]
    down_w, gate_ref, up_ref, inv_ref, out_ref, whole, sems = rest
    block = gate_ref.shape[1]

    @pl.when(pl.program_id(0) == 0)
    def _():
        for copy, _ in fetch(pieces, whole, sems):
            copy.wait()

    for at in range(0, whole.shape[0], chunk):
        span = slice(at, at + chunk)
        d_hidden = jnp.dot(whole[span, :], down_w[...], preferred_element_type=jnp.float32)
        d_hidden = d_hidden * (RESIDUAL * inv_ref[span, :])
        gate = gate_ref[span, :].astype(jnp.float32)
        up = up_ref[span, :].astype(jnp.float32)
        sigma = lax.logistic(gate)
        out_ref[span, :block] = (d_hidden * up * sigma * (1.0 + gate * (1.0 - sigma))).astype(
            jnp.bfloat16
        )
        out_ref[span, block:] = (d_hidden * gate * sigma).astype(jnp.bfloat16)


def gated_back(pieces, down_w, gate, up, inv, block, chunk, others):
    tokens, width = rows_of(pieces), pieces[0].shape[1]
    units = down_w.shape[1]
    tall = pl.BlockSpec((tokens, block), lambda j: (0, j))
    return pl.pallas_call(
        functools.partial(gated_back_kernel, len(pieces), len(others), chunk),
        out_shape=jax.ShapeDtypeStruct((tokens, 2 * units), jnp.bfloat16),
        grid=(units // block,),
        in_specs=[ANYWHERE] * (len(pieces) + len(others))
        + [
            pl.BlockSpec((width, block), lambda j: (0, j)),
            tall,
            tall,
            pl.BlockSpec((tokens, 1), lambda j: (0, 0)),
        ],
        out_specs=pl.BlockSpec((tokens, 2 * block), lambda j: (0, j)),
        scratch_shapes=[
            pltpu.VMEM((tokens, width), jnp.bfloat16),
            pltpu.SemaphoreType.DMA((len(pieces),)),
        ],
        compiler_params=pltpu.CompilerParams(vmem_limit_bytes=VMEM_LIMIT),
        name="gated_back",
    )(*pieces, *others, down_w, gate, up, inv)


def outer_kernel(counts, tokens, block, *refs):
    sources, at = [], 0
    for count, rights in counts:
        sources.append((refs[at : at + count], refs[at + count : at + count + rights]))
        at += count + rights
    out_ref, scratch = refs[at + tokens], refs[at + tokens + 1 :]
    step = pl.program_id(0)

    @pl.when(step == 0)
    def _():
        copies = []
        for n, (pieces, _) in enumerate(sources):
            copies += fetch(pieces, scratch[2 * n], scratch[2 * n + 1])
        for copy, _ in copies:
            copy.wait()

    first = 0
    columns = pl.ds(pl.multiple_of(step * block, block), block)
    for n, (_, rights) in enumerate(sources):
        left = scratch[2 * n][:, columns]
        for right in rights:
            out_ref[:, first : first + right.shape[1]] = dot_tn(left, right[...]).astype(
                out_ref.dtype
            )
            first += right.shape[1]


def outer(sources, block, tokens=(), cost=None):
    operands, in_specs, scratch, counts, total = [], [], [], [], 0
    for pieces, rights in sources:
        count, width = rows_of(pieces), pieces[0].shape[1]
        operands += [*pieces, *rights]
        in_specs += [ANYWHERE] * len(pieces)
        in_specs += [pl.BlockSpec(right.shape, lambda j: (0, 0)) for right in rights]
        scratch += [
            pltpu.VMEM((count, width), jnp.bfloat16),
            pltpu.SemaphoreType.DMA((len(pieces),)),
        ]
        counts.append((len(pieces), len(rights)))
        total += sum(right.shape[1] for right in rights)
    return pl.pallas_call(
        functools.partial(outer_kernel, counts, len(tokens), block),
        out_shape=jax.ShapeDtypeStruct((width, total), jnp.bfloat16),
        grid=(width // block,),
        in_specs=in_specs + [ANYWHERE] * len(tokens),
        out_specs=pl.BlockSpec((block, total), lambda j: (j, 0)),
        scratch_shapes=scratch,
        compiler_params=pltpu.CompilerParams(vmem_limit_bytes=VMEM_LIMIT),
        cost_estimate=cost,
        name="outer",
    )(*operands, *tokens)


def rows_kernel(added, left_ref, weight_ref, *rest):
    product = dot_nt(left_ref[...], weight_ref[...])
    if added:
        product = product + rest[0][...].astype(jnp.float32)
    rest[-1][...] = product.astype(rest[-1].dtype)


def rows_product(left, weight, first, size, add, block):
    width, depth = weight.shape
    out = pl.BlockSpec((size, block), lambda j: (0, j))
    extra = [] if add is None else [add]
    return pl.pallas_call(
        functools.partial(rows_kernel, len(extra)),
        out_shape=jax.ShapeDtypeStruct((size, width), jnp.bfloat16),
        grid=(width // block,),
        in_specs=[
            pl.BlockSpec((size, depth), lambda j: (first // size, 0)),
            pl.BlockSpec((block, depth), lambda j: (j, 0)),
        ]
        + [out] * len(extra),
        out_specs=out,
        compiler_params=pltpu.CompilerParams(vmem_limit_bytes=VMEM_LIMIT),
        name="rows_product",
    )(left, weight, *extra)


def fold_kernel(tokens, mine, from_near, from_ctx, *rest):
    to_ctx, to_near = rest[tokens:]
    rows, half = mine.shape[0] // 4, mine.shape[0] // 8
    ctx_first, near_last = slice(rows, rows + half), slice(2 * rows + half, 3 * rows)
    to_ctx[...] = (
        mine[ctx_first, :].astype(jnp.float32) + from_near[...].astype(jnp.float32)
    ).astype(jnp.bfloat16)
    to_near[...] = (
        mine[near_last, :].astype(jnp.float32) + from_ctx[...].astype(jnp.float32)
    ).astype(jnp.bfloat16)


def fold(mine, from_near, from_ctx, tokens):
    half = jax.ShapeDtypeStruct(from_near.shape, jnp.bfloat16)
    vmem = pl.BlockSpec(memory_space=pltpu.VMEM)
    return pl.pallas_call(
        functools.partial(fold_kernel, len(tokens)),
        out_shape=[half, half],
        in_specs=[vmem] * 3 + [ANYWHERE] * len(tokens),
        out_specs=[vmem] * 2,
        compiler_params=pltpu.CompilerParams(vmem_limit_bytes=VMEM_LIMIT),
        name="fold",
    )(mine, from_near, from_ctx, *tokens)


def finish_kernel(group, me_ref, *refs):
    pieces, rest = refs[:group], refs[group:]
    query_w, key_w, value_w, gain_ref, grad_q, grad_k, grad_v, grad_o, sums = rest
    me, gain = me_ref[0], gain_ref[...]
    lows = [piece[...].astype(jnp.float32) for piece in pieces]
    total = jnp.zeros(sums.shape, jnp.float32)
    for owner in range(group):
        mine = lows[0]
        for m in range(1, group):
            mine = jnp.where(me == (owner ^ m), lows[m], mine)
        first = 0
        for weight, out in ((query_w, grad_q), (key_w, grad_k), (value_w, grad_v)):
            size = weight.shape[1] // group
            grad = mine[:, first : first + size]
            at = slice(owner * size, (owner + 1) * size)
            out[:, at] = grad * gain
            total = total + jnp.sum(
                weight[:, at].astype(jnp.float32) * grad, axis=1, keepdims=True
            )
            first += size
        size = grad_o.shape[1] // group
        grad_o[:, owner * size : (owner + 1) * size] = mine[:, first:] * RESIDUAL
    sums[...] = total


def finish(me, pieces, query_w, key_w, value_w, gain, out_cols):
    deep = query_w.shape[0]
    vmem = pl.BlockSpec(memory_space=pltpu.VMEM)
    shapes = [w.shape[1] for w in (query_w, key_w, value_w)] + [out_cols, 1]
    return pl.pallas_call(
        functools.partial(finish_kernel, len(pieces)),
        out_shape=[jax.ShapeDtypeStruct((deep, cols), jnp.float32) for cols in shapes],
        in_specs=[pl.BlockSpec(memory_space=pltpu.SMEM)] + [vmem] * (len(pieces) + 4),
        out_specs=[vmem] * len(shapes),
        compiler_params=pltpu.CompilerParams(vmem_limit_bytes=VMEM_LIMIT),
        name="finish",
    )(me, *pieces, query_w, key_w, value_w, gain)


def after_kernel(*refs):
    del refs


def after(value, *tokens):
    return pl.pallas_call(
        after_kernel,
        out_shape=jax.ShapeDtypeStruct(value.shape, value.dtype),
        in_specs=[ANYWHERE] * (1 + len(tokens)),
        out_specs=ANYWHERE,
        input_output_aliases={0: 0},
        name="after",
    )(value, *tokens)


def group_shards(
    group, cores,
    hidden_in, segments, gain_attn, query_weight, key_weight, value_weight, out_weight,
    gain_ffn, gate_weight, up_weight, down_weight, cotangent,
):
    bfloat = jnp.bfloat16
    seqs_here, rows_here, width = hidden_in.shape
    length = segments.shape[1]
    rows = rows_here // cores
    near = group // (length // rows_here)
    blocks = length // rows
    heads = HQ // KVH
    me = lax.axis_index(("near", "ctx")).astype(jnp.uint32)
    me_core = lax.axis_index("tp").astype(jnp.uint32)

    def swap(value, m):
        return lax.ppermute(value, ("near", "ctx"), [(i, i ^ m) for i in range(group)])

    def swap_core(value):
        return lax.ppermute(value, "tp", [(0, 1), (1, 0)])

    def gather(own, later=()):
        half = own.shape[0] // 2
        by_ctx, by_near = swap(own, 1), swap(own, 2)
        if later:
            by_ctx, by_near = after(by_ctx, *later), after(by_near, *later)
        opposite = [swap(by_ctx[:half], 2), swap(by_near[half:], 1)]
        same = [own, by_ctx, by_near, *opposite]
        return same + [swap_core(v) for v in same]

    def other_side(product):
        return product(group * rows, group * rows, None)

    def own_side(product, other):
        return product(0, group * rows, other)

    def scatter(mine, *tokens):
        half = rows // 2
        ctx_low, near_low, opposite = (mine[m * rows : (m + 1) * rows] for m in range(1, group))
        from_near, from_ctx = swap(opposite[:half], 2), swap(opposite[half:], 1)
        near_first, ctx_last = swap(near_low[:half], 2), swap(ctx_low[half:], 1)
        to_ctx, to_near = fold(mine, from_near, from_ctx, tokens)
        ctx_first, near_last = swap(to_ctx, 1), swap(to_near, 2)
        total = jnp.concatenate(
            [
                mine[:half].astype(jnp.float32)
                + ctx_first.astype(jnp.float32)
                + near_first.astype(jnp.float32),
                mine[half:rows].astype(jnp.float32)
                + ctx_last.astype(jnp.float32)
                + near_last.astype(jnp.float32),
            ]
        )
        return total, (ctx_first, near_last)

    def scatter_direct(mine):
        total = mine[:rows].astype(jnp.float32)
        for m in range(1, group):
            total = total + swap(mine[m * rows : (m + 1) * rows], m).astype(jnp.float32)
        return total

    def plain(left, weight):
        return lambda first, size, add: rows_product(left, weight, first, size, add, 512)

    def narrow(left, weight):
        def product(first, size, add):
            out = matmul_trans(left[first : first + size], weight)
            return (out if add is None else out + add.astype(jnp.float32)).astype(bfloat)

        return product

    def own_half(value):
        return cut(value, me_core, rows, 0)

    def both_halves(own):
        other = swap_core(own)
        whole = jnp.zeros((rows_here, own.shape[1]), own.dtype)
        whole = put(whole, own, me_core, 0)
        return put(whole, other, me_core ^ jnp.uint32(1), 0)

    def cut(value, index, size, axis):
        starts = [jnp.uint32(0)] * value.ndim
        starts[axis] = index * jnp.uint32(size)
        sizes = list(value.shape)
        sizes[axis] = size
        return lax.dynamic_slice(value, starts, sizes)

    def put(whole, piece, index, axis):
        starts = [jnp.uint32(0)] * whole.ndim
        starts[axis] = index * jnp.uint32(piece.shape[axis])
        return lax.dynamic_update_slice(whole, piece, starts)

    def to_columns(*weights, parts=1, later=()):
        whole = None
        for m in range(group):
            there = me ^ jnp.uint32(m)
            own = [cut(w, there, w.shape[1] // group, 1) for w in weights]
            sizes = [w.shape[1] // parts for w in own]
            piece = jnp.concatenate(
                [w[:, n * size : (n + 1) * size] for n in range(parts) for w, size in zip(own, sizes)],
                axis=1,
            )
            if m:
                piece = swap(after(piece, *later) if later else piece, m)
            if whole is None:
                whole = jnp.zeros((group * piece.shape[0], piece.shape[1]), piece.dtype)
            whole = put(whole, piece, there, 0)
        return whole

    def to_rows(grad):
        deep = grad.shape[0] // group
        pieces = [cut(grad, me ^ jnp.uint32(m), deep, 0) for m in range(group)]
        return [swap(piece, m) if m else piece for m, piece in enumerate(pieces)]

    def unpack(pieces, widths, factors, parts=1):
        first, wholes, turn_width = 0, [], sum(widths) // parts
        for cols, factor in zip(widths, factors):
            size = cols // parts
            whole = jnp.zeros((pieces[0].shape[0], group * cols), jnp.float32)
            for m, piece in enumerate(pieces):
                part = jnp.concatenate(
                    [
                        piece[:, n * turn_width + first : n * turn_width + first + size]
                        for n in range(parts)
                    ],
                    axis=1,
                )
                part = part.astype(jnp.float32) * factor
                whole = put(whole, part, me ^ jnp.uint32(m), 1)
            first += size
            wholes.append(whole)
        return wholes

    def far_gather(weight):
        return lax.all_gather(weight, "far", axis=0, tiled=True)

    def far_scatter(grad):
        return lax.psum_scatter(grad.astype(bfloat), "far", scatter_dimension=0, tiled=True)

    deep = query_weight.shape[0]
    col_gain_a, col_gain_f = gain_attn[:, None], gain_ffn[:, None]

    def scaled(weight, gain):
        return (weight.astype(jnp.float32) * gain).astype(bfloat)

    attn_cols = to_columns(
        scaled(query_weight, col_gain_a),
        scaled(key_weight, col_gain_a),
        scaled(value_weight, col_gain_a),
        out_weight,
    )
    attn_w = far_gather(attn_cols)
    head_cols = heads * HD
    in_w, out_w = attn_w[:, : head_cols + 2 * HD], attn_w[:, head_cols + 2 * HD :]

    gain_later = after(col_gain_f, attn_cols)
    units = down_weight.shape[1] // group
    block = min(units, 256)
    pair_cols = to_columns(
        scaled(gate_weight, gain_later), scaled(up_weight, gain_later), parts=units // block
    )
    seg_all = jnp.concatenate(
        [segments] + [swap(segments, n * (group // near)) for n in range(1, near)],
        axis=0,
    )
    start = jnp.sum((seg_all[:, None, :] < seg_all[:, :, None]).astype(jnp.int32), axis=2)
    places = (jnp.arange(length, dtype=jnp.int32)[None, :] - start).astype(jnp.float32)
    freqs = THETA ** (-jnp.arange(0, HD, 2, dtype=jnp.float32) / HD)
    phase = places.reshape(-1)[:, None] * freqs
    cosine, sine = jnp.cos(phase), jnp.sin(phase)
    cosine = jnp.concatenate([cosine, cosine, cosine, cosine], axis=1)
    sine = jnp.concatenate([-sine, sine, -sine, sine], axis=1)
    start = start.reshape(-1)[:, None]
    at = jnp.arange(near * blocks, dtype=jnp.int32)
    in_seq = at % blocks
    here_ctx = lax.axis_index("ctx")
    place = (
        ((in_seq % cores) ^ lax.axis_index("tp")) * group
        + (at // blocks) * (group // near)
        + ((in_seq // cores) ^ here_ctx)
    ).astype(jnp.int32)

    own_in = after(own_half(hidden_in.reshape(rows_here, width)), pair_cols)
    inputs = gather(own_in, (cosine, sine))
    pair_w = far_gather(pair_cols)
    own_cot = own_half(cotangent.reshape(rows_here, width))

    qkv, inv_a = project(inputs, in_w, True, None, jnp.float32)
    down_cols = to_columns(down_weight, later=(inv_a,))
    down_w = far_gather(down_cols)
    query, kv, mixed, lse = attend(
        place, qkv, cosine, sine, start, near, blocks, rows, heads, ()
    )
    product = narrow(mixed, out_w)
    branch_a, _ = scatter(own_side(product, swap_core(other_side(product))))
    own_f = own_in.astype(jnp.float32)
    middle = own_f + RESIDUAL * branch_a

    mids = gather(after(middle.astype(bfloat), down_cols))
    gate_pre, upward, hidden, inv_f = gated(mids, pair_w, block, 512)
    cots = gather(after(own_cot, *mids[1 : len(mids) // 2]), (inv_f,))
    down_part = outer([(cots, [hidden])], 512)
    down_far = far_scatter(down_part)
    d_both = gated_back(cots, down_w, gate_pre, upward, inv_f, block, 512, (down_part,))
    product = plain(d_both, pair_w)
    other = other_side(product)
    pair_part = outer([(mids, [d_both])], 512, (other,))
    pair_far = far_scatter(pair_part)
    back_mine = own_side(product, after(swap_core(other), pair_part))
    product = plain(after(hidden, back_mine), down_w)
    other = other_side(product)
    back_f, _ = scatter(back_mine, other, down_far)
    branch_mine = own_side(product, swap_core(other))

    def through_norm(grad, unit):
        return grad - unit * jnp.mean(grad * unit, axis=-1, keepdims=True)

    d_middle = own_cot.astype(jnp.float32) + through_norm(back_f, middle * inverse_rms(middle))

    d_mids = gather(after(d_middle.astype(bfloat), branch_mine))
    branch_f = scatter_direct(after(branch_mine, *d_mids[1 : len(d_mids) // 2]))
    middle_out = (middle + RESIDUAL * branch_f).astype(bfloat)
    (d_mixed,) = project(d_mids, out_w, False, RESIDUAL, bfloat)
    down_rows = to_rows(after(down_far, d_mixed))
    d_qkv = attend_back(
        place, query, kv, lse, d_mixed, inv_a, cosine, sine, start, near, blocks, rows, heads
    )
    attn_cols_all = d_qkv.shape[1] + head_cols
    attn_part = outer(
        [(inputs, [d_qkv]), (d_mids, [mixed])],
        512,
        (pair_far,),
        pl.CostEstimate(
            flops=4 * d_qkv.shape[0] * width * attn_cols_all,
            transcendentals=0,
            bytes_accessed=8 * d_qkv.shape[0] * width,
        ),
    )
    attn_far = far_scatter(attn_part)
    pair_rows = to_rows(pair_far)
    product = narrow(after(d_qkv, attn_part, middle_out, *down_rows, *pair_rows), in_w)
    back_mine = own_side(product, swap_core(other_side(product)))
    back_a, passed = scatter(back_mine)
    layer_out = both_halves(after(middle_out, back_mine))
    input_grad = d_middle + through_norm(back_a, own_f * inverse_rms(own_f))

    one = jnp.ones_like(col_gain_a)
    (grad_down,) = unpack(
        [after(piece, back_mine) for piece in down_rows], [units], [RESIDUAL]
    )
    grad_gate, grad_up = unpack(
        [after(piece, back_mine) for piece in pair_rows], [units, units], [one, one], parts=units // block
    )
    attn_rows = to_rows(after(attn_far, *passed))
    grad_query, grad_key, grad_value, grad_out, gain_a = finish(
        me.astype(jnp.int32)[None],
        attn_rows,
        query_weight,
        key_weight,
        value_weight,
        col_gain_a,
        out_weight.shape[1],
    )

    def row_sum(*pairs):
        return sum(jnp.sum(weight.astype(jnp.float32) * grad, axis=1) for weight, grad in pairs)

    input_grad = both_halves(after(input_grad, gain_a))
    gain_f = row_sum((gate_weight, grad_gate), (up_weight, grad_up))
    gain_f = gain_f + swap_core(gain_f)
    gain_a = gain_a[:, 0]
    gain_a = gain_a + swap_core(gain_a)
    return (
        layer_out.reshape(hidden_in.shape),
        input_grad.reshape(hidden_in.shape),
        gain_a,
        grad_query,
        grad_key,
        grad_value,
        grad_out,
        gain_f,
        grad_gate * col_gain_f,
        grad_up * col_gain_f,
        grad_down,
    )


def solution(mesh):
    sizes = dict(mesh.shape)
    fsdp, ctx, tp = sizes["fsdp"], sizes["ctx"], sizes["tp"]
    near = KVH // (ctx * tp)
    group = near * ctx
    fits = (
        tuple(mesh.axis_names) == ("fsdp", "ctx", "tp")
        and tp == 2
        and near > 0
        and group * tp == KVH
        and fsdp % near == 0
        and near == ctx == 2
    )
    if fits:
        mesh = Mesh(
            mesh.devices.reshape(fsdp // near, near, ctx, tp), ("far", "near", "ctx", "tp")
        )
        body, data = functools.partial(group_shards, group, tp), ("far", "near")
    else:
        body, data = generic_shards, ("fsdp",)
    owner = (*data, "ctx")
    weight, gain, tokens = P(owner, "tp"), P(owner), P(data, "ctx", None)
    in_specs = (
        tokens,
        P(data, None),
        gain,
        weight,
        weight,
        weight,
        weight,
        gain,
        weight,
        weight,
        weight,
        tokens,
    )
    out_specs = (
        tokens,
        tokens,
        gain,
        weight,
        weight,
        weight,
        weight,
        gain,
        weight,
        weight,
        weight,
    )
    return jax.shard_map(body, mesh=mesh, in_specs=in_specs, out_specs=out_specs, check_vma=False)
```

```python
import functools

import jax
import jax.numpy as jnp
from jax import lax
from jax.experimental import pallas as pl
from jax.experimental.pallas import tpu as pltpu
from jax.sharding import Mesh
from jax.sharding import PartitionSpec as P

HQ = 32
KVH = 8
HD = 64


EPSILON = 1e-05
SCALE = 0.015625
RESIDUAL = 0.22
THETA = 10000000.0


def rotate_pairs(values, cosine, sine):
    half = values.shape[-1] // 2
    swapped = jnp.concatenate([-values[..., half:], values[..., :half]], axis=-1)
    return values * cosine + swapped * sine


def matmul_low(left, right):
    return jnp.dot(left, right, preferred_element_type=jnp.float32)


def matmul_trans(left, right):
    return lax.dot_general(
        left, right, (((1,), (1,)), ((), ())), preferred_element_type=jnp.float32
    )


def matmul_outer(left, right):
    return lax.dot_general(
        left, right, (((0,), (0,)), ((), ())), preferred_element_type=jnp.float32
    )


def norm_back(grad_normed, gain, unit_rows, inv_rms):
    scaled = grad_normed * gain
    return inv_rms * (scaled - unit_rows * jnp.mean(scaled * unit_rows, axis=-1, keepdims=True))


def reduce_low(grad):
    low = lax.psum_scatter(
        grad.astype(jnp.bfloat16), ("fsdp", "ctx"), scatter_dimension=0, tiled=True
    )
    return low.astype(jnp.float32)


def generic_shards(
    hidden_in,
    segments,
    gain_attn,
    query_weight,
    key_weight,
    value_weight,
    out_weight,
    gain_ffn,
    gate_weight,
    up_weight,
    down_weight,
    cotangent,
):
    seqs_here, rows_here, width = hidden_in.shape
    length = segments.shape[1]
    tokens = seqs_here * rows_here
    kv_local = key_weight.shape[1] // HD
    group_size = HQ // KVH
    head_cols = kv_local * group_size * HD
    bfloat = jnp.bfloat16
    first_row = lax.axis_index("ctx") * rows_here
    own_seg = lax.dynamic_slice_in_dim(segments, first_row, rows_here, 1)
    before = jnp.sum((segments[:, None, :] < own_seg[:, :, None]).astype(jnp.int32), axis=2)
    own_place = first_row + jnp.arange(rows_here, dtype=jnp.int32)
    places = (own_place[None, :] - before).astype(jnp.float32)
    freqs = THETA ** (-jnp.arange(0, HD, 2, dtype=jnp.float32) / HD)
    phase = places[:, :, None] * freqs
    phase = jnp.concatenate([phase, phase], axis=-1)
    cosine = jnp.cos(phase)
    sine = jnp.sin(phase)
    key_place = jnp.arange(length, dtype=jnp.int32)
    allowed = (own_seg[:, :, None] == segments[:, None, :]) & (
        key_place[None, None, :] <= own_place[None, :, None]
    )
    allowed = allowed[:, None, None, :, :]
    attn_full = (
        lax.all_gather(gain_attn.astype(jnp.bfloat16), ("fsdp", "ctx"), axis=0, tiled=True).astype(
            gain_attn.dtype
        ),
        lax.all_gather(query_weight, ("fsdp", "ctx"), axis=0, tiled=True),
        lax.all_gather(key_weight, ("fsdp", "ctx"), axis=0, tiled=True),
        lax.all_gather(value_weight, ("fsdp", "ctx"), axis=0, tiled=True),
        lax.all_gather(out_weight, ("fsdp", "ctx"), axis=0, tiled=True),
    )
    gain_a, query_full, key_full, value_full, out_full = attn_full
    inputs_f = hidden_in.reshape(tokens, width).astype(jnp.float32)
    inv_a = lax.rsqrt(jnp.mean(inputs_f * inputs_f, axis=-1, keepdims=True) + EPSILON)
    unit_a = inputs_f * inv_a
    normed_a = (unit_a * gain_a).astype(bfloat)
    query_raw = matmul_low(normed_a, query_full).reshape(
        seqs_here, rows_here, kv_local, group_size, HD
    )
    key_raw = matmul_low(normed_a, key_full).reshape(seqs_here, rows_here, kv_local, HD)
    value_low = (
        matmul_low(normed_a, value_full).astype(bfloat).reshape(seqs_here, rows_here, kv_local * HD)
    )
    query_rot = rotate_pairs(
        query_raw, cosine[:, :, None, None, :], sine[:, :, None, None, :]
    ).astype(bfloat)
    key_rot = rotate_pairs(key_raw, cosine[:, :, None, :], sine[:, :, None, :]).astype(bfloat)
    key_rot = key_rot.reshape(seqs_here, rows_here, kv_local * HD)
    key_all, value_all = (
        lax.all_gather(key_rot, "ctx", axis=1, tiled=True),
        lax.all_gather(value_low, "ctx", axis=1, tiled=True),
    )
    key_all = key_all.reshape(seqs_here, length, kv_local, HD)
    value_all = value_all.reshape(seqs_here, length, kv_local, HD)

    def masked_scores():
        scores = (
            jnp.einsum("srngd,slnd->sngrl", query_rot, key_all, preferred_element_type=jnp.float32)
            * SCALE
        )
        return jnp.where(allowed, scores, -1e30)

    scores = masked_scores()
    highest = jnp.max(scores, axis=-1, keepdims=True)
    raised = jnp.exp(scores - highest)
    totals = jnp.sum(raised, axis=-1, keepdims=True)
    log_total = highest + jnp.log(totals)
    probs_low = (raised / totals).astype(bfloat)
    mixed = jnp.einsum(
        "sngrl,slnd->srngd", probs_low, value_all, preferred_element_type=jnp.float32
    )
    mixed = mixed.astype(bfloat).reshape(tokens, head_cols)
    branch_a = lax.psum(matmul_trans(mixed, out_full).astype(jnp.bfloat16), "tp").astype(
        jnp.float32
    )
    middle = inputs_f + RESIDUAL * branch_a
    ffn_full = (
        lax.all_gather(gain_ffn.astype(jnp.bfloat16), ("fsdp", "ctx"), axis=0, tiled=True).astype(
            gain_ffn.dtype
        ),
        lax.all_gather(gate_weight, ("fsdp", "ctx"), axis=0, tiled=True),
        lax.all_gather(up_weight, ("fsdp", "ctx"), axis=0, tiled=True),
        lax.all_gather(down_weight, ("fsdp", "ctx"), axis=0, tiled=True),
    )
    gain_f, gate_full, up_full, down_full = ffn_full
    inv_f = lax.rsqrt(jnp.mean(middle * middle, axis=-1, keepdims=True) + EPSILON)
    unit_f = middle * inv_f
    normed_f = (unit_f * gain_f).astype(bfloat)
    gate_pre = matmul_low(normed_f, gate_full)
    upward = matmul_low(normed_f, up_full)
    sigma = jax.nn.sigmoid(gate_pre)
    active = gate_pre * sigma
    hidden = (active * upward).astype(bfloat)
    branch_f = lax.psum(matmul_trans(hidden, down_full).astype(jnp.bfloat16), "tp").astype(
        jnp.float32
    )
    layer_out = (middle + RESIDUAL * branch_f).astype(bfloat).reshape(seqs_here, rows_here, width)
    gain_fb, gate_back, up_back, down_back = (
        lax.all_gather(gain_ffn.astype(jnp.bfloat16), ("fsdp", "ctx"), axis=0, tiled=True).astype(
            gain_ffn.dtype
        ),
        lax.all_gather(gate_weight, ("fsdp", "ctx"), axis=0, tiled=True),
        lax.all_gather(up_weight, ("fsdp", "ctx"), axis=0, tiled=True),
        lax.all_gather(down_weight, ("fsdp", "ctx"), axis=0, tiled=True),
    )
    grad_y = cotangent.reshape(tokens, width).astype(jnp.float32)
    d_branch_f = (RESIDUAL * grad_y).astype(bfloat)
    grad_down = matmul_outer(d_branch_f, hidden)
    d_hidden = matmul_low(d_branch_f, down_back)
    d_gate = (d_hidden * upward * sigma * (1.0 + gate_pre * (1.0 - sigma))).astype(bfloat)
    d_up = (d_hidden * active).astype(bfloat)
    grad_gate = matmul_outer(normed_f, d_gate)
    grad_up = matmul_outer(normed_f, d_up)
    d_normed_f = lax.psum(
        (matmul_trans(d_gate, gate_back) + matmul_trans(d_up, up_back)).astype(jnp.bfloat16), "tp"
    ).astype(jnp.float32)
    grad_gain_ffn = jnp.sum(d_normed_f * unit_f, axis=0)
    d_middle = grad_y + norm_back(d_normed_f, gain_fb, unit_f, inv_f)
    ffn_grads = (
        lax.psum_scatter(grad_gain_ffn, ("fsdp", "ctx"), scatter_dimension=0, tiled=True),
        reduce_low(grad_gate),
        reduce_low(grad_up),
        reduce_low(grad_down),
    )
    gain_ab, query_back, key_back, value_back, out_back = (
        lax.all_gather(gain_attn.astype(jnp.bfloat16), ("fsdp", "ctx"), axis=0, tiled=True).astype(
            gain_attn.dtype
        ),
        lax.all_gather(query_weight, ("fsdp", "ctx"), axis=0, tiled=True),
        lax.all_gather(key_weight, ("fsdp", "ctx"), axis=0, tiled=True),
        lax.all_gather(value_weight, ("fsdp", "ctx"), axis=0, tiled=True),
        lax.all_gather(out_weight, ("fsdp", "ctx"), axis=0, tiled=True),
    )
    d_branch_a = (RESIDUAL * d_middle).astype(bfloat)
    grad_out = matmul_outer(d_branch_a, mixed)
    d_mixed = (
        matmul_low(d_branch_a, out_back)
        .astype(bfloat)
        .reshape(seqs_here, rows_here, kv_local, group_size, HD)
    )
    probs_again = jnp.exp(masked_scores() - log_total)
    probs_again_low = probs_again.astype(bfloat)
    d_probs = jnp.einsum(
        "srngd,slnd->sngrl", d_mixed, value_all, preferred_element_type=jnp.float32
    )
    inner = jnp.sum(probs_again * d_probs, axis=-1, keepdims=True)
    d_scores = (probs_again * (d_probs - inner)).astype(bfloat)
    d_query_rot = (
        jnp.einsum("sngrl,slnd->srngd", d_scores, key_all, preferred_element_type=jnp.float32)
        * SCALE
    )
    d_key_all = (
        jnp.einsum("sngrl,srngd->slnd", d_scores, query_rot, preferred_element_type=jnp.float32)
        * SCALE
    )
    d_value_all = jnp.einsum(
        "sngrl,srngd->slnd", probs_again_low, d_mixed, preferred_element_type=jnp.float32
    )
    d_key_own, d_value_own = (
        lax.psum_scatter(
            d_key_all.reshape(seqs_here, length, kv_local * HD).astype(jnp.bfloat16),
            "ctx",
            scatter_dimension=1,
            tiled=True,
        ).astype(jnp.float32),
        lax.psum_scatter(
            d_value_all.reshape(seqs_here, length, kv_local * HD).astype(jnp.bfloat16),
            "ctx",
            scatter_dimension=1,
            tiled=True,
        ).astype(jnp.float32),
    )
    d_query = (
        rotate_pairs(d_query_rot, cosine[:, :, None, None, :], -sine[:, :, None, None, :])
        .astype(bfloat)
        .reshape(tokens, head_cols)
    )
    d_key = rotate_pairs(
        d_key_own.reshape(seqs_here, rows_here, kv_local, HD),
        cosine[:, :, None, :],
        -sine[:, :, None, :],
    )
    d_key = d_key.astype(bfloat).reshape(tokens, kv_local * HD)
    d_value = d_value_own.reshape(tokens, kv_local * HD).astype(bfloat)
    grad_query = matmul_outer(normed_a, d_query)
    grad_key = matmul_outer(normed_a, d_key)
    grad_value = matmul_outer(normed_a, d_value)
    d_normed_part = (
        matmul_trans(d_query, query_back)
        + matmul_trans(d_key, key_back)
        + matmul_trans(d_value, value_back)
    )
    d_normed_a = lax.psum(d_normed_part.astype(jnp.bfloat16), "tp").astype(jnp.float32)
    grad_gain_attn = jnp.sum(d_normed_a * unit_a, axis=0)
    input_grad = (d_middle + norm_back(d_normed_a, gain_ab, unit_a, inv_a)).reshape(
        seqs_here, rows_here, width
    )
    attn_grads = (
        lax.psum_scatter(grad_gain_attn, ("fsdp", "ctx"), scatter_dimension=0, tiled=True),
        reduce_low(grad_query),
        reduce_low(grad_key),
        reduce_low(grad_value),
        reduce_low(grad_out),
    )
    return (
        layer_out,
        input_grad,
        attn_grads[0],
        attn_grads[1],
        attn_grads[2],
        attn_grads[3],
        attn_grads[4],
        ffn_grads[0],
        ffn_grads[1],
        ffn_grads[2],
        ffn_grads[3],
    )


MAX_DOC = 512
LANES = 128
NEG = -1e30


def half_lanes(rows):
    lane = lax.broadcasted_iota(jnp.int32, (rows, LANES), 1)
    return lane % HD < HD // 2, lane < HD


def turn(slab, cosine, sine_signed):
    first, _ = half_lanes(slab.shape[0])
    swapped = jnp.where(
        first,
        pltpu.roll(slab, LANES - HD // 2, 1),
        pltpu.roll(slab, HD // 2, 1),
    )
    return slab * cosine + swapped * sine_signed


def dot_nt(left, right):
    return lax.dot_general(left, right, (((1,), (1,)), ((), ())), preferred_element_type=jnp.float32)


def dot_tn(left, right):
    return lax.dot_general(left, right, (((0,), (0,)), ((), ())), preferred_element_type=jnp.float32)


def window_mask(start, first_query, first_key, rows, keys):
    query = first_query + lax.broadcasted_iota(jnp.int32, (rows, keys), 0)
    key = first_key + lax.broadcasted_iota(jnp.int32, (rows, keys), 1)
    return (key <= query) & (key >= start)


def each_window(step, rows, window, body):
    last = window // rows - 1
    for early in range(last):
        pl.when(step == early)(functools.partial(body, (early + 1) * rows, 0))
    first = pl.multiple_of(jnp.maximum(step - last, 0) * rows, rows)
    pl.when(step >= last)(functools.partial(body, window, first))


def attend_kernel(
    rows, window, heads, place_ref, qkv_ref, cos_ref, sin_ref, start_ref, *rest,
):
    query_ref, kv_ref, mixed_ref, lse_ref, keys, values = rest[-6:]
    step = pl.program_id(1)
    _, low_half = half_lanes(rows)
    cosine, sine = cos_ref[...], sin_ref[...]

    @pl.when(step == 0)
    def _():
        keys[...] = jnp.zeros_like(keys)
        values[...] = jnp.zeros_like(values)

    width = heads * HD
    raw = qkv_ref[:, width:]
    kv = jnp.where(low_half, turn(raw, cosine, sine), raw)
    kv_ref[...] = kv.astype(jnp.bfloat16)
    moved = pltpu.roll(kv, HD, 1)
    own = pl.ds(pl.multiple_of(step * rows, rows), rows)
    keys[own, :] = jnp.where(low_half, kv, moved).astype(jnp.bfloat16)
    values[own, :] = jnp.where(low_half, moved, kv).astype(jnp.bfloat16)

    def windowed(count, first_key):
        keys_w = keys[pl.ds(first_key, count), :]
        values_w = values[pl.ds(first_key, count), :]
        allowed = window_mask(start_ref[...], step * rows, first_key, rows, count)
        for slab in range(width // LANES):
            at = slice(slab * LANES, (slab + 1) * LANES)
            rot = turn(qkv_ref[:, at], cosine, sine).astype(jnp.bfloat16)
            query_ref[:, at] = rot
            both = []
            for part in range(2):
                mine = low_half if part == 0 else jnp.logical_not(low_half)
                one = jnp.where(mine, rot, jnp.zeros_like(rot))
                scores = jnp.where(allowed, dot_nt(one * SCALE, keys_w), NEG)
                highest = jnp.max(scores, axis=1, keepdims=True)
                raised = jnp.exp(scores - highest)
                total = jnp.sum(raised, axis=1, keepdims=True)
                mixed = jnp.dot(
                    raised.astype(jnp.bfloat16), values_w, preferred_element_type=jnp.float32
                )
                both.append(mixed / total)
                head = slab * 2 + part
                lse_ref[:, head : head + 1] = highest + jnp.log(total)
            mixed_ref[:, at] = jnp.where(low_half, both[0], both[1]).astype(jnp.bfloat16)

    each_window(step, rows, window, windowed)


def attend_back_kernel(
    rows, window, heads, blocks, place_ref, query_ref, kv_ref, lse_ref, grad_ref, inv_ref, cos_ref, sin_ref, start_ref,
    out_ref, keys, values, d_keys, d_values,
):
    seq = pl.program_id(0)
    step = blocks - 1 - pl.program_id(1)
    _, low_half = half_lanes(rows)
    inv = inv_ref[...]
    cosine, sine = cos_ref[...], sin_ref[...]

    @pl.when(step == blocks - 1)
    def _():
        for block in range(blocks):
            source = pl.multiple_of(place_ref[seq * blocks + block] * rows, rows)
            kv = kv_ref[pl.ds(source, rows), :].astype(jnp.float32)
            moved = pltpu.roll(kv, HD, 1)
            at = slice(block * rows, (block + 1) * rows)
            keys[at, :] = jnp.where(low_half, kv, moved).astype(jnp.bfloat16)
            values[at, :] = jnp.where(low_half, moved, kv).astype(jnp.bfloat16)
        d_keys[...] = jnp.zeros_like(d_keys)
        d_values[...] = jnp.zeros_like(d_values)

    width = heads * HD

    def windowed(count, first_key):
        span = pl.ds(first_key, count)
        keys_w = keys[span, :]
        values_w = values[span, :]
        allowed = window_mask(start_ref[...], step * rows, first_key, rows, count)
        d_keys_w = jnp.zeros((count, LANES), jnp.float32)
        d_values_w = jnp.zeros((count, LANES), jnp.float32)
        for slab in range(width // LANES):
            at = slice(slab * LANES, (slab + 1) * LANES)
            query, grad = query_ref[:, at], grad_ref[:, at]
            both = []
            for part in range(2):
                mine = low_half if part == 0 else jnp.logical_not(low_half)
                head = slab * 2 + part
                one = jnp.where(mine, query, jnp.zeros_like(query)) * SCALE
                one_grad = jnp.where(mine, grad, jnp.zeros_like(grad))
                scores = dot_nt(one, keys_w) - lse_ref[:, head : head + 1]
                probs = jnp.exp(jnp.where(allowed, scores, NEG))
                d_probs = dot_nt(one_grad, values_w)
                inner = jnp.sum(probs * d_probs, axis=1, keepdims=True)
                d_scores = (probs * (d_probs - inner)).astype(jnp.bfloat16)
                both.append(jnp.dot(d_scores, keys_w, preferred_element_type=jnp.float32))
                d_keys_w = d_keys_w + dot_tn(d_scores, one)
                d_values_w = d_values_w + dot_tn(probs.astype(jnp.bfloat16), one_grad)
            d_query = jnp.where(low_half, both[0], both[1]) * SCALE
            out_ref[:, at] = (turn(d_query, cosine, -sine) * inv).astype(jnp.bfloat16)
        d_keys[span, :] += d_keys_w
        d_values[span, :] += d_values_w

    each_window(step, rows, window, windowed)
    own = pl.ds(pl.multiple_of(step * rows, rows), rows)
    d_key = d_keys[own, :]
    d_key = turn(d_key + pltpu.roll(d_key, HD, 1), cosine, -sine)
    d_value = d_values[own, :]
    d_value = d_value + pltpu.roll(d_value, HD, 1)
    out_ref[:, width:] = (jnp.where(low_half, d_key, d_value) * inv).astype(jnp.bfloat16)


def attend(place, qkv, cosine, sine, start, seqs, blocks, rows, heads, others):
    tokens = qkv.shape[0]
    width = heads * HD
    window = min(blocks * rows, rows + -(-MAX_DOC // rows) * rows)

    def placed(cols):
        return pl.BlockSpec((rows, cols), lambda s, i, place: (place[s * blocks + i], 0))

    def natural(cols):
        return pl.BlockSpec((rows, cols), lambda s, i, place: (s * blocks + i, 0))

    return pl.pallas_call(
        functools.partial(attend_kernel, rows, window, heads),
        out_shape=(
            jax.ShapeDtypeStruct((tokens, width), jnp.bfloat16),
            jax.ShapeDtypeStruct((tokens, LANES), jnp.bfloat16),
            jax.ShapeDtypeStruct((tokens, width), jnp.bfloat16),
            jax.ShapeDtypeStruct((tokens, heads), jnp.float32),
        ),
        grid_spec=pltpu.PrefetchScalarGridSpec(
            num_scalar_prefetch=1,
            grid=(seqs, blocks),
            in_specs=[placed(width + LANES), natural(LANES), natural(LANES), natural(1)]
            + [ANYWHERE] * len(others),
            out_specs=[placed(width), placed(LANES), placed(width), placed(heads)],
            scratch_shapes=[pltpu.VMEM((blocks * rows, LANES), jnp.bfloat16)] * 2,
        ),
        compiler_params=pltpu.CompilerParams(vmem_limit_bytes=48 << 20),
        name="attend",
    )(place, qkv, cosine, sine, start, *others)


def attend_back(place, query, kv, lse, grad, inv, cosine, sine, start, seqs, blocks, rows, heads):
    tokens = query.shape[0]
    width = heads * HD
    window = min(blocks * rows, rows + -(-MAX_DOC // rows) * rows)

    def placed(cols):
        return pl.BlockSpec(
            (rows, cols), lambda s, i, place: (place[s * blocks + blocks - 1 - i], 0)
        )

    def natural(cols):
        return pl.BlockSpec((rows, cols), lambda s, i, place: (s * blocks + blocks - 1 - i, 0))

    return pl.pallas_call(
        functools.partial(attend_back_kernel, rows, window, heads, blocks),
        out_shape=jax.ShapeDtypeStruct((tokens, width + LANES), jnp.bfloat16),
        grid_spec=pltpu.PrefetchScalarGridSpec(
            num_scalar_prefetch=1,
            grid=(seqs, blocks),
            in_specs=[
                placed(width),
                pl.BlockSpec((tokens, LANES), lambda s, i, place: (0, 0)),
                placed(heads),
                placed(width),
                placed(1),
                natural(LANES),
                natural(LANES),
                natural(1),
            ],
            out_specs=placed(width + LANES),
            scratch_shapes=[pltpu.VMEM((blocks * rows, LANES), jnp.bfloat16)] * 2
            + [pltpu.VMEM((blocks * rows, LANES), jnp.float32)] * 2,
        ),
        compiler_params=pltpu.CompilerParams(vmem_limit_bytes=48 << 20),
        cost_estimate=pl.CostEstimate(
            flops=48 * tokens * window * heads * LANES,
            transcendentals=tokens * window * heads,
            bytes_accessed=tokens * (8 * width + 12 * LANES),
        ),
        name="attend_back",
    )(place, query, kv, lse, grad, inv, cosine, sine, start)


VMEM_LIMIT = 56 << 20
ANYWHERE = pl.BlockSpec(memory_space=pl.ANY)


def fetch(pieces, whole, sems):
    copies, at = [], 0
    for n, piece in enumerate(pieces):
        span = slice(at, at + piece.shape[0])
        copy = pltpu.make_async_copy(piece, whole.at[span, :], sems.at[n])
        copy.start()
        copies.append((copy, span))
        at += piece.shape[0]
    return copies


def inverse_rms(values):
    values = values.astype(jnp.float32)
    return lax.rsqrt(jnp.mean(values * values, axis=-1, keepdims=True) + EPSILON)


def rows_of(pieces):
    return sum(piece.shape[0] for piece in pieces)


def project_kernel(count, tokens, normed, factor, *refs):
    pieces, rest = refs[:count], refs[count + tokens :]
    weight_ref, out_ref = rest[:2]
    whole, sems = rest[-2:]
    for copy, span in fetch(pieces, whole, sems):
        copy.wait()
        values = whole[span, :]
        product = jnp.dot(values, weight_ref[...], preferred_element_type=jnp.float32)
        if normed:
            inv = inverse_rms(values)
            rest[2][span, :] = inv
            product = product * inv
        else:
            product = product * factor
        out_ref[span, :] = product.astype(out_ref.dtype)


def project(pieces, weight, normed, factor, dtype, tokens=()):
    count, width = rows_of(pieces), pieces[0].shape[1]
    out_shape = [jax.ShapeDtypeStruct((count, weight.shape[1]), dtype)]
    if normed:
        out_shape.append(jax.ShapeDtypeStruct((count, 1), jnp.float32))
    vmem = pl.BlockSpec(memory_space=pltpu.VMEM)
    return pl.pallas_call(
        functools.partial(project_kernel, len(pieces), len(tokens), normed, factor),
        out_shape=out_shape,
        in_specs=[ANYWHERE] * (len(pieces) + len(tokens)) + [vmem],
        out_specs=[vmem] * len(out_shape),
        scratch_shapes=[
            pltpu.VMEM((count, width), jnp.bfloat16),
            pltpu.SemaphoreType.DMA((len(pieces),)),
        ],
        compiler_params=pltpu.CompilerParams(vmem_limit_bytes=VMEM_LIMIT),
        cost_estimate=pl.CostEstimate(
            flops=4 * count * width * weight.shape[1],
            transcendentals=0,
            bytes_accessed=2 * count * width,
        ),
        name="project",
    )(*pieces, *tokens, weight)


def gated_kernel(count, chunk, *refs):
    pieces, rest = refs[:count], refs[count:]
    pair_w, gate_ref, up_ref, hidden_ref, inv_ref, whole, sems = rest
    block = gate_ref.shape[1]

    @pl.when(pl.program_id(0) == 0)
    def _():
        for copy, span in fetch(pieces, whole, sems):
            copy.wait()
            inv_ref[span, :] = inverse_rms(whole[span, :])

    for at in range(0, whole.shape[0], chunk):
        span = slice(at, at + chunk)
        both = jnp.dot(whole[span, :], pair_w[...], preferred_element_type=jnp.float32)
        both = both * inv_ref[span, :]
        gate, up = both[:, :block], both[:, block:]
        gate_ref[span, :] = gate.astype(jnp.bfloat16)
        up_ref[span, :] = up.astype(jnp.bfloat16)
        hidden_ref[span, :] = (gate * lax.logistic(gate) * up).astype(jnp.bfloat16)


def gated(pieces, pair_w, block, chunk):
    tokens, width = rows_of(pieces), pieces[0].shape[1]
    units = pair_w.shape[1] // 2
    low = jax.ShapeDtypeStruct((tokens, units), jnp.bfloat16)
    out = pl.BlockSpec((tokens, block), lambda j: (0, j))
    return pl.pallas_call(
        functools.partial(gated_kernel, len(pieces), chunk),
        out_shape=[low, low, low, jax.ShapeDtypeStruct((tokens, 1), jnp.float32)],
        grid=(units // block,),
        in_specs=[ANYWHERE] * len(pieces)
        + [pl.BlockSpec((width, 2 * block), lambda j: (0, j))],
        out_specs=[out, out, out, pl.BlockSpec((tokens, 1), lambda j: (0, 0))],
        scratch_shapes=[
            pltpu.VMEM((tokens, width), jnp.bfloat16),
            pltpu.SemaphoreType.DMA((len(pieces),)),
        ],
        compiler_params=pltpu.CompilerParams(vmem_limit_bytes=VMEM_LIMIT),
        name="gated",
    )(*pieces, pair_w)


def gated_back_kernel(count, tokens, chunk, *refs):
    pieces, rest = refs[:count], refs[count + tokens :]
    down_w, gate_ref, up_ref, inv_ref, out_ref, whole, sems = rest
    block = gate_ref.shape[1]

    @pl.when(pl.program_id(0) == 0)
    def _():
        for copy, _ in fetch(pieces, whole, sems):
            copy.wait()

    for at in range(0, whole.shape[0], chunk):
        span = slice(at, at + chunk)
        d_hidden = jnp.dot(whole[span, :], down_w[...], preferred_element_type=jnp.float32)
        d_hidden = d_hidden * (RESIDUAL * inv_ref[span, :])
        gate = gate_ref[span, :].astype(jnp.float32)
        up = up_ref[span, :].astype(jnp.float32)
        sigma = lax.logistic(gate)
        out_ref[span, :block] = (d_hidden * up * sigma * (1.0 + gate * (1.0 - sigma))).astype(
            jnp.bfloat16
        )
        out_ref[span, block:] = (d_hidden * gate * sigma).astype(jnp.bfloat16)


def gated_back(pieces, down_w, gate, up, inv, block, chunk, others):
    tokens, width = rows_of(pieces), pieces[0].shape[1]
    units = down_w.shape[1]
    tall = pl.BlockSpec((tokens, block), lambda j: (0, j))
    return pl.pallas_call(
        functools.partial(gated_back_kernel, len(pieces), len(others), chunk),
        out_shape=jax.ShapeDtypeStruct((tokens, 2 * units), jnp.bfloat16),
        grid=(units // block,),
        in_specs=[ANYWHERE] * (len(pieces) + len(others))
        + [
            pl.BlockSpec((width, block), lambda j: (0, j)),
            tall,
            tall,
            pl.BlockSpec((tokens, 1), lambda j: (0, 0)),
        ],
        out_specs=pl.BlockSpec((tokens, 2 * block), lambda j: (0, j)),
        scratch_shapes=[
            pltpu.VMEM((tokens, width), jnp.bfloat16),
            pltpu.SemaphoreType.DMA((len(pieces),)),
        ],
        compiler_params=pltpu.CompilerParams(vmem_limit_bytes=VMEM_LIMIT),
        name="gated_back",
    )(*pieces, *others, down_w, gate, up, inv)


def outer_kernel(counts, tokens, block, *refs):
    sources, at = [], 0
    for count, rights in counts:
        sources.append((refs[at : at + count], refs[at + count : at + count + rights]))
        at += count + rights
    out_ref, scratch = refs[at + tokens], refs[at + tokens + 1 :]
    step = pl.program_id(0)

    @pl.when(step == 0)
    def _():
        copies = []
        for n, (pieces, _) in enumerate(sources):
            copies += fetch(pieces, scratch[2 * n], scratch[2 * n + 1])
        for copy, _ in copies:
            copy.wait()

    first = 0
    columns = pl.ds(pl.multiple_of(step * block, block), block)
    for n, (_, rights) in enumerate(sources):
        left = scratch[2 * n][:, columns]
        for right in rights:
            out_ref[:, first : first + right.shape[1]] = dot_tn(left, right[...]).astype(
                out_ref.dtype
            )
            first += right.shape[1]


def outer(sources, block, tokens=(), cost=None):
    operands, in_specs, scratch, counts, total = [], [], [], [], 0
    for pieces, rights in sources:
        count, width = rows_of(pieces), pieces[0].shape[1]
        operands += [*pieces, *rights]
        in_specs += [ANYWHERE] * len(pieces)
        in_specs += [pl.BlockSpec(right.shape, lambda j: (0, 0)) for right in rights]
        scratch += [
            pltpu.VMEM((count, width), jnp.bfloat16),
            pltpu.SemaphoreType.DMA((len(pieces),)),
        ]
        counts.append((len(pieces), len(rights)))
        total += sum(right.shape[1] for right in rights)
    return pl.pallas_call(
        functools.partial(outer_kernel, counts, len(tokens), block),
        out_shape=jax.ShapeDtypeStruct((width, total), jnp.bfloat16),
        grid=(width // block,),
        in_specs=in_specs + [ANYWHERE] * len(tokens),
        out_specs=pl.BlockSpec((block, total), lambda j: (j, 0)),
        scratch_shapes=scratch,
        compiler_params=pltpu.CompilerParams(vmem_limit_bytes=VMEM_LIMIT),
        cost_estimate=cost,
        name="outer",
    )(*operands, *tokens)


def rows_kernel(added, left_ref, weight_ref, *rest):
    product = dot_nt(left_ref[...], weight_ref[...])
    if added:
        product = product + rest[0][...].astype(jnp.float32)
    rest[-1][...] = product.astype(rest[-1].dtype)


def rows_product(left, weight, first, size, add, block):
    width, depth = weight.shape
    out = pl.BlockSpec((size, block), lambda j: (0, j))
    extra = [] if add is None else [add]
    return pl.pallas_call(
        functools.partial(rows_kernel, len(extra)),
        out_shape=jax.ShapeDtypeStruct((size, width), jnp.bfloat16),
        grid=(width // block,),
        in_specs=[
            pl.BlockSpec((size, depth), lambda j: (first // size, 0)),
            pl.BlockSpec((block, depth), lambda j: (j, 0)),
        ]
        + [out] * len(extra),
        out_specs=out,
        compiler_params=pltpu.CompilerParams(vmem_limit_bytes=VMEM_LIMIT),
        name="rows_product",
    )(left, weight, *extra)


def fold_kernel(tokens, mine, from_near, from_ctx, *rest):
    to_ctx, to_near = rest[tokens:]
    rows, half = mine.shape[0] // 4, mine.shape[0] // 8
    ctx_first, near_last = slice(rows, rows + half), slice(2 * rows + half, 3 * rows)
    to_ctx[...] = (
        mine[ctx_first, :].astype(jnp.float32) + from_near[...].astype(jnp.float32)
    ).astype(jnp.bfloat16)
    to_near[...] = (
        mine[near_last, :].astype(jnp.float32) + from_ctx[...].astype(jnp.float32)
    ).astype(jnp.bfloat16)


def fold(mine, from_near, from_ctx, tokens):
    half = jax.ShapeDtypeStruct(from_near.shape, jnp.bfloat16)
    vmem = pl.BlockSpec(memory_space=pltpu.VMEM)
    return pl.pallas_call(
        functools.partial(fold_kernel, len(tokens)),
        out_shape=[half, half],
        in_specs=[vmem] * 3 + [ANYWHERE] * len(tokens),
        out_specs=[vmem] * 2,
        compiler_params=pltpu.CompilerParams(vmem_limit_bytes=VMEM_LIMIT),
        name="fold",
    )(mine, from_near, from_ctx, *tokens)


def finish_kernel(group, me_ref, *refs):
    pieces, rest = refs[:group], refs[group:]
    query_w, key_w, value_w, gain_ref, grad_q, grad_k, grad_v, grad_o, sums = rest
    me, gain = me_ref[0], gain_ref[...]
    lows = [piece[...].astype(jnp.float32) for piece in pieces]
    total = jnp.zeros(sums.shape, jnp.float32)
    for owner in range(group):
        mine = lows[0]
        for m in range(1, group):
            mine = jnp.where(me == (owner ^ m), lows[m], mine)
        first = 0
        for weight, out in ((query_w, grad_q), (key_w, grad_k), (value_w, grad_v)):
            size = weight.shape[1] // group
            grad = mine[:, first : first + size]
            at = slice(owner * size, (owner + 1) * size)
            out[:, at] = grad * gain
            total = total + jnp.sum(
                weight[:, at].astype(jnp.float32) * grad, axis=1, keepdims=True
            )
            first += size
        size = grad_o.shape[1] // group
        grad_o[:, owner * size : (owner + 1) * size] = mine[:, first:] * RESIDUAL
    sums[...] = total


def finish(me, pieces, query_w, key_w, value_w, gain, out_cols):
    deep = query_w.shape[0]
    vmem = pl.BlockSpec(memory_space=pltpu.VMEM)
    shapes = [w.shape[1] for w in (query_w, key_w, value_w)] + [out_cols, 1]
    return pl.pallas_call(
        functools.partial(finish_kernel, len(pieces)),
        out_shape=[jax.ShapeDtypeStruct((deep, cols), jnp.float32) for cols in shapes],
        in_specs=[pl.BlockSpec(memory_space=pltpu.SMEM)] + [vmem] * (len(pieces) + 4),
        out_specs=[vmem] * len(shapes),
        compiler_params=pltpu.CompilerParams(vmem_limit_bytes=VMEM_LIMIT),
        name="finish",
    )(me, *pieces, query_w, key_w, value_w, gain)


def after_kernel(*refs):
    del refs


def after(value, *tokens):
    return pl.pallas_call(
        after_kernel,
        out_shape=jax.ShapeDtypeStruct(value.shape, value.dtype),
        in_specs=[ANYWHERE] * (1 + len(tokens)),
        out_specs=ANYWHERE,
        input_output_aliases={0: 0},
        name="after",
    )(value, *tokens)


def group_shards(
    group, cores,
    hidden_in, segments, gain_attn, query_weight, key_weight, value_weight, out_weight,
    gain_ffn, gate_weight, up_weight, down_weight, cotangent,
):
    bfloat = jnp.bfloat16
    seqs_here, rows_here, width = hidden_in.shape
    length = segments.shape[1]
    rows = rows_here // cores
    near = group // (length // rows_here)
    blocks = length // rows
    heads = HQ // KVH
    me = lax.axis_index(("near", "ctx")).astype(jnp.uint32)
    me_core = lax.axis_index("tp").astype(jnp.uint32)

    def swap(value, m):
        return lax.ppermute(value, ("near", "ctx"), [(i, i ^ m) for i in range(group)])

    def swap_core(value):
        return lax.ppermute(value, "tp", [(0, 1), (1, 0)])

    def gather(own, later=()):
        half = own.shape[0] // 2
        by_ctx, by_near = swap(own, 1), swap(own, 2)
        if later:
            by_ctx, by_near = after(by_ctx, *later), after(by_near, *later)
        opposite = [swap(by_ctx[:half], 2), swap(by_near[half:], 1)]
        same = [own, by_ctx, by_near, *opposite]
        return same + [swap_core(v) for v in same]

    def other_side(product):
        return product(group * rows, group * rows, None)

    def own_side(product, other):
        return product(0, group * rows, other)

    def scatter(mine, *tokens):
        half = rows // 2
        ctx_low, near_low, opposite = (mine[m * rows : (m + 1) * rows] for m in range(1, group))
        from_near, from_ctx = swap(opposite[:half], 2), swap(opposite[half:], 1)
        near_first, ctx_last = swap(near_low[:half], 2), swap(ctx_low[half:], 1)
        to_ctx, to_near = fold(mine, from_near, from_ctx, tokens)
        ctx_first, near_last = swap(to_ctx, 1), swap(to_near, 2)
        total = jnp.concatenate(
            [
                mine[:half].astype(jnp.float32)
                + ctx_first.astype(jnp.float32)
                + near_first.astype(jnp.float32),
                mine[half:rows].astype(jnp.float32)
                + ctx_last.astype(jnp.float32)
                + near_last.astype(jnp.float32),
            ]
        )
        return total, (to_ctx, to_near)

    def scatter_direct(mine):
        total = mine[:rows].astype(jnp.float32)
        for m in range(1, group):
            total = total + swap(mine[m * rows : (m + 1) * rows], m).astype(jnp.float32)
        return total

    def plain(left, weight):
        return lambda first, size, add: rows_product(left, weight, first, size, add, 512)

    def narrow(left, weight):
        def product(first, size, add):
            out = matmul_trans(left[first : first + size], weight)
            return (out if add is None else out + add.astype(jnp.float32)).astype(bfloat)

        return product

    def own_half(value):
        return cut(value, me_core, rows, 0)

    def both_halves(own):
        other = swap_core(own)
        whole = jnp.zeros((rows_here, own.shape[1]), own.dtype)
        whole = put(whole, own, me_core, 0)
        return put(whole, other, me_core ^ jnp.uint32(1), 0)

    def cut(value, index, size, axis):
        starts = [jnp.uint32(0)] * value.ndim
        starts[axis] = index * jnp.uint32(size)
        sizes = list(value.shape)
        sizes[axis] = size
        return lax.dynamic_slice(value, starts, sizes)

    def put(whole, piece, index, axis):
        starts = [jnp.uint32(0)] * whole.ndim
        starts[axis] = index * jnp.uint32(piece.shape[axis])
        return lax.dynamic_update_slice(whole, piece, starts)

    def to_columns(*weights, parts=1, later=()):
        whole = None
        for m in range(group):
            there = me ^ jnp.uint32(m)
            own = [cut(w, there, w.shape[1] // group, 1) for w in weights]
            sizes = [w.shape[1] // parts for w in own]
            piece = jnp.concatenate(
                [w[:, n * size : (n + 1) * size] for n in range(parts) for w, size in zip(own, sizes)],
                axis=1,
            )
            if m:
                piece = swap(after(piece, *later) if later else piece, m)
            if whole is None:
                whole = jnp.zeros((group * piece.shape[0], piece.shape[1]), piece.dtype)
            whole = put(whole, piece, there, 0)
        return whole

    def to_rows(grad):
        deep = grad.shape[0] // group
        pieces = [cut(grad, me ^ jnp.uint32(m), deep, 0) for m in range(group)]
        return [swap(piece, m) if m else piece for m, piece in enumerate(pieces)]

    def unpack(pieces, widths, factors, parts=1):
        first, wholes, turn_width = 0, [], sum(widths) // parts
        for cols, factor in zip(widths, factors):
            size = cols // parts
            whole = jnp.zeros((pieces[0].shape[0], group * cols), jnp.float32)
            for m, piece in enumerate(pieces):
                part = jnp.concatenate(
                    [
                        piece[:, n * turn_width + first : n * turn_width + first + size]
                        for n in range(parts)
                    ],
                    axis=1,
                )
                part = part.astype(jnp.float32) * factor
                whole = put(whole, part, me ^ jnp.uint32(m), 1)
            first += size
            wholes.append(whole)
        return wholes

    def far_gather(weight):
        return lax.all_gather(weight, "far", axis=0, tiled=True)

    def far_scatter(grad):
        return lax.psum_scatter(grad.astype(bfloat), "far", scatter_dimension=0, tiled=True)

    deep = query_weight.shape[0]
    col_gain_a, col_gain_f = gain_attn[:, None], gain_ffn[:, None]

    def scaled(weight, gain):
        return (weight.astype(jnp.float32) * gain).astype(bfloat)

    attn_cols = to_columns(
        scaled(query_weight, col_gain_a),
        scaled(key_weight, col_gain_a),
        scaled(value_weight, col_gain_a),
        out_weight,
    )
    attn_w = far_gather(attn_cols)
    head_cols = heads * HD
    in_w, out_w = attn_w[:, : head_cols + 2 * HD], attn_w[:, head_cols + 2 * HD :]

    gain_later = after(col_gain_f, attn_cols)
    units = down_weight.shape[1] // group
    block = min(units, 256)
    pair_cols = to_columns(
        scaled(gate_weight, gain_later), scaled(up_weight, gain_later), parts=units // block
    )
    seg_all = jnp.concatenate(
        [segments] + [swap(segments, n * (group // near)) for n in range(1, near)],
        axis=0,
    )
    start = jnp.sum((seg_all[:, None, :] < seg_all[:, :, None]).astype(jnp.int32), axis=2)
    places = (jnp.arange(length, dtype=jnp.int32)[None, :] - start).astype(jnp.float32)
    freqs = THETA ** (-jnp.arange(0, HD, 2, dtype=jnp.float32) / HD)
    phase = places.reshape(-1)[:, None] * freqs
    cosine, sine = jnp.cos(phase), jnp.sin(phase)
    cosine = jnp.concatenate([cosine, cosine, cosine, cosine], axis=1)
    sine = jnp.concatenate([-sine, sine, -sine, sine], axis=1)
    start = start.reshape(-1)[:, None]
    at = jnp.arange(near * blocks, dtype=jnp.int32)
    in_seq = at % blocks
    here_ctx = lax.axis_index("ctx")
    place = (
        ((in_seq % cores) ^ lax.axis_index("tp")) * group
        + (at // blocks) * (group // near)
        + ((in_seq // cores) ^ here_ctx)
    ).astype(jnp.int32)

    own_in = after(own_half(hidden_in.reshape(rows_here, width)), pair_cols)
    inputs = gather(own_in, (cosine, sine))
    pair_w = far_gather(pair_cols)
    own_cot = own_half(cotangent.reshape(rows_here, width))

    qkv, inv_a = project(inputs, in_w, True, None, jnp.float32)
    down_cols = to_columns(down_weight, later=(inv_a,))
    down_w = far_gather(down_cols)
    query, kv, mixed, lse = attend(
        place, qkv, cosine, sine, start, near, blocks, rows, heads, ()
    )
    product = narrow(mixed, out_w)
    branch_a, _ = scatter(own_side(product, swap_core(other_side(product))))
    own_f = own_in.astype(jnp.float32)
    middle = own_f + RESIDUAL * branch_a

    mids = gather(after(middle.astype(bfloat), down_cols))
    gate_pre, upward, hidden, inv_f = gated(mids, pair_w, block, 512)
    cots = gather(after(own_cot, *mids[1 : len(mids) // 2]), (inv_f,))
    down_part = outer([(cots, [hidden])], 512)
    down_far = far_scatter(down_part)
    d_both = gated_back(cots, down_w, gate_pre, upward, inv_f, block, 512, (down_part,))
    product = plain(d_both, pair_w)
    other = other_side(product)
    pair_part = outer([(mids, [d_both])], 512, (other,))
    pair_far = far_scatter(pair_part)
    back_mine = own_side(product, after(swap_core(other), pair_part))
    product = plain(after(hidden, back_mine), down_w)
    other = other_side(product)
    back_f, _ = scatter(back_mine, other, down_far)
    branch_mine = own_side(product, swap_core(other))

    def through_norm(grad, unit):
        return grad - unit * jnp.mean(grad * unit, axis=-1, keepdims=True)

    d_middle = own_cot.astype(jnp.float32) + through_norm(back_f, middle * inverse_rms(middle))

    d_mids = gather(after(d_middle.astype(bfloat), branch_mine))
    branch_f = scatter_direct(after(branch_mine, *d_mids[1 : len(d_mids) // 2]))
    middle_out = (middle + RESIDUAL * branch_f).astype(bfloat)
    (d_mixed,) = project(d_mids, out_w, False, RESIDUAL, bfloat)
    down_rows = to_rows(after(down_far, d_mixed))
    d_qkv = attend_back(
        place, query, kv, lse, d_mixed, inv_a, cosine, sine, start, near, blocks, rows, heads
    )
    attn_cols_all = d_qkv.shape[1] + head_cols
    attn_part = outer(
        [(inputs, [d_qkv]), (d_mids, [mixed])],
        512,
        (pair_far,),
        pl.CostEstimate(
            flops=4 * d_qkv.shape[0] * width * attn_cols_all,
            transcendentals=0,
            bytes_accessed=8 * d_qkv.shape[0] * width,
        ),
    )
    attn_far = far_scatter(attn_part)
    pair_rows = to_rows(pair_far)
    product = narrow(after(d_qkv, attn_part, middle_out, *down_rows), in_w)
    back_mine = own_side(product, swap_core(other_side(product)))
    back_a, passed = scatter(back_mine, *pair_rows)
    layer_out = both_halves(after(middle_out, back_mine))
    input_grad = d_middle + through_norm(back_a, own_f * inverse_rms(own_f))

    one = jnp.ones_like(col_gain_a)
    (grad_down,) = unpack(
        [after(piece, back_mine) for piece in down_rows], [units], [RESIDUAL]
    )
    grad_gate, grad_up = unpack(
        [after(piece, back_mine) for piece in pair_rows], [units, units], [one, one], parts=units // block
    )
    attn_rows = to_rows(after(attn_far, *passed))
    grad_query, grad_key, grad_value, grad_out, gain_a = finish(
        me.astype(jnp.int32)[None],
        attn_rows,
        query_weight,
        key_weight,
        value_weight,
        col_gain_a,
        out_weight.shape[1],
    )

    def row_sum(*pairs):
        return sum(jnp.sum(weight.astype(jnp.float32) * grad, axis=1) for weight, grad in pairs)

    input_grad = both_halves(after(input_grad, gain_a))
    gain_f = row_sum((gate_weight, grad_gate), (up_weight, grad_up))
    gain_f = gain_f + swap_core(gain_f)
    gain_a = gain_a[:, 0]
    gain_a = gain_a + swap_core(gain_a)
    return (
        layer_out.reshape(hidden_in.shape),
        input_grad.reshape(hidden_in.shape),
        gain_a,
        grad_query,
        grad_key,
        grad_value,
        grad_out,
        gain_f,
        grad_gate * col_gain_f,
        grad_up * col_gain_f,
        grad_down,
    )


def solution(mesh):
    sizes = dict(mesh.shape)
    fsdp, ctx, tp = sizes["fsdp"], sizes["ctx"], sizes["tp"]
    near = KVH // (ctx * tp)
    group = near * ctx
    fits = (
        tuple(mesh.axis_names) == ("fsdp", "ctx", "tp")
        and tp == 2
        and near > 0
        and group * tp == KVH
        and fsdp % near == 0
        and near == ctx == 2
    )
    if fits:
        mesh = Mesh(
            mesh.devices.reshape(fsdp // near, near, ctx, tp), ("far", "near", "ctx", "tp")
        )
        body, data = functools.partial(group_shards, group, tp), ("far", "near")
    else:
        body, data = generic_shards, ("fsdp",)
    owner = (*data, "ctx")
    weight, gain, tokens = P(owner, "tp"), P(owner), P(data, "ctx", None)
    in_specs = (
        tokens,
        P(data, None),
        gain,
        weight,
        weight,
        weight,
        weight,
        gain,
        weight,
        weight,
        weight,
        tokens,
    )
    out_specs = (
        tokens,
        tokens,
        gain,
        weight,
        weight,
        weight,
        weight,
        gain,
        weight,
        weight,
        weight,
    )
    return jax.shard_map(body, mesh=mesh, in_specs=in_specs, out_specs=out_specs, check_vma=False)
```
